32 devices in a mesh: seq: 4 (over y, x), fsdp: 8 (over z, core).
Axes of the slice: x: 2, y: 2, z: 4, core: 2. Of those that a mesh axis runs over, the one named last changes fastest.
Arguments:
- block_input: bfloat16 [8, 2048, 1024], P('fsdp', 'seq'), may hold values from -6 to 6
- norm_gain_a: float32 [1024], P('fsdp'), may hold values from 0.1 to 1.9
- weight_qkv: float32 [1024, 3072], P('fsdp'), may hold values from -0.1875 to 0.1875
- weight_out: float32 [1024, 1024], P('fsdp'), may hold values from -3 to 3
- norm_gain_b: float32 [1024], P('fsdp'), may hold values from 0.1 to 1.9
- weight_gate_up: float32 [1024, 8192], P('fsdp'), may hold values from -0.1875 to 0.1875
- weight_down: float32 [1024, 4096], P('fsdp'), may hold values from -0.09375 to 0.09375
- cotangent: bfloat16 [8, 2048, 1024], P('fsdp', 'seq'), may hold values from -6 to 6
- permutation: int32 [8, 2048], P('fsdp'), may hold values from 0 to 2047, each once within a row
- lengths: int32 [8, 3], P('fsdp'), may hold values from 256 to 1024, as said below
- offsets: int32 [8, 3], P('fsdp'), may hold values from 0 to 1792, as said below
Outputs:
- block_output: bfloat16 [8, 2048, 1024], P('fsdp', 'seq')
- grad_input: bfloat16 [8, 2048, 1024], P('fsdp', 'seq')
- grad_gain_a: float32 [1024], P('fsdp')
- grad_qkv: float32 [1024, 3072], P('fsdp')
- grad_out: float32 [1024, 1024], P('fsdp')
- grad_gain_b: float32 [1024], P('fsdp')
- grad_gate_up: float32 [1024, 8192], P('fsdp')
- grad_down: float32 [1024, 4096], P('fsdp')
The draws below stay inside these ranges and needn't reach their ends.
Inputs may be any that keep to these rules, and one draw needn't show every extreme that they name: A group's 3 lengths sum to 2048, and its longest is exactly 1024. offsets[g, k] is the sum of lengths[g, i] over i < k, so that a group's sequences tile its positions.
All inputs are finite; a program needn't handle non-finite values.
Results may differ from the reference program's by a relative error of at most 0.02.
Values may be sent and summed in bfloat16 or wider, within the bound.
A program may use at most 256 MiB of HBM per device.

```python
import jax
import jax.numpy as jnp
from jax import lax

D = 1024
HEADS = 16
HEAD_DIM = 64
FF = 4096
SEQS = 3
GROUPS = 8
GROUP_TOK = 2048


def split_lengths(key):
    group_len = GROUP_TOK
    longest = group_len // 2
    middle = jax.random.randint(jax.random.fold_in(key, 11), (GROUPS,), group_len // 8, 3 * group_len // 8 + 1).astype(jnp.int32)
    raw_lengths = jnp.stack([jnp.full((GROUPS,), longest, jnp.int32), middle, group_len - longest - middle], axis=1)
    scores = jax.random.randint(jax.random.fold_in(key, 12), (GROUPS, 3), 0, 1 << 20).astype(jnp.int32) * 3 + jnp.arange(3, dtype=jnp.int32)[None, :]
    placing = jnp.argsort(scores, axis=1)
    shuffled = jnp.take_along_axis(raw_lengths, placing, axis=1)
    starts = jnp.cumsum(shuffled, axis=1) - shuffled
    return (shuffled.astype(jnp.int32), starts.astype(jnp.int32))


def draw_lengths(key, part):
    return split_lengths(key)[0]


def draw_offsets(key, part):
    return split_lengths(key)[1]


def strengthened(values, stream_key, source, target, parts, factor):
    owner, partner = [(jnp.arange(values.shape[axis_at]) // (values.shape[axis_at] // parts)).reshape([-1 if axis == axis_at else 1 for axis in range(values.ndim)]) for axis_at in (source, target)]
    chosen = jax.random.permutation(stream_key, parts)[partner]
    strong = (owner == chosen) | (owner == (partner + parts // 2) % parts)
    return jnp.where(strong, factor * values, values)


def levels(stream_key, dims, pieces, least, top_value):
    loudness = 1.0
    for dim, blocks in pieces:
        draws = jax.random.uniform(jax.random.fold_in(jax.random.fold_in(stream_key, 6), dim), (blocks,), jnp.float32, least / len(pieces), top_value / len(pieces))
        loudness = loudness * jnp.repeat(jnp.exp(draws), dims[dim] // blocks).reshape((-1,) + (1,) * (len(dims) - 1 - dim))
    return loudness


def bell_draw(own_key, dims, spread, limit, pieces=(), kind=jnp.bfloat16):
    loudness = levels(own_key, dims, pieces, -0.22, 0.18) if pieces else 1.0
    values = jax.random.normal(own_key, dims, jnp.float32) * spread * loudness
    return jnp.minimum(jnp.maximum(values, -limit), limit).astype(kind)


def gaussian_with(rng, shape, deviation, bound, shards, heavy, kind=jnp.bfloat16):
    values = deviation * jax.random.normal(rng, shape, jnp.float32)
    if shards:
        values = values * levels(rng, shape, shards, -0.22, 0.18)
    return jnp.clip(strengthened(values, jax.random.fold_in(rng, 3), *heavy), -bound, bound).astype(kind)


def setup_inputs(seed: int = 0) -> dict:
    streams_of = jax.random.split(jax.random.key(seed), 12)
    block_input = bell_draw(streams_of[0], (GROUPS, GROUP_TOK, D), 1.0, 6.0, ((0, 8), (1, 4)))
    norm_gain_a = jnp.clip(1.0 + 0.18 * jax.random.normal(streams_of[1], (D,), jnp.float32), 0.1, 1.9)
    weight_qkv = bell_draw(streams_of[2], (D, 3 * D), D ** -0.5, 0.1875, ((0, 8),), jnp.float32)
    weight_out = bell_draw(streams_of[3], (D, D), (max(D // 256, 1)) ** -0.5, 3.0, ((0, 8),), jnp.float32)
    norm_gain_b = jnp.clip(1.0 + 0.18 * jax.random.normal(streams_of[4], (D,), jnp.float32), 0.1, 1.9)
    weight_gate_up = bell_draw(streams_of[5], (D, 2 * FF), D ** -0.5, 0.1875, ((0, 8),), jnp.float32)
    weight_down = bell_draw(streams_of[6], (D, FF), FF ** -0.5, 0.09375, ((0, 8),), jnp.float32)
    cotangent = gaussian_with(streams_of[7], (GROUPS, GROUP_TOK, D), 1.0, 6.0, ((0, 8), (1, 4)), (0, 2, 8, 2.0))
    permutation = jax.vmap(lambda own: jax.random.permutation(own, GROUP_TOK))(jax.random.split(streams_of[8], GROUPS)).reshape((GROUPS, GROUP_TOK)).astype(jnp.int32)
    lengths = draw_lengths(jax.random.fold_in(streams_of[11], 71), 0)
    offsets = draw_offsets(jax.random.fold_in(streams_of[11], 71), 0)
    return {"block_input": block_input, "norm_gain_a": norm_gain_a, "weight_qkv": weight_qkv, "weight_out": weight_out, "norm_gain_b": norm_gain_b, "weight_gate_up": weight_gate_up, "weight_down": weight_down, "cotangent": cotangent, "permutation": permutation, "lengths": lengths, "offsets": offsets}


@jax.custom_vjp
def low(v):
    return lax.optimization_barrier(v.astype(jnp.bfloat16)).astype(jnp.float32)

@jax.custom_vjp
def low_back(v):
    return v

def low_keep(v):
    return (low(v), None)

def low_pass(kept, grad):
    return (grad,)

def back_keep(v):
    return (v, None)

def back_low(kept, grad):
    return (low(grad),)
low.defvjp(low_keep, low_pass)
low_back.defvjp(back_keep, back_low)
epsilon = 1e-05
highest = lax.Precision.HIGHEST

def product(left, right):
    return jnp.dot(left, right, precision=highest)

def attention(queries, key_rows, values, segment, position):
    group_len = queries.shape[0]
    blk_rows = min(512, group_len)
    block_count = group_len // blk_rows
    score_scale = HEAD_DIM ** (-0.5)

    def one_block(block_item):
        query_blk, seg_blk, pos_blk = block_item
        scores = jnp.einsum('qhd,khd->hqk', query_blk, key_rows, precision=highest) * score_scale
        scores = low_back(scores)
        allowed = (seg_blk[:, None] == segment[None, :]) & (position[None, :] <= pos_blk[:, None])
        scores = jnp.where(allowed[None], scores, -1e+30)
        row_top = lax.optimization_barrier(jnp.max(scores, axis=-1, keepdims=True))
        exponent = jnp.exp(scores - row_top)
        probability = exponent / lax.optimization_barrier(jnp.sum(exponent, axis=-1, keepdims=True))
        return jnp.einsum('hqk,khd->qhd', low(probability), values, precision=highest)
    result = lax.map(jax.checkpoint(one_block), (queries.reshape(block_count, blk_rows, HEADS, HEAD_DIM), segment.reshape(block_count, blk_rows), position.reshape(block_count, blk_rows)))
    return result.reshape(group_len, HEADS * HEAD_DIM)

def group_forward(inputs, gain_a, weight_qkv, weight_out, gain_b, weight_gate_up, weight_down, permutation, lengths, offsets):
    group_len = inputs.shape[0]
    inv_first = lax.rsqrt(lax.optimization_barrier(jnp.mean(inputs * inputs, axis=-1, keepdims=True)) + epsilon)
    normed_a = low(inputs * inv_first * gain_a)
    qkv_rows = low(low_back(product(normed_a, weight_qkv)))
    position = jnp.arange(group_len, dtype=jnp.int32)
    inverse = jnp.zeros((group_len,), jnp.int32).at[permutation].set(position)
    ordered = qkv_rows[inverse].reshape(group_len, 3, HEADS, HEAD_DIM)
    inside = (position[:, None] >= offsets[None, :]) & (position[:, None] < offsets[None, :] + lengths[None, :])
    segment = lax.optimization_barrier(jnp.sum(inside.astype(jnp.int32) * jnp.arange(SEQS, dtype=jnp.int32)[None, :], axis=1))
    attended = attention(ordered[:, 0], ordered[:, 1], ordered[:, 2], segment, position)
    dealt = low(low_back(attended[permutation]))
    hidden = inputs + low_back(product(dealt, weight_out))
    inv_second = lax.rsqrt(lax.optimization_barrier(jnp.mean(hidden * hidden, axis=-1, keepdims=True)) + epsilon)
    normed_b = low(hidden * inv_second * gain_b)
    gate_up = low_back(product(normed_b, weight_gate_up))
    gate_part = gate_up[:, :FF]
    up_part = gate_up[:, FF:]
    activation = low(jax.nn.silu(gate_part) * up_part)
    return hidden + low_back(product(activation, weight_down.T))

def reference(block_input, norm_gain_a, weight_qkv, weight_out, norm_gain_b, weight_gate_up, weight_down, cotangent, permutation, lengths, offsets):
    inputs = block_input.astype(jnp.float32)
    seed_grad = cotangent.astype(jnp.float32)
    params = (norm_gain_a, weight_qkv, weight_out, norm_gain_b, weight_gate_up, weight_down)

    def forward(inputs, params):
        lowered = tuple((low(entry) for entry in params))
        stepper = jax.checkpoint(group_forward)

        def scan_step(carry, group_item):
            return (carry, stepper(group_item[0], lowered[0], lowered[1], lowered[2], lowered[3], lowered[4], lowered[5], group_item[1], group_item[2], group_item[3]))
        final_carry, outputs = lax.scan(scan_step, jnp.zeros((), jnp.float32), (inputs, permutation, lengths, offsets))
        return outputs
    outputs, pullback = jax.vjp(forward, inputs, params)
    input_grad, grads = pullback(seed_grad)
    return (outputs.astype(jnp.bfloat16), input_grad.astype(jnp.bfloat16), grads[0], grads[1], grads[2], grads[3], grads[4], grads[5])
```

```python
import jax
import jax.numpy as jnp
from jax import lax
from jax.experimental import pallas as pl
from jax.experimental.pallas import tpu as pltpu
from jax.sharding import PartitionSpec as P

HEAD_DIM = 64
BLK = 256
LOG2E = 1.4426950408889634

NT = (((1,), (1,)), ((), ()))
NN = (((1,), (0,)), ((), ()))


def dot(a, b, dims=NN):
    return lax.dot_general(a, b, dims, preferred_element_type=jnp.float32)


def first_block(offs_ref, row0):
    best = jnp.int32(0)
    for k in range(offs_ref.shape[0]):
        off = offs_ref[k]
        best = jnp.where(off <= row0, jnp.maximum(best, off), best)
    return best // BLK


def sort_rows(perm_row_ref, src_ref, dst_ref):
    group_len = src_ref.shape[0]

    def step(i, carry):
        rows = pl.ds(pl.multiple_of(i * BLK, BLK), BLK)
        pos = lax.broadcasted_iota(jnp.int32, (BLK, group_len), 0) + i * BLK
        pick = (perm_row_ref[...] == pos).astype(jnp.float32).astype(jnp.bfloat16)
        dst_ref[rows, :] = dot(pick, src_ref[...]).astype(dst_ref.dtype)
        return carry

    lax.fori_loop(0, group_len // BLK, step, 0)


def deal_rows(perm_col_ref, src_ref, dst_ref):
    group_len = src_ref.shape[0]

    def step(i, carry):
        rows = pl.ds(pl.multiple_of(i * BLK, BLK), BLK)
        pos = lax.broadcasted_iota(jnp.int32, (BLK, group_len), 1)
        pick = (perm_col_ref[rows, :] == pos).astype(jnp.float32).astype(jnp.bfloat16)
        dst_ref[rows, :] = dot(pick, src_ref[...]).astype(dst_ref.dtype)
        return carry

    lax.fori_loop(0, group_len // BLK, step, 0)


def allowed_block(start_ref, cols, qb, kb):
    key_pos = lax.broadcasted_iota(jnp.int32, (BLK, BLK), 0) + kb * BLK
    query_pos = lax.broadcasted_iota(jnp.int32, (BLK, BLK), 1) + qb * BLK
    return (key_pos <= query_pos) & (key_pos >= start_ref[:, cols])


def forward_kernel(offs_ref, qkv_ref, perm_row_ref, perm_col_ref, start_ref,
                   sorted_ref, dealt_ref, wide_ref, lse_ref, vt_ref, low_ref):
    group_len = qkv_ref.shape[0]
    width = qkv_ref.shape[1] // 3
    heads = width // HEAD_DIM
    scale = HEAD_DIM ** -0.5 * LOG2E
    sort_rows(perm_row_ref, qkv_ref, sorted_ref)

    def flip(i, carry):
        rows = pl.ds(pl.multiple_of(i * BLK, BLK), BLK)
        vt_ref[:, rows] = sorted_ref[rows, 2 * width:].T
        return carry

    lax.fori_loop(0, group_len // BLK, flip, 0)

    def query_step(qb, carry):
        qrow = pl.multiple_of(qb * BLK, BLK)
        cols = pl.ds(qrow, BLK)

        def key_step(kb, state):
            krow = pl.multiple_of(kb * BLK, BLK)
            krows = pl.ds(krow, BLK)
            allowed = allowed_block(start_ref, cols, qb, kb)
            fresh = []
            for h in range(heads):
                top, total, acc = state[3 * h: 3 * h + 3]
                hq = slice(h * HEAD_DIM, (h + 1) * HEAD_DIM)
                hk = slice(width + h * HEAD_DIM, width + (h + 1) * HEAD_DIM)
                s = dot(sorted_ref[krows, hk], sorted_ref[cols, hq], NT) * scale
                s = jnp.where(allowed, s, -1e30)
                new_top = jnp.maximum(top, jnp.max(s, axis=0, keepdims=True))
                shrink = jnp.exp2(top - new_top)
                p = jnp.exp2(s - new_top)
                total = total * shrink + jnp.sum(p, axis=0, keepdims=True)
                acc = acc * shrink + dot(vt_ref[hq, krows], p.astype(jnp.bfloat16))
                fresh += [new_top, total, acc]
            return tuple(fresh)

        init = []
        for h in range(heads):
            init += [jnp.full((1, BLK), -1e30, jnp.float32), jnp.zeros((1, BLK), jnp.float32),
                     jnp.zeros((HEAD_DIM, BLK), jnp.float32)]
        state = lax.fori_loop(first_block(offs_ref, qrow), qb + 1, key_step, tuple(init))
        parts = []
        for h in range(heads):
            top, total, acc = state[3 * h: 3 * h + 3]
            out = acc / total
            wide_ref[h * HEAD_DIM:(h + 1) * HEAD_DIM, cols] = out
            lse_ref[h:h + 1, cols] = top + jnp.log2(total)
            parts.append(out)
        low_ref[cols, :] = jnp.concatenate(parts, axis=0).T.astype(jnp.bfloat16)
        return carry

    lax.fori_loop(0, group_len // BLK, query_step, 0)
    deal_rows(perm_col_ref, low_ref, dealt_ref)


def backward_kernel(offs_ref, grad_ref, sorted_ref, perm_row_ref, perm_col_ref, start_ref, wide_ref, lse_ref,
                    dealt_ref, do_ref, kt_ref, delta_ref, dk_ref, dv_ref, low_ref):
    group_len = sorted_ref.shape[0]
    width = sorted_ref.shape[1] // 3
    heads = width // HEAD_DIM
    unit = HEAD_DIM ** -0.5
    scale = unit * LOG2E
    sort_rows(perm_row_ref, grad_ref, do_ref)
    dk_ref[...] = jnp.zeros_like(dk_ref)
    dv_ref[...] = jnp.zeros_like(dv_ref)

    def flip(i, carry):
        rows = pl.ds(pl.multiple_of(i * BLK, BLK), BLK)
        kt_ref[:, rows] = sorted_ref[rows, width: 2 * width].T
        product = do_ref[rows, :].astype(jnp.float32).T * wide_ref[:, rows]
        for h in range(heads):
            delta_ref[h:h + 1, rows] = jnp.sum(product[h * HEAD_DIM:(h + 1) * HEAD_DIM], axis=0, keepdims=True)
        return carry

    lax.fori_loop(0, group_len // BLK, flip, 0)

    def query_step(qb, carry):
        qrow = pl.multiple_of(qb * BLK, BLK)
        cols = pl.ds(qrow, BLK)

        def key_step(kb, state):
            krow = pl.multiple_of(kb * BLK, BLK)
            krows = pl.ds(krow, BLK)
            allowed = allowed_block(start_ref, cols, qb, kb)
            fresh = []
            for h in range(heads):
                hq = slice(h * HEAD_DIM, (h + 1) * HEAD_DIM)
                hk = slice(width + h * HEAD_DIM, width + (h + 1) * HEAD_DIM)
                hv = slice(2 * width + h * HEAD_DIM, 2 * width + (h + 1) * HEAD_DIM)
                q = sorted_ref[cols, hq]
                do = do_ref[cols, hq]
                s = dot(sorted_ref[krows, hk], q, NT) * scale
                s = jnp.where(allowed, s, -1e30)
                p = jnp.exp2(s - lse_ref[h:h + 1, cols])
                dp = dot(sorted_ref[krows, hv], do, NT)
                ds = (p * (dp - delta_ref[h:h + 1, cols])).astype(jnp.bfloat16)
                dv_ref[krows, hq] += dot(p.astype(jnp.bfloat16), do)
                dk_ref[krows, hq] += dot(ds, q)
                fresh.append(state[h] + dot(kt_ref[hq, krows], ds))
            return tuple(fresh)

        state = lax.fori_loop(first_block(offs_ref, qrow), qb + 1, key_step,
                              tuple(jnp.zeros((HEAD_DIM, BLK), jnp.float32) for _ in range(heads)))
        low_ref[cols, :width] = (jnp.concatenate(state, axis=0) * unit).T.astype(jnp.bfloat16)
        return carry

    lax.fori_loop(0, group_len // BLK, query_step, 0)
    low_ref[:, width:2 * width] = (dk_ref[...] * unit).astype(jnp.bfloat16)
    low_ref[:, 2 * width:] = dv_ref[...].astype(jnp.bfloat16)
    deal_rows(perm_col_ref, low_ref, dealt_ref)


def vmem():
    return pl.BlockSpec(memory_space=pltpu.VMEM)


def attention_forward(offs, qkv, perm, start):
    group_len, columns = qkv.shape
    width = columns // 3
    return pl.pallas_call(
        forward_kernel,
        name="attention_forward",
        out_shape=(
            jax.ShapeDtypeStruct((group_len, columns), jnp.bfloat16),
            jax.ShapeDtypeStruct((group_len, width), jnp.bfloat16),
            jax.ShapeDtypeStruct((width, group_len), jnp.float32),
            jax.ShapeDtypeStruct((8, group_len), jnp.float32),
        ),
        in_specs=[pl.BlockSpec(memory_space=pltpu.SMEM)] + [vmem()] * 4,
        out_specs=(vmem(),) * 4,
        scratch_shapes=[pltpu.VMEM((width, group_len), jnp.bfloat16), pltpu.VMEM((group_len, width), jnp.bfloat16)],
        compiler_params=pltpu.CompilerParams(vmem_limit_bytes=48 << 20),
        cost_estimate=pl.CostEstimate(flops=20_000_000_000, bytes_accessed=16 << 20, transcendentals=0),
    )(offs, qkv, perm.reshape(1, group_len), perm.reshape(group_len, 1), start.reshape(1, group_len))


def attention_backward(offs, grad, ordered, perm, start, wide, lse):
    group_len, columns = ordered.shape
    width = columns // 3
    return pl.pallas_call(
        backward_kernel,
        name="attention_backward",
        out_shape=jax.ShapeDtypeStruct((group_len, columns), jnp.bfloat16),
        in_specs=[pl.BlockSpec(memory_space=pltpu.SMEM)] + [vmem()] * 7,
        out_specs=vmem(),
        scratch_shapes=[
            pltpu.VMEM((group_len, width), jnp.bfloat16),
            pltpu.VMEM((width, group_len), jnp.bfloat16),
            pltpu.VMEM((8, group_len), jnp.float32),
            pltpu.VMEM((group_len, width), jnp.float32),
            pltpu.VMEM((group_len, width), jnp.float32),
            pltpu.VMEM((group_len, columns), jnp.bfloat16),
        ],
        compiler_params=pltpu.CompilerParams(vmem_limit_bytes=48 << 20),
        cost_estimate=pl.CostEstimate(flops=40_000_000_000, bytes_accessed=16 << 20, transcendentals=0),
    )(offs, grad, ordered, perm.reshape(1, group_len), perm.reshape(group_len, 1), start.reshape(1, group_len), wide, lse)


epsilon = 1e-05


def rms_scale(values):
    return lax.rsqrt(jnp.mean(values * values, axis=-1, keepdims=True) + epsilon)


def norm_backward(values, inv_scale, grad_normed, gain):
    scaled = grad_normed * gain
    gain_grad = jnp.sum(grad_normed * values * inv_scale, axis=0)
    input_grad = inv_scale * scaled - values * inv_scale**3 * jnp.mean(values * scaled, axis=-1, keepdims=True)
    return (input_grad, gain_grad)


def matmul(spec, left, right):
    return jnp.einsum(spec, left, right, preferred_element_type=jnp.float32)


def on_device(block_input, norm_gain_a, weight_qkv, weight_out, norm_gain_b, weight_gate_up, weight_down,
              cotangent, permutation, lengths, offsets):
    low = jnp.bfloat16
    seq_count = lax.axis_size("seq")
    mine = lax.axis_index("seq")
    row_count, model_width = block_input.shape[1:]
    group_len = row_count * seq_count
    shard = weight_qkv.shape[0]
    head_width = weight_qkv.shape[1] // 3 // seq_count
    part_units = weight_down.shape[1] // seq_count
    perm = permutation[0]
    offs = offsets[0]
    position = jnp.arange(group_len, dtype=jnp.int32)
    start = jnp.max(jnp.where(offs[None, :] <= position[:, None], offs[None, :], 0), axis=1)

    def columns(weight, blocks, width):
        cut = weight.reshape(shard, blocks, seq_count, width)
        return lax.dynamic_index_in_dim(cut, mine, 2, keepdims=False).reshape(shard, blocks * width).astype(low)

    gather_weight = lambda piece: lax.all_gather(piece, "fsdp", axis=0, tiled=True)
    gather_rows = lambda rows: lax.all_gather(rows, "seq", axis=0, tiled=True)
    scatter_rows = lambda part: lax.psum_scatter(part.astype(low), "seq", scatter_dimension=0, tiled=True)

    gains = gather_weight(jnp.stack([norm_gain_a, norm_gain_b], axis=1)).astype(low).astype(jnp.float32)
    gain_a, gain_b = gains[:, 0], gains[:, 1]
    rows_all = gather_rows(block_input[0])
    part_qkv = gather_weight(columns(weight_qkv, 3, head_width))
    full_out = gather_weight(weight_out.astype(low))
    part_gate_up = gather_weight(columns(weight_gate_up, 2, part_units))
    part_down = gather_weight(columns(weight_down, 1, part_units))
    grad_rows_all = gather_rows(cotangent[0])

    wide_all = rows_all.astype(jnp.float32)
    normed_a = (wide_all * rms_scale(wide_all) * gain_a).astype(low)
    qkv = matmul("rd,de->re", normed_a, part_qkv).astype(low)
    ordered, dealt_out, wide_out, log_total = attention_forward(offs, qkv, perm, start)
    mixed = lax.all_to_all(
        dealt_out.reshape(group_len, 1, head_width), "seq", split_axis=0, concat_axis=1, tiled=True
    ).reshape(row_count, model_width)
    inputs = block_input[0].astype(jnp.float32)
    inv_first = rms_scale(inputs)
    hidden = inputs + matmul("rd,de->re", mixed, full_out)
    inv_second = rms_scale(hidden)
    normed_b = gather_rows((hidden * inv_second * gain_b).astype(low))

    gate_up = matmul("rd,df->rf", normed_b, part_gate_up)
    gate_part, up_part = gate_up[:, :part_units], gate_up[:, part_units:]
    gate_sigmoid = jax.nn.sigmoid(gate_part)
    gate_silu = gate_part * gate_sigmoid
    activation = (gate_silu * up_part).astype(low)
    branch_out = scatter_rows(matmul("rf,df->rd", activation, part_down)).astype(jnp.float32)
    result_rows = (hidden + branch_out).astype(low)

    grad_activation = matmul("rd,df->rf", grad_rows_all, part_down)
    grad_gate = grad_activation * up_part * gate_sigmoid * (1.0 + gate_part * (1.0 - gate_sigmoid))
    grad_up = grad_activation * gate_silu
    grad_gate_up = jnp.concatenate([grad_gate, grad_up], axis=1).astype(low)
    grad_normed_b = scatter_rows(matmul("rf,df->rd", grad_gate_up, part_gate_up)).astype(jnp.float32)
    down_term = matmul("rd,rf->df", grad_rows_all, activation)
    gate_up_term = matmul("rd,rf->df", normed_b, grad_gate_up)
    hidden_back, gain_b_term = norm_backward(hidden, inv_second, grad_normed_b, gain_b)
    grad_hidden = cotangent[0].astype(jnp.float32) + hidden_back
    grad_branch = grad_hidden.astype(low)
    grad_mixed = matmul("re,de->rd", grad_branch, full_out).astype(low)
    grad_heads = lax.all_to_all(
        grad_mixed.reshape(row_count, seq_count, head_width), "seq", split_axis=1, concat_axis=0, tiled=True
    ).reshape(group_len, head_width)
    dealt_grad = attention_backward(offs, grad_heads, ordered, perm, start, wide_out, log_total)
    out_term = matmul("rd,re->de", mixed, grad_branch)
    out_part = lax.psum_scatter(out_term.astype(low), "seq", scatter_dimension=1, tiled=True)
    qkv_term = matmul("rd,re->de", normed_a, dealt_grad)
    grad_normed_a = scatter_rows(matmul("re,de->rd", dealt_grad, part_qkv)).astype(jnp.float32)
    input_back, gain_a_term = norm_backward(inputs, inv_first, grad_normed_a, gain_a)
    input_grad = (grad_hidden + input_back).astype(low)

    def finish(term):
        piece = lax.psum_scatter(term.astype(low), "fsdp", scatter_dimension=0, tiled=True)
        return lax.all_gather(piece, "seq", axis=0, tiled=False)

    def spread(pieces, blocks):
        width = pieces.shape[-1] // blocks
        return pieces.reshape(seq_count, shard, blocks, width).transpose(1, 2, 0, 3).reshape(
            shard, -1).astype(jnp.float32)

    grad_mlp = finish(jnp.concatenate([gate_up_term, down_term], axis=1))
    grad_attn = finish(jnp.concatenate([qkv_term.astype(low), out_part], axis=1))
    gain_terms = lax.psum(jnp.stack([gain_a_term, gain_b_term]), ("seq", "fsdp"))
    gain_terms = lax.dynamic_slice_in_dim(gain_terms, lax.axis_index("fsdp") * shard, shard, axis=1)
    return (
        result_rows[None],
        input_grad[None],
        gain_terms[0],
        spread(grad_attn[:, :, : 3 * head_width], 3),
        spread(grad_attn[:, :, 3 * head_width:], 1),
        gain_terms[1],
        spread(grad_mlp[:, :, : 2 * part_units], 2),
        spread(grad_mlp[:, :, 2 * part_units:], 1),
    )


def solution(mesh):
    rows = P("fsdp", "seq", None)
    vector = P("fsdp")
    matrix = P("fsdp", None)
    return jax.shard_map(
        on_device,
        mesh=mesh,
        in_specs=(rows, vector, matrix, matrix, vector, matrix, matrix, rows, matrix, matrix, matrix),
        out_specs=(rows, rows, vector, matrix, matrix, vector, matrix, matrix),
        check_vma=False,
    )
```

```python
import jax
import jax.numpy as jnp
from jax import lax
from jax.experimental import pallas as pl
from jax.experimental.pallas import tpu as pltpu
from jax.sharding import PartitionSpec as P

HEAD_DIM = 64
BLK = 256
LOG2E = 1.4426950408889634

NT = (((1,), (1,)), ((), ()))
NN = (((1,), (0,)), ((), ()))


def dot(a, b, dims=NN):
    return lax.dot_general(a, b, dims, preferred_element_type=jnp.float32)


def first_block(offs_ref, row0):
    best = jnp.int32(0)
    for k in range(offs_ref.shape[0]):
        off = offs_ref[k]
        best = jnp.where(off <= row0, jnp.maximum(best, off), best)
    return best // BLK


def sort_rows(perm_row_ref, src_ref, dst_ref):
    group_len = src_ref.shape[0]

    def step(i, carry):
        rows = pl.ds(pl.multiple_of(i * BLK, BLK), BLK)
        pos = lax.broadcasted_iota(jnp.int32, (BLK, group_len), 0) + i * BLK
        pick = (perm_row_ref[...] == pos).astype(jnp.float32).astype(jnp.bfloat16)
        dst_ref[rows, :] = dot(pick, src_ref[...]).astype(dst_ref.dtype)
        return carry

    lax.fori_loop(0, group_len // BLK, step, 0)


def deal_rows(perm_col_ref, src_ref, dst_ref):
    group_len = src_ref.shape[0]

    def step(i, carry):
        rows = pl.ds(pl.multiple_of(i * BLK, BLK), BLK)
        pos = lax.broadcasted_iota(jnp.int32, (BLK, group_len), 1)
        pick = (perm_col_ref[rows, :] == pos).astype(jnp.float32).astype(jnp.bfloat16)
        dst_ref[rows, :] = dot(pick, src_ref[...]).astype(dst_ref.dtype)
        return carry

    lax.fori_loop(0, group_len // BLK, step, 0)


def allowed_block(start_ref, cols, qb, kb):
    key_pos = lax.broadcasted_iota(jnp.int32, (BLK, BLK), 0) + kb * BLK
    query_pos = lax.broadcasted_iota(jnp.int32, (BLK, BLK), 1) + qb * BLK
    return (key_pos <= query_pos) & (key_pos >= start_ref[:, cols])


def forward_kernel(offs_ref, qkv_ref, perm_row_ref, perm_col_ref, start_ref,
                   sorted_ref, dealt_ref, wide_ref, lse_ref, vt_ref, low_ref):
    group_len = qkv_ref.shape[0]
    width = qkv_ref.shape[1] // 3
    heads = width // HEAD_DIM
    scale = HEAD_DIM ** -0.5 * LOG2E
    sort_rows(perm_row_ref, qkv_ref, sorted_ref)

    def flip(i, carry):
        rows = pl.ds(pl.multiple_of(i * BLK, BLK), BLK)
        vt_ref[:, rows] = sorted_ref[rows, 2 * width:].T
        return carry

    lax.fori_loop(0, group_len // BLK, flip, 0)

    def query_step(qb, carry):
        qrow = pl.multiple_of(qb * BLK, BLK)
        cols = pl.ds(qrow, BLK)

        def key_step(kb, state):
            krow = pl.multiple_of(kb * BLK, BLK)
            krows = pl.ds(krow, BLK)
            allowed = allowed_block(start_ref, cols, qb, kb)
            fresh = []
            for h in range(heads):
                top, total, acc = state[3 * h: 3 * h + 3]
                hq = slice(h * HEAD_DIM, (h + 1) * HEAD_DIM)
                hk = slice(width + h * HEAD_DIM, width + (h + 1) * HEAD_DIM)
                s = dot(sorted_ref[krows, hk], sorted_ref[cols, hq], NT) * scale
                s = jnp.where(allowed, s, -1e30)
                new_top = jnp.maximum(top, jnp.max(s, axis=0, keepdims=True))
                shrink = jnp.exp2(top - new_top)
                p = jnp.exp2(s - new_top)
                total = total * shrink + jnp.sum(p, axis=0, keepdims=True)
                acc = acc * shrink + dot(vt_ref[hq, krows], p.astype(jnp.bfloat16))
                fresh += [new_top, total, acc]
            return tuple(fresh)

        init = []
        for h in range(heads):
            init += [jnp.full((1, BLK), -1e30, jnp.float32), jnp.zeros((1, BLK), jnp.float32),
                     jnp.zeros((HEAD_DIM, BLK), jnp.float32)]
        state = lax.fori_loop(first_block(offs_ref, qrow), qb + 1, key_step, tuple(init))
        parts = []
        for h in range(heads):
            top, total, acc = state[3 * h: 3 * h + 3]
            out = acc / total
            wide_ref[h * HEAD_DIM:(h + 1) * HEAD_DIM, cols] = out
            lse_ref[h:h + 1, cols] = top + jnp.log2(total)
            parts.append(out)
        low_ref[cols, :] = jnp.concatenate(parts, axis=0).T.astype(jnp.bfloat16)
        return carry

    lax.fori_loop(0, group_len // BLK, query_step, 0)
    deal_rows(perm_col_ref, low_ref, dealt_ref)


def backward_kernel(offs_ref, grad_ref, sorted_ref, perm_row_ref, perm_col_ref, start_ref, wide_ref, lse_ref,
                    dealt_ref, do_ref, kt_ref, delta_ref, dk_ref, dv_ref, low_ref):
    group_len = sorted_ref.shape[0]
    width = sorted_ref.shape[1] // 3
    heads = width // HEAD_DIM
    unit = HEAD_DIM ** -0.5
    scale = unit * LOG2E
    sort_rows(perm_row_ref, grad_ref, do_ref)
    dk_ref[...] = jnp.zeros_like(dk_ref)
    dv_ref[...] = jnp.zeros_like(dv_ref)

    def flip(i, carry):
        rows = pl.ds(pl.multiple_of(i * BLK, BLK), BLK)
        kt_ref[:, rows] = sorted_ref[rows, width: 2 * width].T
        product = do_ref[rows, :].astype(jnp.float32).T * wide_ref[:, rows]
        for h in range(heads):
            delta_ref[h:h + 1, rows] = jnp.sum(product[h * HEAD_DIM:(h + 1) * HEAD_DIM], axis=0, keepdims=True)
        return carry

    lax.fori_loop(0, group_len // BLK, flip, 0)

    def query_step(qb, carry):
        qrow = pl.multiple_of(qb * BLK, BLK)
        cols = pl.ds(qrow, BLK)

        def key_step(kb, state):
            krow = pl.multiple_of(kb * BLK, BLK)
            krows = pl.ds(krow, BLK)
            allowed = allowed_block(start_ref, cols, qb, kb)
            fresh = []
            for h in range(heads):
                hq = slice(h * HEAD_DIM, (h + 1) * HEAD_DIM)
                hk = slice(width + h * HEAD_DIM, width + (h + 1) * HEAD_DIM)
                hv = slice(2 * width + h * HEAD_DIM, 2 * width + (h + 1) * HEAD_DIM)
                q = sorted_ref[cols, hq]
                do = do_ref[cols, hq]
                s = dot(sorted_ref[krows, hk], q, NT) * scale
                s = jnp.where(allowed, s, -1e30)
                p = jnp.exp2(s - lse_ref[h:h + 1, cols])
                dp = dot(sorted_ref[krows, hv], do, NT)
                ds = (p * (dp - delta_ref[h:h + 1, cols])).astype(jnp.bfloat16)
                dv_ref[krows, hq] += dot(p.astype(jnp.bfloat16), do)
                dk_ref[krows, hq] += dot(ds, q)
                fresh.append(state[h] + dot(kt_ref[hq, krows], ds))
            return tuple(fresh)

        state = lax.fori_loop(first_block(offs_ref, qrow), qb + 1, key_step,
                              tuple(jnp.zeros((HEAD_DIM, BLK), jnp.float32) for _ in range(heads)))
        low_ref[cols, :width] = (jnp.concatenate(state, axis=0) * unit).T.astype(jnp.bfloat16)
        return carry

    lax.fori_loop(0, group_len // BLK, query_step, 0)
    low_ref[:, width:2 * width] = (dk_ref[...] * unit).astype(jnp.bfloat16)
    low_ref[:, 2 * width:] = dv_ref[...].astype(jnp.bfloat16)
    deal_rows(perm_col_ref, low_ref, dealt_ref)


def vmem():
    return pl.BlockSpec(memory_space=pltpu.VMEM)


def attention_forward(offs, qkv, perm, start):
    group_len, columns = qkv.shape
    width = columns // 3
    return pl.pallas_call(
        forward_kernel,
        name="attention_forward",
        out_shape=(
            jax.ShapeDtypeStruct((group_len, columns), jnp.bfloat16),
            jax.ShapeDtypeStruct((group_len, width), jnp.bfloat16),
            jax.ShapeDtypeStruct((width, group_len), jnp.float32),
            jax.ShapeDtypeStruct((8, group_len), jnp.float32),
        ),
        in_specs=[pl.BlockSpec(memory_space=pltpu.SMEM)] + [vmem()] * 4,
        out_specs=(vmem(),) * 4,
        scratch_shapes=[pltpu.VMEM((width, group_len), jnp.bfloat16), pltpu.VMEM((group_len, width), jnp.bfloat16)],
        compiler_params=pltpu.CompilerParams(vmem_limit_bytes=48 << 20),
        cost_estimate=pl.CostEstimate(flops=20_000_000_000, bytes_accessed=16 << 20, transcendentals=0),
    )(offs, qkv, perm.reshape(1, group_len), perm.reshape(group_len, 1), start.reshape(1, group_len))


def attention_backward(offs, grad, ordered, perm, start, wide, lse):
    group_len, columns = ordered.shape
    width = columns // 3
    return pl.pallas_call(
        backward_kernel,
        name="attention_backward",
        out_shape=jax.ShapeDtypeStruct((group_len, columns), jnp.bfloat16),
        in_specs=[pl.BlockSpec(memory_space=pltpu.SMEM)] + [vmem()] * 7,
        out_specs=vmem(),
        scratch_shapes=[
            pltpu.VMEM((group_len, width), jnp.bfloat16),
            pltpu.VMEM((width, group_len), jnp.bfloat16),
            pltpu.VMEM((8, group_len), jnp.float32),
            pltpu.VMEM((group_len, width), jnp.float32),
            pltpu.VMEM((group_len, width), jnp.float32),
            pltpu.VMEM((group_len, columns), jnp.bfloat16),
        ],
        compiler_params=pltpu.CompilerParams(vmem_limit_bytes=48 << 20),
        cost_estimate=pl.CostEstimate(flops=40_000_000_000, bytes_accessed=16 << 20, transcendentals=0),
    )(offs, grad, ordered, perm.reshape(1, group_len), perm.reshape(group_len, 1), start.reshape(1, group_len), wide, lse)


epsilon = 1e-05


def rms_scale(values):
    return lax.rsqrt(jnp.mean(values * values, axis=-1, keepdims=True) + epsilon)


def norm_backward(values, inv_scale, grad_normed, gain):
    scaled = grad_normed * gain
    gain_grad = jnp.sum(grad_normed * values * inv_scale, axis=0)
    input_grad = inv_scale * scaled - values * inv_scale**3 * jnp.mean(values * scaled, axis=-1, keepdims=True)
    return (input_grad, gain_grad)

MESH = pl.DeviceIdType.MESH
TN = (((0,), (0,)), ((), ()))
TILE = 256


def seq_peers():
    mine = lax.axis_index("seq")
    return mine, (mine + 1 - 2 * lax.rem(mine, 2), lax.rem(mine + 2, 4), 3 - mine)


def greet(peers, axis):
    barrier = pltpu.get_barrier_semaphore()
    for peer in peers:
        pl.semaphore_signal(barrier, inc=1, device_id={axis: peer}, device_id_type=MESH)
    pl.semaphore_wait(barrier, len(peers))


def middle_kernel(out_ref, x_ref, weight_ref, gain_ref, dy0_ref, dy1_ref, dy2_ref, dy3_ref,
                  hidden_ref, branch_ref, grad_gate_up_ref, grad_down_ref, grad_out_ref, dh_ref, do_ref, gain_grad_ref,
                  heads_ref, normed_ref, act_ref, dgu_ref, give_ref, take_ref, own_ref, do_give_ref,
                  send_sem, recv_sem):
    low = jnp.bfloat16
    rows, model = x_ref.shape
    width = out_ref.shape[1]
    units = grad_down_ref.shape[1]
    gate_at, up_at, down_at = model, model + units, model + 2 * units
    dy_refs = (dy0_ref, dy1_ref, dy2_ref, dy3_ref)
    mine, peers = seq_peers()
    half = rows // 2
    top, bottom = pl.ds(0, half), pl.ds(half, half)

    def send(index, src, dst, peer):
        return pltpu.make_async_remote_copy(
            src_ref=src, dst_ref=dst, send_sem=send_sem.at[index], recv_sem=recv_sem.at[index],
            device_id={"seq": peer}, device_id_type=MESH)

    def rows_of(peer, size):
        return pl.ds(pl.multiple_of(peer * size, size), size)

    def tiles(count, body):
        def step(i, carry):
            body(pl.multiple_of(i * TILE, TILE))
            return carry
        lax.fori_loop(0, count // TILE, step, 0)

    greet(peers, "seq")
    turn = [send(k, out_ref.at[rows_of(peer, rows), :], heads_ref.at[k], peer) for k, peer in enumerate(peers)]
    for k in (2, 0, 1):
        turn[k].start()

    def project(source, peer, base):
        def body(c):
            cols = pl.ds(c, TILE)
            hidden_ref[:, cols] = base(cols) + dot(source, weight_ref[rows_of(peer, width), cols])
        tiles(model, body)

    project(out_ref[rows_of(mine, rows), :], mine, lambda cols: x_ref[:, cols].astype(jnp.float32))
    for k, peer in enumerate(peers):
        turn[k].wait()
        project(heads_ref[k], peer, lambda cols: hidden_ref[:, cols])

    def norm(i, carry):
        part = pl.ds(pl.multiple_of(i * 128, 128), 128)
        h = hidden_ref[part, :]
        normed_ref[0, part, :] = (h * rms_scale(h) * gain_ref[...]).astype(low)
        return carry

    lax.fori_loop(0, rows // 128, norm, 0)

    px, py, pd = peers
    x_top = send(3, normed_ref.at[0, top], normed_ref.at[1, top], px)
    y_bottom = send(4, normed_ref.at[0, bottom], normed_ref.at[2, bottom], py)
    x_bottom = send(5, normed_ref.at[0, bottom], normed_ref.at[1, bottom], px)
    y_top = send(6, normed_ref.at[0, top], normed_ref.at[2, top], py)
    for copy in (x_top, y_bottom, x_bottom, y_top):
        copy.start()

    def feed(slot):
        def body(f):
            gate = dot(normed_ref[slot], weight_ref[:, pl.ds(gate_at + f, TILE)])
            up = dot(normed_ref[slot], weight_ref[:, pl.ds(up_at + f, TILE)])
            grad_act = dot(dy_refs[slot][...], weight_ref[:, pl.ds(down_at + f, TILE)])
            sigmoid = jax.nn.sigmoid(gate)
            silu = gate * sigmoid
            act_ref[slot, :, pl.ds(f, TILE)] = (silu * up).astype(low)
            dgu_ref[slot, :, pl.ds(f, TILE)] = (
                grad_act * up * sigmoid * (1.0 + gate * (1.0 - sigmoid))).astype(low)
            dgu_ref[slot, :, pl.ds(units + f, TILE)] = (grad_act * silu).astype(low)
        tiles(units, body)

    def back(slot, store):
        def body(c):
            cols = pl.ds(c, TILE)
            store(cols, dot(dgu_ref[slot], weight_ref[cols, gate_at:down_at], NT))
        tiles(model, body)

    def keep(cols, value):
        own_ref[:, cols] = value

    def branch(slot):
        def body(c):
            cols = pl.ds(c, TILE)
            branch_ref[slot, :, cols] = dot(act_ref[slot], weight_ref[cols, down_at:], NT).astype(low)
        tiles(model, body)

    feed(0)
    back(0, keep)
    x_top.wait_recv()
    x_relay = send(7, normed_ref.at[1, top], normed_ref.at[3, top], py)
    x_relay.start()
    y_bottom.wait_recv()
    y_relay = send(8, normed_ref.at[2, bottom], normed_ref.at[3, bottom], px)
    y_relay.start()
    branch(0)
    partials = [send(9 + k, give_ref.at[k], take_ref.at[k], peer) for k, peer in enumerate(peers)]
    waits = ((x_bottom,), (y_top,), (x_relay, y_relay))
    for k in range(3):
        for copy in waits[k]:
            copy.wait_recv()
        feed(k + 1)

        def hand(cols, value, k=k):
            give_ref[k, :, cols] = value.astype(low)

        back(k + 1, hand)
        partials[k].start()
    for copy in (x_top, y_bottom, x_bottom, y_top, x_relay, y_relay):
        copy.wait_send()

    def gate_up_grad(f):
        for d in range(0, model, 512):
            part = pl.ds(d, 512)
            acc = dot(normed_ref[0, :, part], dgu_ref[0, :, pl.ds(f, TILE)], TN)
            for slot in range(1, 4):
                acc += dot(normed_ref[slot, :, part], dgu_ref[slot, :, pl.ds(f, TILE)], TN)
            grad_gate_up_ref[part, pl.ds(f, TILE)] = acc.astype(low)

    tiles(2 * units, gate_up_grad)
    for slot in range(1, 4):
        branch(slot)
    for copy in partials:
        copy.wait()

    gain_grad_ref[...] = jnp.zeros_like(gain_grad_ref)

    def norm_back(i, carry):
        part = pl.ds(pl.multiple_of(i * 64, 64), 64)
        h = hidden_ref[part, :]
        inv = rms_scale(h)
        grad = own_ref[part, :]
        for k in range(3):
            grad += take_ref[k, part, :].astype(jnp.float32)
        gain_grad_ref[0:1, :] += jnp.sum(grad * h * inv, axis=0, keepdims=True)
        scaled = grad * gain_ref[...]
        dh = dy0_ref[part, :].astype(jnp.float32) + (
            inv * scaled - h * inv**3 * jnp.mean(h * scaled, axis=-1, keepdims=True))
        dh_ref[part, :] = dh
        normed_ref[1, part, :] = dh.astype(low)
        return carry

    lax.fori_loop(0, rows // 64, norm_back, 0)

    sends = [send(12 + k, do_give_ref.at[k], do_ref.at[rows_of(mine, rows), :], peer) for k, peer in enumerate(peers)]
    for k in (2, 0, 1):
        do_give_ref[k] = dot(normed_ref[1], weight_ref[rows_of(peers[k], width), :model], NT).astype(low)
        sends[k].start()
    do_ref[rows_of(mine, rows), :] = dot(normed_ref[1], weight_ref[rows_of(mine, width), :model], NT).astype(low)

    def down_grad(f):
        for d in range(0, model, 512):
            part = pl.ds(d, 512)
            acc = dot(dy_refs[0][:, part], act_ref[0, :, pl.ds(f, TILE)], TN)
            for slot in range(1, 4):
                acc += dot(dy_refs[slot][:, part], act_ref[slot, :, pl.ds(f, TILE)], TN)
            grad_down_ref[part, pl.ds(f, TILE)] = acc.astype(low)

    tiles(units, down_grad)
    grad_out_ref[rows_of(mine, width), :] = dot(out_ref[rows_of(mine, rows), :], normed_ref[1], TN).astype(low)
    for k, peer in enumerate(peers):
        grad_out_ref[rows_of(peer, width), :] = dot(heads_ref[k], normed_ref[1], TN).astype(low)
    for copy in sends:
        copy.wait()


def middle(dealt_out, x, weights, gain, dy, units):
    low = jnp.bfloat16
    group_len, width = dealt_out.shape
    rows, model = x.shape
    f32 = jnp.float32
    shape = jax.ShapeDtypeStruct
    return pl.pallas_call(
        middle_kernel,
        name="middle",
        out_shape=(
            shape((rows, model), f32),
            shape((4, rows, model), low),
            shape((model, 2 * units), low),
            shape((model, units), low),
            shape((model, model), low),
            shape((rows, model), f32),
            shape((group_len, width), low),
            shape((8, model), f32),
        ),
        in_specs=[vmem()] * 8,
        out_specs=(vmem(),) * 8,
        scratch_shapes=[
            pltpu.VMEM((3, rows, width), low),
            pltpu.VMEM((4, rows, model), low),
            pltpu.VMEM((4, rows, units), low),
            pltpu.VMEM((4, rows, 2 * units), low),
            pltpu.VMEM((3, rows, model), low),
            pltpu.VMEM((3, rows, model), low),
            pltpu.VMEM((rows, model), f32),
            pltpu.VMEM((3, rows, width), low),
            pltpu.SemaphoreType.DMA((15,)),
            pltpu.SemaphoreType.DMA((15,)),
        ],
        compiler_params=pltpu.CompilerParams(
            vmem_limit_bytes=62 << 20, collective_id=1, has_side_effects=True),
        cost_estimate=pl.CostEstimate(flops=60_000_000_000, bytes_accessed=40 << 20, transcendentals=0),
    )(dealt_out, x, weights, gain, *dy)


def matmul(spec, left, right):
    return jnp.einsum(spec, left, right, preferred_element_type=jnp.float32)


def swaps(rows):
    return [lax.ppermute(piece, "seq", table) for piece, table in zip(
        rows, ([(i, i ^ 1) for i in range(4)], [(i, (i + 2) % 4) for i in range(4)], [(i, 3 - i) for i in range(4)]))]


def on_device(block_input, norm_gain_a, weight_qkv, weight_out, norm_gain_b, weight_gate_up, weight_down,
              cotangent, permutation, lengths, offsets):
    low = jnp.bfloat16
    seq_count = lax.axis_size("seq")
    mine = lax.axis_index("seq")
    row_count, model_width = block_input.shape[1:]
    group_len = row_count * seq_count
    shard = weight_qkv.shape[0]
    head_width = weight_qkv.shape[1] // 3 // seq_count
    part_units = weight_down.shape[1] // seq_count
    perm = permutation[0]
    offs = offsets[0]
    position = jnp.arange(group_len, dtype=jnp.int32)
    start = jnp.max(jnp.where(offs[None, :] <= position[:, None], offs[None, :], 0), axis=1)

    def columns(weight, blocks, width):
        cut = weight.reshape(shard, blocks, seq_count, width)
        return lax.dynamic_index_in_dim(cut, mine, 2, keepdims=False).reshape(shard, blocks * width).astype(low)

    gather_weight = lambda piece: lax.all_gather(piece, "fsdp", axis=0, tiled=True)
    gather_rows = lambda rows: lax.all_gather(rows, "seq", axis=0, tiled=True)
    scatter_rows = lambda part: lax.psum_scatter(part.astype(low), "seq", scatter_dimension=0, tiled=True)

    gains = gather_weight(jnp.stack([norm_gain_a, norm_gain_b], axis=1)).astype(low).astype(jnp.float32)
    gain_a, gain_b = gains[:, 0], gains[:, 1]
    rows_all = gather_rows(block_input[0])
    part_qkv = gather_weight(columns(weight_qkv, 3, head_width))
    weights = gather_weight(jnp.concatenate(
        [weight_out.astype(low), columns(weight_gate_up, 2, part_units), columns(weight_down, 1, part_units)], axis=1))
    grad_rows = [cotangent[0]] + swaps([cotangent[0]] * 3)

    wide_all = rows_all.astype(jnp.float32)
    normed_a = (wide_all * rms_scale(wide_all) * gain_a).astype(low)
    qkv = matmul("rd,de->re", normed_a, part_qkv).astype(low)
    ordered, dealt_out, wide_out, log_total = attention_forward(offs, qkv, perm, start)
    hidden, branch, gate_up_term, down_term, out_term, grad_hidden, grad_heads, gain_b_term = middle(
        dealt_out, block_input[0], weights, gain_b.reshape(1, model_width), grad_rows, part_units)
    branch_sum = branch[0].astype(jnp.float32)
    for piece in swaps([branch[k] for k in (1, 2, 3)]):
        branch_sum = branch_sum + piece.astype(jnp.float32)
    result_rows = (hidden + branch_sum).astype(low)
    dealt_grad = attention_backward(offs, grad_heads, ordered, perm, start, wide_out, log_total)
    out_part = lax.psum_scatter(out_term, "seq", scatter_dimension=1, tiled=True)
    qkv_term = matmul("rd,re->de", normed_a, dealt_grad)
    grad_normed_a = scatter_rows(matmul("re,de->rd", dealt_grad, part_qkv)).astype(jnp.float32)
    inputs = block_input[0].astype(jnp.float32)
    input_back, gain_a_term = norm_backward(inputs, rms_scale(inputs), grad_normed_a, gain_a)
    input_grad = (grad_hidden + input_back).astype(low)

    def finish(term):
        piece = lax.psum_scatter(term.astype(low), "fsdp", scatter_dimension=0, tiled=True)
        return lax.all_gather(piece, "seq", axis=0, tiled=False)

    def spread(pieces, blocks):
        width = pieces.shape[-1] // blocks
        return pieces.reshape(seq_count, shard, blocks, width).transpose(1, 2, 0, 3).reshape(
            shard, -1).astype(jnp.float32)

    grad_mlp = finish(jnp.concatenate([gate_up_term, down_term], axis=1))
    grad_attn = finish(jnp.concatenate([qkv_term.astype(low), out_part], axis=1))
    gain_terms = lax.psum(jnp.stack([gain_a_term, gain_b_term[0]]), ("seq", "fsdp"))
    gain_terms = lax.dynamic_slice_in_dim(gain_terms, lax.axis_index("fsdp") * shard, shard, axis=1)
    return (
        result_rows[None],
        input_grad[None],
        gain_terms[0],
        spread(grad_attn[:, :, : 3 * head_width], 3),
        spread(grad_attn[:, :, 3 * head_width:], 1),
        gain_terms[1],
        spread(grad_mlp[:, :, : 2 * part_units], 2),
        spread(grad_mlp[:, :, 2 * part_units:], 1),
    )


def solution(mesh):
    rows = P("fsdp", "seq", None)
    vector = P("fsdp")
    matrix = P("fsdp", None)
    return jax.shard_map(
        on_device,
        mesh=mesh,
        in_specs=(rows, vector, matrix, matrix, vector, matrix, matrix, rows, matrix, matrix, matrix),
        out_specs=(rows, rows, vector, matrix, matrix, vector, matrix, matrix),
        check_vma=False,
    )
```

```python
import jax
import jax.numpy as jnp
from jax import lax
from jax.experimental import pallas as pl
from jax.experimental.pallas import tpu as pltpu
from jax.sharding import PartitionSpec as P

HEAD_DIM = 64
BLK = 256
LOG2E = 1.4426950408889634

NT = (((1,), (1,)), ((), ()))
NN = (((1,), (0,)), ((), ()))


def dot(a, b, dims=NN):
    return lax.dot_general(a, b, dims, preferred_element_type=jnp.float32)


def first_block(offs_ref, row0):
    best = jnp.int32(0)
    for k in range(offs_ref.shape[0]):
        off = offs_ref[k]
        best = jnp.where(off <= row0, jnp.maximum(best, off), best)
    return best // BLK


def sort_rows(perm_row_ref, src_ref, dst_ref):
    group_len = src_ref.shape[0]

    def step(i, carry):
        rows = pl.ds(pl.multiple_of(i * BLK, BLK), BLK)
        pos = lax.broadcasted_iota(jnp.int32, (BLK, group_len), 0) + i * BLK
        pick = (perm_row_ref[...] == pos).astype(jnp.float32).astype(jnp.bfloat16)
        dst_ref[rows, :] = dot(pick, src_ref[...]).astype(dst_ref.dtype)
        return carry

    lax.fori_loop(0, group_len // BLK, step, 0)


def deal_rows(perm_col_ref, src_ref, dst_ref):
    group_len = src_ref.shape[0]

    def step(i, carry):
        rows = pl.ds(pl.multiple_of(i * BLK, BLK), BLK)
        pos = lax.broadcasted_iota(jnp.int32, (BLK, group_len), 1)
        pick = (perm_col_ref[rows, :] == pos).astype(jnp.float32).astype(jnp.bfloat16)
        dst_ref[rows, :] = dot(pick, src_ref[...]).astype(dst_ref.dtype)
        return carry

    lax.fori_loop(0, group_len // BLK, step, 0)


def allowed_block(start_ref, cols, qb, kb):
    key_pos = lax.broadcasted_iota(jnp.int32, (BLK, BLK), 0) + kb * BLK
    query_pos = lax.broadcasted_iota(jnp.int32, (BLK, BLK), 1) + qb * BLK
    return (key_pos <= query_pos) & (key_pos >= start_ref[:, cols])


def forward_kernel(offs_ref, qkv_ref, perm_row_ref, perm_col_ref, start_ref,
                   sorted_ref, dealt_ref, wide_ref, lse_ref, vt_ref, low_ref):
    group_len = qkv_ref.shape[0]
    width = qkv_ref.shape[1] // 3
    heads = width // HEAD_DIM
    scale = HEAD_DIM ** -0.5 * LOG2E
    sort_rows(perm_row_ref, qkv_ref, sorted_ref)

    def flip(i, carry):
        rows = pl.ds(pl.multiple_of(i * BLK, BLK), BLK)
        vt_ref[:, rows] = sorted_ref[rows, 2 * width:].T
        return carry

    lax.fori_loop(0, group_len // BLK, flip, 0)

    def query_step(qb, carry):
        qrow = pl.multiple_of(qb * BLK, BLK)
        cols = pl.ds(qrow, BLK)

        def key_step(kb, state):
            krow = pl.multiple_of(kb * BLK, BLK)
            krows = pl.ds(krow, BLK)
            allowed = allowed_block(start_ref, cols, qb, kb)
            fresh = []
            for h in range(heads):
                top, total, acc = state[3 * h: 3 * h + 3]
                hq = slice(h * HEAD_DIM, (h + 1) * HEAD_DIM)
                hk = slice(width + h * HEAD_DIM, width + (h + 1) * HEAD_DIM)
                s = dot(sorted_ref[krows, hk], sorted_ref[cols, hq], NT) * scale
                s = jnp.where(allowed, s, -1e30)
                new_top = jnp.maximum(top, jnp.max(s, axis=0, keepdims=True))
                shrink = jnp.exp2(top - new_top)
                p = jnp.exp2(s - new_top)
                total = total * shrink + jnp.sum(p, axis=0, keepdims=True)
                acc = acc * shrink + dot(vt_ref[hq, krows], p.astype(jnp.bfloat16))
                fresh += [new_top, total, acc]
            return tuple(fresh)

        init = []
        for h in range(heads):
            init += [jnp.full((1, BLK), -1e30, jnp.float32), jnp.zeros((1, BLK), jnp.float32),
                     jnp.zeros((HEAD_DIM, BLK), jnp.float32)]
        state = lax.fori_loop(first_block(offs_ref, qrow), qb + 1, key_step, tuple(init))
        parts = []
        for h in range(heads):
            top, total, acc = state[3 * h: 3 * h + 3]
            out = acc / total
            wide_ref[h * HEAD_DIM:(h + 1) * HEAD_DIM, cols] = out
            lse_ref[h:h + 1, cols] = top + jnp.log2(total)
            parts.append(out)
        low_ref[cols, :] = jnp.concatenate(parts, axis=0).T.astype(jnp.bfloat16)
        return carry

    lax.fori_loop(0, group_len // BLK, query_step, 0)
    deal_rows(perm_col_ref, low_ref, dealt_ref)


def backward_kernel(offs_ref, grad_ref, sorted_ref, perm_row_ref, perm_col_ref, start_ref, wide_ref, lse_ref,
                    dealt_ref, do_ref, kt_ref, delta_ref, dk_ref, dv_ref, low_ref):
    group_len = sorted_ref.shape[0]
    width = sorted_ref.shape[1] // 3
    heads = width // HEAD_DIM
    unit = HEAD_DIM ** -0.5
    scale = unit * LOG2E
    sort_rows(perm_row_ref, grad_ref, do_ref)
    dk_ref[...] = jnp.zeros_like(dk_ref)
    dv_ref[...] = jnp.zeros_like(dv_ref)

    def flip(i, carry):
        rows = pl.ds(pl.multiple_of(i * BLK, BLK), BLK)
        kt_ref[:, rows] = sorted_ref[rows, width: 2 * width].T
        product = do_ref[rows, :].astype(jnp.float32).T * wide_ref[:, rows]
        for h in range(heads):
            delta_ref[h:h + 1, rows] = jnp.sum(product[h * HEAD_DIM:(h + 1) * HEAD_DIM], axis=0, keepdims=True)
        return carry

    lax.fori_loop(0, group_len // BLK, flip, 0)

    def query_step(qb, carry):
        qrow = pl.multiple_of(qb * BLK, BLK)
        cols = pl.ds(qrow, BLK)

        def key_step(kb, state):
            krow = pl.multiple_of(kb * BLK, BLK)
            krows = pl.ds(krow, BLK)
            allowed = allowed_block(start_ref, cols, qb, kb)
            fresh = []
            for h in range(heads):
                hq = slice(h * HEAD_DIM, (h + 1) * HEAD_DIM)
                hk = slice(width + h * HEAD_DIM, width + (h + 1) * HEAD_DIM)
                hv = slice(2 * width + h * HEAD_DIM, 2 * width + (h + 1) * HEAD_DIM)
                q = sorted_ref[cols, hq]
                do = do_ref[cols, hq]
                s = dot(sorted_ref[krows, hk], q, NT) * scale
                s = jnp.where(allowed, s, -1e30)
                p = jnp.exp2(s - lse_ref[h:h + 1, cols])
                dp = dot(sorted_ref[krows, hv], do, NT)
                ds = (p * (dp - delta_ref[h:h + 1, cols])).astype(jnp.bfloat16)
                dv_ref[krows, hq] += dot(p.astype(jnp.bfloat16), do)
                dk_ref[krows, hq] += dot(ds, q)
                fresh.append(state[h] + dot(kt_ref[hq, krows], ds))
            return tuple(fresh)

        state = lax.fori_loop(first_block(offs_ref, qrow), qb + 1, key_step,
                              tuple(jnp.zeros((HEAD_DIM, BLK), jnp.float32) for _ in range(heads)))
        low_ref[cols, :width] = (jnp.concatenate(state, axis=0) * unit).T.astype(jnp.bfloat16)
        return carry

    lax.fori_loop(0, group_len // BLK, query_step, 0)
    low_ref[:, width:2 * width] = (dk_ref[...] * unit).astype(jnp.bfloat16)
    low_ref[:, 2 * width:] = dv_ref[...].astype(jnp.bfloat16)
    deal_rows(perm_col_ref, low_ref, dealt_ref)


def vmem():
    return pl.BlockSpec(memory_space=pltpu.VMEM)


def attention_forward(offs, qkv, perm, start):
    group_len, columns = qkv.shape
    width = columns // 3
    return pl.pallas_call(
        forward_kernel,
        name="attention_forward",
        out_shape=(
            jax.ShapeDtypeStruct((group_len, columns), jnp.bfloat16),
            jax.ShapeDtypeStruct((group_len, width), jnp.bfloat16),
            jax.ShapeDtypeStruct((width, group_len), jnp.float32),
            jax.ShapeDtypeStruct((8, group_len), jnp.float32),
        ),
        in_specs=[pl.BlockSpec(memory_space=pltpu.SMEM)] + [vmem()] * 4,
        out_specs=(vmem(),) * 4,
        scratch_shapes=[pltpu.VMEM((width, group_len), jnp.bfloat16), pltpu.VMEM((group_len, width), jnp.bfloat16)],
        compiler_params=pltpu.CompilerParams(vmem_limit_bytes=48 << 20),
        cost_estimate=pl.CostEstimate(flops=20_000_000_000, bytes_accessed=16 << 20, transcendentals=0),
    )(offs, qkv, perm.reshape(1, group_len), perm.reshape(group_len, 1), start.reshape(1, group_len))


def attention_backward(offs, grad, ordered, perm, start, wide, lse):
    group_len, columns = ordered.shape
    width = columns // 3
    return pl.pallas_call(
        backward_kernel,
        name="attention_backward",
        out_shape=jax.ShapeDtypeStruct((group_len, columns), jnp.bfloat16),
        in_specs=[pl.BlockSpec(memory_space=pltpu.SMEM)] + [vmem()] * 7,
        out_specs=vmem(),
        scratch_shapes=[
            pltpu.VMEM((group_len, width), jnp.bfloat16),
            pltpu.VMEM((width, group_len), jnp.bfloat16),
            pltpu.VMEM((8, group_len), jnp.float32),
            pltpu.VMEM((group_len, width), jnp.float32),
            pltpu.VMEM((group_len, width), jnp.float32),
            pltpu.VMEM((group_len, columns), jnp.bfloat16),
        ],
        compiler_params=pltpu.CompilerParams(vmem_limit_bytes=48 << 20),
        cost_estimate=pl.CostEstimate(flops=40_000_000_000, bytes_accessed=16 << 20, transcendentals=0),
    )(offs, grad, ordered, perm.reshape(1, group_len), perm.reshape(group_len, 1), start.reshape(1, group_len), wide, lse)


epsilon = 1e-05


def rms_scale(values):
    return lax.rsqrt(jnp.mean(values * values, axis=-1, keepdims=True) + epsilon)


MESH = pl.DeviceIdType.MESH
TN = (((0,), (0,)), ((), ()))
TILE = 256


def seq_peers():
    mine = lax.axis_index("seq")
    return mine, (mine + 1 - 2 * lax.rem(mine, 2), lax.rem(mine + 2, 4), 3 - mine)


def greet(peers, others=()):
    barrier = pltpu.get_barrier_semaphore()
    for peer in others:
        pl.semaphore_signal(barrier, inc=1, device_id={"fsdp": peer}, device_id_type=MESH)
    for peer in peers:
        pl.semaphore_signal(barrier, inc=1, device_id={"seq": peer}, device_id_type=MESH)
    pl.semaphore_wait(barrier, len(peers) + len(others))


def span(index, size):
    return pl.ds(pl.multiple_of(index * size, size), size)


def sender(send_sem, recv_sem):
    def send(index, src, dst, axis, peer):
        return pltpu.make_async_remote_copy(
            src_ref=src, dst_ref=dst, send_sem=send_sem.at[index], recv_sem=recv_sem.at[index],
            device_id={axis: peer}, device_id_type=MESH)
    return send


def shard_peers(count):
    mine = lax.axis_index("fsdp")
    sibling = mine + 1 - 2 * lax.rem(mine, 2)
    return mine, sibling, [lax.rem(mine + 2 * k, count) for k in range(1, count // 2)]


def spread(send, base, own, slots, peers):
    px, py, _ = peers
    half = own.shape[0] // 2
    top, bottom = pl.ds(0, half), pl.ds(half, half)
    x_slot, y_slot, far_slot = slots
    x_top = send(base, own.at[top], x_slot.at[top], "seq", px)
    y_bottom = send(base + 1, own.at[bottom], y_slot.at[bottom], "seq", py)
    x_bottom = send(base + 2, own.at[bottom], x_slot.at[bottom], "seq", px)
    y_top = send(base + 3, own.at[top], y_slot.at[top], "seq", py)
    x_relay = send(base + 4, x_slot.at[top], far_slot.at[top], "seq", py)
    y_relay = send(base + 5, y_slot.at[bottom], far_slot.at[bottom], "seq", px)
    for copy in (x_top, y_bottom, x_bottom, y_top):
        copy.start()

    def forward():
        x_top.wait_recv()
        x_relay.start()
        y_bottom.wait_recv()
        y_relay.start()

    def finish():
        for copy in (x_top, y_bottom, x_bottom, y_top, x_relay, y_relay):
            copy.wait_send()

    return forward, (x_bottom.wait_recv, y_top.wait_recv, lambda: (x_relay.wait_recv(), y_relay.wait_recv())), finish


def collect(send, base, give, transit, take, peers):
    px, py, _ = peers
    half = give.shape[1] // 2
    top, bottom = pl.ds(0, half), pl.ds(half, half)
    far_top = send(base, give.at[2, top], transit.at[0], "seq", px)
    far_bottom = send(base + 1, give.at[2, bottom], transit.at[1], "seq", py)
    x_top = send(base + 2, give.at[0, top], take.at[0, top], "seq", px)
    y_bottom = send(base + 3, give.at[1, bottom], take.at[1, bottom], "seq", py)
    y_top = send(base + 4, give.at[1, top], take.at[1, top], "seq", py)
    x_bottom = send(base + 5, give.at[0, bottom], take.at[0, bottom], "seq", px)

    def add(k, part, t):
        def step(i, carry):
            rows = pl.ds(pl.multiple_of(part.start + i * 64, 64), 64)
            more = pl.ds(pl.multiple_of(i * 64, 64), 64)
            give[k, rows, :] = (give[k, rows, :].astype(jnp.float32)
                                + transit[t, more, :].astype(jnp.float32)).astype(jnp.bfloat16)
            return carry
        lax.fori_loop(0, half // 64, step, 0)

    def far():
        far_top.start()
        far_bottom.start()

    def merge():
        far_top.wait_recv()
        add(1, top, 0)
        y_top.start()
        far_bottom.wait_recv()
        add(0, bottom, 1)
        x_bottom.start()

    def finish():
        for copy in (x_top, y_bottom, y_top, x_bottom):
            copy.wait()
        far_top.wait_send()
        far_bottom.wait_send()

    return far, x_top.start, y_bottom.start, merge, finish


def middle_kernel(out_ref, x_ref, weight_ref, gain_ref, dy0_ref, dy1_ref, dy2_ref, dy3_ref,
                  hidden_ref, branch_ref, grads_ref, dh_ref, do_ref, gain_grad_ref,
                  heads_ref, normed_ref, act_ref, dgu_ref, give_ref, take_ref, own_ref, do_give_ref,
                  send_sem, recv_sem):
    low = jnp.bfloat16
    rows, model = x_ref.shape
    width = out_ref.shape[1]
    units = act_ref.shape[2]
    gate_at, up_at, down_at = model, model + units, model + 2 * units
    dy_refs = (dy0_ref, dy1_ref, dy2_ref, dy3_ref)
    mine, peers = seq_peers()
    half = rows // 2
    top, bottom = pl.ds(0, half), pl.ds(half, half)

    def send(index, src, dst, peer):
        return pltpu.make_async_remote_copy(
            src_ref=src, dst_ref=dst, send_sem=send_sem.at[index], recv_sem=recv_sem.at[index],
            device_id={"seq": peer}, device_id_type=MESH)

    def rows_of(peer, size):
        return pl.ds(pl.multiple_of(peer * size, size), size)

    def tiles(count, body):
        def step(i, carry):
            body(pl.multiple_of(i * TILE, TILE))
            return carry
        lax.fori_loop(0, count // TILE, step, 0)

    greet(peers)
    turn = [send(k, out_ref.at[rows_of(peer, rows), :], heads_ref.at[k], peer) for k, peer in enumerate(peers)]
    for k in (2, 0, 1):
        turn[k].start()

    def project(source, peer, base):
        def body(c):
            cols = pl.ds(c, TILE)
            hidden_ref[:, cols] = base(cols) + dot(source, weight_ref[rows_of(peer, width), cols])
        tiles(model, body)

    project(out_ref[rows_of(mine, rows), :], mine, lambda cols: x_ref[:, cols].astype(jnp.float32))
    for k, peer in enumerate(peers):
        turn[k].wait()
        project(heads_ref[k], peer, lambda cols: hidden_ref[:, cols])

    def norm(i, carry):
        part = pl.ds(pl.multiple_of(i * 128, 128), 128)
        h = hidden_ref[part, :]
        normed_ref[0, part, :] = (h * rms_scale(h) * gain_ref[...]).astype(low)
        return carry

    lax.fori_loop(0, rows // 128, norm, 0)

    px, py, pd = peers
    x_top = send(3, normed_ref.at[0, top], normed_ref.at[1, top], px)
    y_bottom = send(4, normed_ref.at[0, bottom], normed_ref.at[2, bottom], py)
    x_bottom = send(5, normed_ref.at[0, bottom], normed_ref.at[1, bottom], px)
    y_top = send(6, normed_ref.at[0, top], normed_ref.at[2, top], py)
    for copy in (x_top, y_bottom, x_bottom, y_top):
        copy.start()

    def feed(slot):
        def body(f):
            gate = dot(normed_ref[slot], weight_ref[:, pl.ds(gate_at + f, TILE)])
            up = dot(normed_ref[slot], weight_ref[:, pl.ds(up_at + f, TILE)])
            grad_act = dot(dy_refs[slot][...], weight_ref[:, pl.ds(down_at + f, TILE)])
            sigmoid = jax.nn.sigmoid(gate)
            silu = gate * sigmoid
            act_ref[slot, :, pl.ds(f, TILE)] = (silu * up).astype(low)
            dgu_ref[slot, :, pl.ds(f, TILE)] = (
                grad_act * up * sigmoid * (1.0 + gate * (1.0 - sigmoid))).astype(low)
            dgu_ref[slot, :, pl.ds(units + f, TILE)] = (grad_act * silu).astype(low)
        tiles(units, body)

    def back(slot, store):
        def body(c):
            cols = pl.ds(c, TILE)
            store(cols, dot(dgu_ref[slot], weight_ref[cols, gate_at:down_at], NT))
        tiles(model, body)

    def keep(cols, value):
        own_ref[:, cols] = value

    def branch(slot):
        def body(c):
            cols = pl.ds(c, TILE)
            branch_ref[slot, :, cols] = dot(act_ref[slot], weight_ref[cols, down_at:], NT).astype(low)
        tiles(model, body)

    feed(0)
    back(0, keep)
    x_top.wait_recv()
    x_relay = send(7, normed_ref.at[1, top], normed_ref.at[3, top], py)
    x_relay.start()
    y_bottom.wait_recv()
    y_relay = send(8, normed_ref.at[2, bottom], normed_ref.at[3, bottom], px)
    y_relay.start()
    branch(0)
    partials = [send(9 + k, give_ref.at[k], take_ref.at[k], peer) for k, peer in enumerate(peers)]
    waits = ((x_bottom,), (y_top,), (x_relay, y_relay))
    for k in range(3):
        for copy in waits[k]:
            copy.wait_recv()
        feed(k + 1)

        def hand(cols, value, k=k):
            give_ref[k, :, cols] = value.astype(low)

        back(k + 1, hand)
        partials[k].start()
    for copy in (x_top, y_bottom, x_bottom, y_top, x_relay, y_relay):
        copy.wait_send()

    def gate_up_grad(f):
        for d in range(0, model, 512):
            part = pl.ds(d, 512)
            acc = dot(normed_ref[0, :, part], dgu_ref[0, :, pl.ds(f, TILE)], TN)
            for slot in range(1, 4):
                acc += dot(normed_ref[slot, :, part], dgu_ref[slot, :, pl.ds(f, TILE)], TN)
            grads_ref[part, pl.ds(f, TILE)] = acc.astype(low)

    tiles(2 * units, gate_up_grad)
    for slot in range(1, 4):
        branch(slot)
    for copy in partials:
        copy.wait()

    gain_grad_ref[...] = jnp.zeros_like(gain_grad_ref)

    def norm_back(i, carry):
        part = pl.ds(pl.multiple_of(i * 64, 64), 64)
        h = hidden_ref[part, :]
        inv = rms_scale(h)
        grad = own_ref[part, :]
        for k in range(3):
            grad += take_ref[k, part, :].astype(jnp.float32)
        gain_grad_ref[0:1, :] += jnp.sum(grad * h * inv, axis=0, keepdims=True)
        scaled = grad * gain_ref[...]
        dh = dy0_ref[part, :].astype(jnp.float32) + (
            inv * scaled - h * inv**3 * jnp.mean(h * scaled, axis=-1, keepdims=True))
        dh_ref[part, :] = dh
        normed_ref[1, part, :] = dh.astype(low)
        return carry

    lax.fori_loop(0, rows // 64, norm_back, 0)

    sends = [send(12 + k, do_give_ref.at[k], do_ref.at[rows_of(mine, rows), :], peer) for k, peer in enumerate(peers)]
    for k in (2, 0, 1):
        do_give_ref[k] = dot(normed_ref[1], weight_ref[rows_of(peers[k], width), :model], NT).astype(low)
        sends[k].start()
    do_ref[rows_of(mine, rows), :] = dot(normed_ref[1], weight_ref[rows_of(mine, width), :model], NT).astype(low)

    def down_grad(f):
        for d in range(0, model, 512):
            part = pl.ds(d, 512)
            acc = dot(dy_refs[0][:, part], act_ref[0, :, pl.ds(f, TILE)], TN)
            for slot in range(1, 4):
                acc += dot(dy_refs[slot][:, part], act_ref[slot, :, pl.ds(f, TILE)], TN)
            grads_ref[part, pl.ds(2 * units + f, TILE)] = acc.astype(low)

    tiles(units, down_grad)
    grads_ref[rows_of(mine, width), 3 * units:] = dot(out_ref[rows_of(mine, rows), :], normed_ref[1], TN).astype(low)
    for k, peer in enumerate(peers):
        grads_ref[rows_of(peer, width), 3 * units:] = dot(heads_ref[k], normed_ref[1], TN).astype(low)
    for copy in sends:
        copy.wait()


def middle(dealt_out, x, weights, gain, dy, units):
    low = jnp.bfloat16
    group_len, width = dealt_out.shape
    rows, model = x.shape
    f32 = jnp.float32
    shape = jax.ShapeDtypeStruct
    return pl.pallas_call(
        middle_kernel,
        name="middle",
        out_shape=(
            shape((rows, model), f32),
            shape((4, rows, model), low),
            shape((model, 3 * units + model), low),
            shape((rows, model), f32),
            shape((group_len, width), low),
            shape((8, model), f32),
        ),
        in_specs=[vmem()] * 8,
        out_specs=(vmem(),) * 6,
        scratch_shapes=[
            pltpu.VMEM((3, rows, width), low),
            pltpu.VMEM((4, rows, model), low),
            pltpu.VMEM((4, rows, units), low),
            pltpu.VMEM((4, rows, 2 * units), low),
            pltpu.VMEM((3, rows, model), low),
            pltpu.VMEM((3, rows, model), low),
            pltpu.VMEM((rows, model), f32),
            pltpu.VMEM((3, rows, width), low),
            pltpu.SemaphoreType.DMA((15,)),
            pltpu.SemaphoreType.DMA((15,)),
        ],
        compiler_params=pltpu.CompilerParams(
            vmem_limit_bytes=62 << 20, collective_id=1, has_side_effects=True),
        cost_estimate=pl.CostEstimate(flops=60_000_000_000, bytes_accessed=40 << 20, transcendentals=0),
    )(dealt_out, x, weights, gain, *dy)


def front_kernel(x_ref, weight_ref, gain_cols_ref, qkv_ref, normed_ref, slab_ref, gains_ref, slots_ref, send_sem, recv_sem):
    low = jnp.bfloat16
    rows, model = x_ref.shape
    shard = weight_ref.shape[0]
    width = weight_ref.shape[1] // 12
    count = model // shard
    mine, peers = seq_peers()
    place, sibling, others = shard_peers(count)
    send = sender(send_sem, recv_sem)
    own = span(place, shard)
    for b in range(3):
        slab_ref[own, b * width:(b + 1) * width] = weight_ref[:, pl.ds(
            pl.multiple_of(b * 4 * width + mine * width, width), width)].astype(low)
    slab_ref[own, 3 * width:] = gain_cols_ref[...].astype(low)
    greet(peers, [sibling] + others)
    forward, arrivals, finish = spread(send, 0, x_ref, [slots_ref.at[k] for k in range(3)], peers)
    direct = [send(6 + k, slab_ref.at[own], slab_ref.at[own], "fsdp", peer) for k, peer in enumerate(others)]
    twins = [send(6 + len(others), slab_ref.at[own], slab_ref.at[own], "fsdp", sibling)]
    for copy in direct:
        copy.start()
    twins[0].start()

    def pass_on(k):
        direct[k].wait_recv()
        part = span(lax.rem(place - 2 * (k + 1) + count, count), shard)
        copy = send(7 + len(others) + k, slab_ref.at[part], slab_ref.at[part], "fsdp", sibling)
        copy.start()
        twins.append(copy)

    pass_on(0)
    forward()
    for k in range(1, len(others)):
        pass_on(k)
    for copy in twins:
        copy.wait_recv()

    def flip(i, carry):
        part = pl.ds(pl.multiple_of(i * 128, 128), 128)
        gains_ref[:, part] = slab_ref[part, 3 * width:].astype(jnp.float32).T[:8]
        return carry

    lax.fori_loop(0, model // 128, flip, 0)

    def project(source, owner):
        def norm(i, carry):
            part = pl.ds(pl.multiple_of(i * 64, 64), 64)
            x = source[part, :].astype(jnp.float32)
            normed_ref[pl.ds(pl.multiple_of(owner * rows + i * 64, 64), 64), :] = (
                x * rms_scale(x) * gains_ref[0:1, :]).astype(low)
            return carry

        lax.fori_loop(0, rows // 64, norm, 0)
        block = span(owner, rows)
        for b in range(3):
            part = slice(b * width, (b + 1) * width)
            qkv_ref[block, part] = dot(normed_ref[block, :], slab_ref[:, part]).astype(low)

    project(x_ref, mine)
    for k in range(3):
        arrivals[k]()
        project(slots_ref.at[k], peers[k])
    finish()
    for copy in direct + twins:
        copy.wait_send()


def front(x, weight, gain_cols):
    low = jnp.bfloat16
    rows, model = x.shape
    shard, columns = weight.shape
    part = columns // 4
    shape = jax.ShapeDtypeStruct
    copies = 8 + 2 * (model // shard // 2)
    return pl.pallas_call(
        front_kernel,
        name="front",
        out_shape=(
            shape((4 * rows, part), low),
            shape((4 * rows, model), low),
            shape((model, part + 128), low),
            shape((8, model), jnp.float32),
        ),
        in_specs=[vmem()] * 3,
        out_specs=(vmem(),) * 4,
        scratch_shapes=[
            pltpu.VMEM((3, rows, model), low),
            pltpu.SemaphoreType.DMA((copies,)),
            pltpu.SemaphoreType.DMA((copies,)),
        ],
        compiler_params=pltpu.CompilerParams(
            vmem_limit_bytes=40 << 20, collective_id=0, has_side_effects=True),
        cost_estimate=pl.CostEstimate(flops=40_000_000_000, bytes_accessed=20 << 20, transcendentals=0),
    )(x, weight, gain_cols)


def rear_kernel(grad_ref, normed_ref, slab_ref, gains_ref, x_ref, dh_ref, input_grad_ref, gain_grad_ref, piece_ref,
                give_ref, transit_ref, take_ref, own_ref, term_ref, twin_ref, sum_ref, shard_take_ref, send_sem, recv_sem):
    low = jnp.bfloat16
    rows, model = x_ref.shape
    shard, columns = piece_ref.shape
    count = model // shard
    mine, peers = seq_peers()
    place, sibling, others = shard_peers(count)
    send = sender(send_sem, recv_sem)

    def partial(owner, store):
        block = span(owner, rows)
        def body(i, carry):
            cols = pl.ds(pl.multiple_of(i * TILE, TILE), TILE)
            store(cols, dot(grad_ref[block, :], slab_ref[cols, :columns], NT))
            return carry
        lax.fori_loop(0, model // TILE, body, 0)

    def hand(k):
        def store(cols, value):
            give_ref[k, :, cols] = value.astype(low)
        return store

    def keep(cols, value):
        own_ref[:, cols] = value

    greet(peers, [sibling] + others)
    far, x_start, y_start, merge, finish = collect(send, 0, give_ref, transit_ref, take_ref, peers)
    partial(peers[2], hand(2))
    far()
    partial(peers[0], hand(0))
    x_start()
    partial(peers[1], hand(1))
    y_start()

    def weight_term(i, carry):
        part = pl.ds(pl.multiple_of(i * TILE, TILE), TILE)
        term_ref[part, :] = dot(normed_ref[:, part], grad_ref[...], TN).astype(low)
        return carry

    lax.fori_loop(0, model // TILE, weight_term, 0)
    twins = []
    for k in range(count // 2):
        part = span(lax.rem(sibling + 2 * k, count), shard)
        twins.append(send(6 + k, term_ref.at[part], twin_ref.at[k], "fsdp", sibling))
        twins[k].start()
    merge()
    direct = []
    for k in range(count // 2):
        twins[k].wait_recv()
        part = span(lax.rem(place + 2 * k, count), shard)
        sum_ref[k] = (term_ref[part, :].astype(jnp.float32) + twin_ref[k].astype(jnp.float32)).astype(low)
        if k > 0:
            copy = send(6 + count // 2 + k, sum_ref.at[k], shard_take_ref.at[k], "fsdp", others[k - 1])
            copy.start()
            direct.append(copy)
    partial(mine, keep)
    for copy in twins:
        copy.wait_send()
    finish()
    gain_grad_ref[...] = jnp.zeros_like(gain_grad_ref)

    def norm_back(i, carry):
        part = pl.ds(pl.multiple_of(i * 64, 64), 64)
        x = x_ref[part, :].astype(jnp.float32)
        inv = rms_scale(x)
        grad = own_ref[part, :] + take_ref[0, part, :].astype(jnp.float32) + take_ref[1, part, :].astype(jnp.float32)
        gain_grad_ref[0:1, :] += jnp.sum(grad * x * inv, axis=0, keepdims=True)
        scaled = grad * gains_ref[0:1, :]
        input_grad_ref[part, :] = (dh_ref[part, :] + (
            inv * scaled - x * inv**3 * jnp.mean(x * scaled, axis=-1, keepdims=True))).astype(low)
        return carry

    lax.fori_loop(0, rows // 64, norm_back, 0)
    total = sum_ref[0].astype(jnp.float32)
    for k in range(1, count // 2):
        direct[k - 1].wait()
        total += shard_take_ref[k].astype(jnp.float32)
    piece_ref[...] = total.astype(low)


def rear(grad, normed, slab, gains, x, dh, shard):
    low = jnp.bfloat16
    rows, model = x.shape
    columns = grad.shape[1]
    count = model // shard
    shape = jax.ShapeDtypeStruct
    copies = 8 + count
    return pl.pallas_call(
        rear_kernel,
        name="rear",
        out_shape=(shape((rows, model), low), shape((8, model), jnp.float32), shape((shard, columns), low)),
        in_specs=[vmem()] * 6,
        out_specs=(vmem(),) * 3,
        scratch_shapes=[
            pltpu.VMEM((3, rows, model), low),
            pltpu.VMEM((2, rows // 2, model), low),
            pltpu.VMEM((2, rows, model), low),
            pltpu.VMEM((rows, model), jnp.float32),
            pltpu.VMEM((model, columns), low),
            pltpu.VMEM((count // 2, shard, columns), low),
            pltpu.VMEM((count // 2, shard, columns), low),
            pltpu.VMEM((count // 2, shard, columns), low),
            pltpu.SemaphoreType.DMA((copies,)),
            pltpu.SemaphoreType.DMA((copies,)),
        ],
        compiler_params=pltpu.CompilerParams(
            vmem_limit_bytes=48 << 20, collective_id=2, has_side_effects=True),
        cost_estimate=pl.CostEstimate(flops=50_000_000_000, bytes_accessed=20 << 20, transcendentals=0),
    )(grad, normed, slab, gains, x, dh)


def last_kernel(pieces_ref, qkv_ref, gain_a_ref, gain_b_ref, out_qkv_ref, out_out_ref, out_gate_up_ref, out_down_ref,
                gains_ref, block_ref, slots_ref, gain_own_ref, gain_take_ref, gain_slots_ref, send_sem, recv_sem):
    low = jnp.bfloat16
    shard, columns = qkv_ref.shape
    model = gain_a_ref.shape[1]
    count = model // shard
    units = out_down_ref.shape[1] // 4
    width = columns // 3
    mine, peers = seq_peers()
    place, sibling, _ = shard_peers(count)
    everyone = [lax.rem(place + k, count) for k in range(1, count)]
    send = sender(send_sem, recv_sem)
    block_ref[:, :columns] = qkv_ref[...]
    block_ref[:, columns:] = pieces_ref[...]
    gain_own_ref[0:1, :] = gain_a_ref[0:1, :]
    gain_own_ref[1:2, :] = gain_b_ref[0:1, :]
    gain_own_ref[2:8, :] = jnp.zeros((6, model), jnp.float32)
    greet(peers, everyone)
    forward, arrivals, finish = spread(send, 0, block_ref, [slots_ref.at[k] for k in range(3)], peers)
    gain_sends = [send(6 + k, gain_own_ref, gain_take_ref.at[k], "fsdp", peer) for k, peer in enumerate(everyone)]
    for copy in gain_sends:
        copy.start()

    def place_block(source, owner, first):
        at = columns
        for b in range(3):
            out_qkv_ref[:, span(b * 4 + owner, width)] = source[:, b * width:(b + 1) * width]
        for b in range(2):
            out_gate_up_ref[:, span(b * 4 + owner, units)] = source[:, at:at + units]
            at += units
        out_down_ref[:, span(owner, units)] = source[:, at:at + units]
        at += units
        if first:
            out_out_ref[...] = source[:, at:].astype(jnp.float32)
        else:
            out_out_ref[...] += source[:, at:].astype(jnp.float32)

    place_block(block_ref, mine, True)
    forward()
    total = gain_own_ref[...]
    for k, copy in enumerate(gain_sends):
        copy.wait_recv()
        total += gain_take_ref[k]
    gains_ref[...] = total
    seq_sends = [send(6 + len(everyone) + k, gains_ref, gain_slots_ref.at[k], "seq", peer) for k, peer in enumerate(peers)]
    for copy in seq_sends:
        copy.start()
    for k in range(3):
        arrivals[k]()
        place_block(slots_ref.at[k], peers[k], False)
    for copy in seq_sends:
        copy.wait()
    gains_ref[...] += gain_slots_ref[0] + gain_slots_ref[1] + gain_slots_ref[2]
    for copy in gain_sends:
        copy.wait_send()
    finish()


def last(pieces, qkv_piece, gain_a, gain_b, units):
    low = jnp.bfloat16
    shard, columns = qkv_piece.shape
    model = gain_a.shape[1]
    count = model // shard
    f32 = jnp.float32
    shape = jax.ShapeDtypeStruct
    wide = columns + pieces.shape[1]
    copies = 9 + count
    return pl.pallas_call(
        last_kernel,
        name="last",
        out_shape=(
            shape((shard, 4 * columns), low),
            shape((shard, model), f32),
            shape((shard, 8 * units), low),
            shape((shard, 4 * units), low),
            shape((8, model), f32),
        ),
        in_specs=[vmem()] * 4,
        out_specs=(vmem(),) * 5,
        scratch_shapes=[
            pltpu.VMEM((shard, wide), low),
            pltpu.VMEM((3, shard, wide), low),
            pltpu.VMEM((8, model), f32),
            pltpu.VMEM((count - 1, 8, model), f32),
            pltpu.VMEM((3, 8, model), f32),
            pltpu.SemaphoreType.DMA((copies,)),
            pltpu.SemaphoreType.DMA((copies,)),
        ],
        compiler_params=pltpu.CompilerParams(
            vmem_limit_bytes=40 << 20, collective_id=3, has_side_effects=True),
        cost_estimate=pl.CostEstimate(flops=40_000_000_000, bytes_accessed=20 << 20, transcendentals=0),
    )(pieces, qkv_piece, gain_a, gain_b)


def swaps(rows):
    return [lax.ppermute(piece, "seq", table) for piece, table in zip(
        rows, ([(i, i ^ 1) for i in range(4)], [(i, (i + 2) % 4) for i in range(4)], [(i, 3 - i) for i in range(4)]))]


def on_device(block_input, norm_gain_a, weight_qkv, weight_out, norm_gain_b, weight_gate_up, weight_down,
              cotangent, permutation, lengths, offsets):
    low = jnp.bfloat16
    f32 = jnp.float32
    seq_count = lax.axis_size("seq")
    mine = lax.axis_index("seq")
    row_count, model_width = block_input.shape[1:]
    group_len = row_count * seq_count
    shard = weight_qkv.shape[0]
    part_units = weight_down.shape[1] // seq_count
    perm = permutation[0]
    offs = offsets[0]
    position = jnp.arange(group_len, dtype=jnp.int32)
    start = jnp.max(jnp.where(offs[None, :] <= position[:, None], offs[None, :], 0), axis=1)

    def columns(weight, blocks, width):
        cut = weight.reshape(shard, blocks, seq_count, width)
        return lax.dynamic_index_in_dim(cut, mine, 2, keepdims=False).reshape(shard, blocks * width).astype(low)

    weights = lax.all_gather(jnp.concatenate(
        [weight_out.astype(low), columns(weight_gate_up, 2, part_units), columns(weight_down, 1, part_units)], axis=1),
        "fsdp", axis=0, tiled=True)
    gain_cols = jnp.pad(jnp.stack([norm_gain_a, norm_gain_b], axis=1), ((0, 0), (0, 126)))
    qkv, normed_a, slab, gains = front(block_input[0], weight_qkv, gain_cols)
    grad_own, qkv = lax.optimization_barrier((cotangent[0], qkv))
    grad_rows = [cotangent[0]] + swaps([grad_own] * 3)
    ordered, dealt_out, wide_out, log_total = attention_forward(offs, qkv, perm, start)
    hidden, branch, grads, grad_hidden, grad_heads, gain_b_term = middle(
        dealt_out, block_input[0], weights, gains[1:2], grad_rows, part_units)
    pieces = lax.psum_scatter(grads, "fsdp", scatter_dimension=0, tiled=True)
    branch_sum = branch[0].astype(f32)
    for piece in swaps([branch[k] for k in (1, 2, 3)]):
        branch_sum = branch_sum + piece.astype(f32)
    result_rows = (hidden + branch_sum).astype(low)
    dealt_grad = attention_backward(offs, grad_heads, ordered, perm, start, wide_out, log_total)
    input_grad, gain_a_term, qkv_piece = rear(dealt_grad, normed_a, slab, gains, block_input[0], grad_hidden, shard)
    grad_qkv, grad_out, grad_gate_up, grad_down, gain_terms = last(
        pieces, qkv_piece, gain_a_term, gain_b_term, part_units)
    gain_terms = lax.dynamic_slice_in_dim(gain_terms, lax.axis_index("fsdp") * shard, shard, axis=1)
    return (
        result_rows[None],
        input_grad[None],
        gain_terms[0],
        grad_qkv.astype(f32),
        grad_out,
        gain_terms[1],
        grad_gate_up.astype(f32),
        grad_down.astype(f32),
    )


def solution(mesh):
    rows = P("fsdp", "seq", None)
    vector = P("fsdp")
    matrix = P("fsdp", None)
    return jax.shard_map(
        on_device,
        mesh=mesh,
        in_specs=(rows, vector, matrix, matrix, vector, matrix, matrix, rows, matrix, matrix, matrix),
        out_specs=(rows, rows, vector, matrix, matrix, vector, matrix, matrix),
        check_vma=False,
    )
```

```python
import jax
import jax.numpy as jnp
from jax import lax
from jax.experimental import pallas as pl
from jax.experimental.pallas import tpu as pltpu
from jax.sharding import PartitionSpec as P

HEAD_DIM = 64
BLK = 256
LOG2E = 1.4426950408889634

NT = (((1,), (1,)), ((), ()))
NN = (((1,), (0,)), ((), ()))


def dot(a, b, dims=NN):
    return lax.dot_general(a, b, dims, preferred_element_type=jnp.float32)


def first_block(offs_ref, row0):
    best = jnp.int32(0)
    for k in range(offs_ref.shape[0]):
        off = offs_ref[k]
        best = jnp.where(off <= row0, jnp.maximum(best, off), best)
    return best // BLK


def sort_rows(perm_row_ref, src_ref, dst_ref):
    group_len = src_ref.shape[0]

    def step(i, carry):
        rows = pl.ds(pl.multiple_of(i * BLK, BLK), BLK)
        pos = lax.broadcasted_iota(jnp.int32, (BLK, group_len), 0) + i * BLK
        pick = (perm_row_ref[...] == pos).astype(jnp.float32).astype(jnp.bfloat16)
        dst_ref[rows, :] = dot(pick, src_ref[...]).astype(dst_ref.dtype)
        return carry

    lax.fori_loop(0, group_len // BLK, step, 0)


def deal_rows(perm_col_ref, src_ref, dst_ref):
    group_len = src_ref.shape[0]

    def step(i, carry):
        rows = pl.ds(pl.multiple_of(i * BLK, BLK), BLK)
        pos = lax.broadcasted_iota(jnp.int32, (BLK, group_len), 1)
        pick = (perm_col_ref[rows, :] == pos).astype(jnp.float32).astype(jnp.bfloat16)
        dst_ref[rows, :] = dot(pick, src_ref[...]).astype(dst_ref.dtype)
        return carry

    lax.fori_loop(0, group_len // BLK, step, 0)


def allowed_block(start_ref, cols, qb, kb):
    key_pos = lax.broadcasted_iota(jnp.int32, (BLK, BLK), 0) + kb * BLK
    query_pos = lax.broadcasted_iota(jnp.int32, (BLK, BLK), 1) + qb * BLK
    return (key_pos <= query_pos) & (key_pos >= start_ref[:, cols])


def forward_kernel(offs_ref, x_ref, slab_ref, perm_row_ref, perm_col_ref, start_ref,
                   sorted_ref, dealt_ref, wide_ref, lse_ref, normed_ref, gains_ref, qkv_ref, vt_ref, low_ref):
    group_len, model = x_ref.shape
    width = qkv_ref.shape[1] // 3
    heads = width // HEAD_DIM
    scale = HEAD_DIM ** -0.5 * LOG2E

    def gain(i, carry):
        part = pl.ds(pl.multiple_of(i * 128, 128), 128)
        gains_ref[:, part] = slab_ref[part, 3 * width:].astype(jnp.float32).T[:8]
        return carry

    lax.fori_loop(0, model // 128, gain, 0)

    def project(i, carry):
        rows = pl.ds(pl.multiple_of(i * BLK, BLK), BLK)
        for r in range(0, BLK, 64):
            part = pl.ds(pl.multiple_of(i * BLK + r, 64), 64)
            x = x_ref[part, :].astype(jnp.float32)
            normed_ref[part, :] = (x * rms_scale(x) * gains_ref[0:1, :]).astype(jnp.bfloat16)
        qkv_ref[rows, :] = dot(normed_ref[rows, :], slab_ref[:, :3 * width]).astype(jnp.bfloat16)
        return carry

    lax.fori_loop(0, group_len // BLK, project, 0)
    sort_rows(perm_row_ref, qkv_ref, sorted_ref)

    def flip(i, carry):
        rows = pl.ds(pl.multiple_of(i * BLK, BLK), BLK)
        vt_ref[:, rows] = sorted_ref[rows, 2 * width:].T
        return carry

    lax.fori_loop(0, group_len // BLK, flip, 0)

    def query_step(qb, carry):
        qrow = pl.multiple_of(qb * BLK, BLK)
        cols = pl.ds(qrow, BLK)

        def key_step(kb, state):
            krow = pl.multiple_of(kb * BLK, BLK)
            krows = pl.ds(krow, BLK)
            allowed = allowed_block(start_ref, cols, qb, kb)
            fresh = []
            for h in range(heads):
                top, total, acc = state[3 * h: 3 * h + 3]
                hq = slice(h * HEAD_DIM, (h + 1) * HEAD_DIM)
                hk = slice(width + h * HEAD_DIM, width + (h + 1) * HEAD_DIM)
                s = dot(sorted_ref[krows, hk], sorted_ref[cols, hq], NT) * scale
                s = jnp.where(allowed, s, -1e30)
                new_top = jnp.maximum(top, jnp.max(s, axis=0, keepdims=True))
                shrink = jnp.exp2(top - new_top)
                p = jnp.exp2(s - new_top)
                total = total * shrink + jnp.sum(p, axis=0, keepdims=True)
                acc = acc * shrink + dot(vt_ref[hq, krows], p.astype(jnp.bfloat16))
                fresh += [new_top, total, acc]
            return tuple(fresh)

        init = []
        for h in range(heads):
            init += [jnp.full((1, BLK), -1e30, jnp.float32), jnp.zeros((1, BLK), jnp.float32),
                     jnp.zeros((HEAD_DIM, BLK), jnp.float32)]
        state = lax.fori_loop(first_block(offs_ref, qrow), qb + 1, key_step, tuple(init))
        parts = []
        for h in range(heads):
            top, total, acc = state[3 * h: 3 * h + 3]
            out = acc / total
            wide_ref[h * HEAD_DIM:(h + 1) * HEAD_DIM, cols] = out
            lse_ref[h:h + 1, cols] = top + jnp.log2(total)
            parts.append(out)
        low_ref[cols, :] = jnp.concatenate(parts, axis=0).T.astype(jnp.bfloat16)
        return carry

    lax.fori_loop(0, group_len // BLK, query_step, 0)
    deal_rows(perm_col_ref, low_ref, dealt_ref)


def backward_kernel(offs_ref, grad_ref, sorted_ref, perm_row_ref, perm_col_ref, start_ref, wide_ref, lse_ref,
                    dealt_ref, do_ref, kt_ref, delta_ref, dk_ref, dv_ref, low_ref):
    group_len = sorted_ref.shape[0]
    width = sorted_ref.shape[1] // 3
    heads = width // HEAD_DIM
    unit = HEAD_DIM ** -0.5
    scale = unit * LOG2E
    sort_rows(perm_row_ref, grad_ref, do_ref)
    dk_ref[...] = jnp.zeros_like(dk_ref)
    dv_ref[...] = jnp.zeros_like(dv_ref)

    def flip(i, carry):
        rows = pl.ds(pl.multiple_of(i * BLK, BLK), BLK)
        kt_ref[:, rows] = sorted_ref[rows, width: 2 * width].T
        product = do_ref[rows, :].astype(jnp.float32).T * wide_ref[:, rows]
        for h in range(heads):
            delta_ref[h:h + 1, rows] = jnp.sum(product[h * HEAD_DIM:(h + 1) * HEAD_DIM], axis=0, keepdims=True)
        return carry

    lax.fori_loop(0, group_len // BLK, flip, 0)

    def query_step(qb, carry):
        qrow = pl.multiple_of(qb * BLK, BLK)
        cols = pl.ds(qrow, BLK)

        def key_step(kb, state):
            krow = pl.multiple_of(kb * BLK, BLK)
            krows = pl.ds(krow, BLK)
            allowed = allowed_block(start_ref, cols, qb, kb)
            fresh = []
            for h in range(heads):
                hq = slice(h * HEAD_DIM, (h + 1) * HEAD_DIM)
                hk = slice(width + h * HEAD_DIM, width + (h + 1) * HEAD_DIM)
                hv = slice(2 * width + h * HEAD_DIM, 2 * width + (h + 1) * HEAD_DIM)
                q = sorted_ref[cols, hq]
                do = do_ref[cols, hq]
                s = dot(sorted_ref[krows, hk], q, NT) * scale
                s = jnp.where(allowed, s, -1e30)
                p = jnp.exp2(s - lse_ref[h:h + 1, cols])
                dp = dot(sorted_ref[krows, hv], do, NT)
                ds = (p * (dp - delta_ref[h:h + 1, cols])).astype(jnp.bfloat16)
                dv_ref[krows, hq] += dot(p.astype(jnp.bfloat16), do)
                dk_ref[krows, hq] += dot(ds, q)
                fresh.append(state[h] + dot(kt_ref[hq, krows], ds))
            return tuple(fresh)

        state = lax.fori_loop(first_block(offs_ref, qrow), qb + 1, key_step,
                              tuple(jnp.zeros((HEAD_DIM, BLK), jnp.float32) for _ in range(heads)))
        low_ref[cols, :width] = (jnp.concatenate(state, axis=0) * unit).T.astype(jnp.bfloat16)
        return carry

    lax.fori_loop(0, group_len // BLK, query_step, 0)
    low_ref[:, width:2 * width] = (dk_ref[...] * unit).astype(jnp.bfloat16)
    low_ref[:, 2 * width:] = dv_ref[...].astype(jnp.bfloat16)
    deal_rows(perm_col_ref, low_ref, dealt_ref)


def hbm():
    return pl.BlockSpec(memory_space=pl.ANY)


def vmem():
    return pl.BlockSpec(memory_space=pltpu.VMEM)


def attention_forward(offs, rows, slab, perm, start):
    group_len, model = rows.shape
    columns = slab.shape[1] - 128
    width = columns // 3
    shape = jax.ShapeDtypeStruct
    return pl.pallas_call(
        forward_kernel,
        name="attention_forward",
        out_shape=(
            shape((group_len, columns), jnp.bfloat16),
            shape((group_len, width), jnp.bfloat16),
            shape((width, group_len), jnp.float32),
            shape((8, group_len), jnp.float32),
            shape((group_len, model), jnp.bfloat16),
            shape((8, model), jnp.float32),
        ),
        in_specs=[pl.BlockSpec(memory_space=pltpu.SMEM)] + [vmem()] * 5,
        out_specs=(vmem(),) * 6,
        scratch_shapes=[
            pltpu.VMEM((group_len, columns), jnp.bfloat16),
            pltpu.VMEM((width, group_len), jnp.bfloat16),
            pltpu.VMEM((group_len, width), jnp.bfloat16),
        ],
        compiler_params=pltpu.CompilerParams(vmem_limit_bytes=48 << 20),
        cost_estimate=pl.CostEstimate(flops=24_000_000_000, bytes_accessed=16 << 20, transcendentals=0),
    )(offs, rows, slab, perm.reshape(1, group_len), perm.reshape(group_len, 1), start.reshape(1, group_len))


def attention_backward(offs, grad, ordered, perm, start, wide, lse):
    group_len, columns = ordered.shape
    width = columns // 3
    return pl.pallas_call(
        backward_kernel,
        name="attention_backward",
        out_shape=jax.ShapeDtypeStruct((group_len, columns), jnp.bfloat16),
        in_specs=[pl.BlockSpec(memory_space=pltpu.SMEM)] + [vmem()] * 7,
        out_specs=vmem(),
        scratch_shapes=[
            pltpu.VMEM((group_len, width), jnp.bfloat16),
            pltpu.VMEM((width, group_len), jnp.bfloat16),
            pltpu.VMEM((8, group_len), jnp.float32),
            pltpu.VMEM((group_len, width), jnp.float32),
            pltpu.VMEM((group_len, width), jnp.float32),
            pltpu.VMEM((group_len, columns), jnp.bfloat16),
        ],
        compiler_params=pltpu.CompilerParams(vmem_limit_bytes=48 << 20),
        cost_estimate=pl.CostEstimate(flops=40_000_000_000, bytes_accessed=16 << 20, transcendentals=0),
    )(offs, grad, ordered, perm.reshape(1, group_len), perm.reshape(group_len, 1), start.reshape(1, group_len), wide, lse)


epsilon = 1e-05


def rms_scale(values):
    return lax.rsqrt(jnp.mean(values * values, axis=-1, keepdims=True) + epsilon)


MESH = pl.DeviceIdType.MESH
TN = (((0,), (0,)), ((), ()))
TILE = 256


def seq_peers():
    mine = lax.axis_index("seq")
    return mine, (mine + 1 - 2 * lax.rem(mine, 2), lax.rem(mine + 2, 4), 3 - mine)


def greet(peers, others=()):
    barrier = pltpu.get_barrier_semaphore()
    for peer in others:
        pl.semaphore_signal(barrier, inc=1, device_id={"fsdp": peer}, device_id_type=MESH)
    for peer in peers:
        pl.semaphore_signal(barrier, inc=1, device_id={"seq": peer}, device_id_type=MESH)
    pl.semaphore_wait(barrier, len(peers) + len(others))


def span(index, size):
    return pl.ds(pl.multiple_of(index * size, size), size)


def sender(send_sem, recv_sem):
    def send(index, src, dst, axis, peer):
        return pltpu.make_async_remote_copy(
            src_ref=src, dst_ref=dst, send_sem=send_sem.at[index], recv_sem=recv_sem.at[index],
            device_id={axis: peer}, device_id_type=MESH)
    return send


def shard_peers(count):
    mine = lax.axis_index("fsdp")
    sibling = mine + 1 - 2 * lax.rem(mine, 2)
    return mine, sibling, [lax.rem(mine + 2 * k, count) for k in range(1, count // 2)]


def spread(send, base, own, slots, peers):
    px, py, _ = peers
    half = own.shape[0] // 2
    top, bottom = pl.ds(0, half), pl.ds(half, half)
    x_slot, y_slot, far_slot = slots
    x_top = send(base, own.at[top], x_slot.at[top], "seq", px)
    y_bottom = send(base + 1, own.at[bottom], y_slot.at[bottom], "seq", py)
    x_bottom = send(base + 2, own.at[bottom], x_slot.at[bottom], "seq", px)
    y_top = send(base + 3, own.at[top], y_slot.at[top], "seq", py)
    x_relay = send(base + 4, x_slot.at[top], far_slot.at[top], "seq", py)
    y_relay = send(base + 5, y_slot.at[bottom], far_slot.at[bottom], "seq", px)
    for copy in (x_top, y_bottom, x_bottom, y_top):
        copy.start()

    def forward():
        x_top.wait_recv()
        x_relay.start()
        y_bottom.wait_recv()
        y_relay.start()

    def finish():
        for copy in (x_top, y_bottom, x_bottom, y_top, x_relay, y_relay):
            copy.wait_send()

    return forward, (x_bottom.wait_recv, y_top.wait_recv, lambda: (x_relay.wait_recv(), y_relay.wait_recv())), finish


def collect(send, base, give, transit, take, peers, cut):
    px, py, _ = peers
    half = give.shape[1] // 2
    size = half // cut
    halves = (pl.ds(0, half), pl.ds(half, half))
    pieces = [[pl.ds(h * half + c * size, size) for c in range(cut)] for h in range(2)]
    first, second = (px, py), (py, px)
    far = [[send(base + h * cut + c, give.at[2, pieces[h][c]], transit.at[h, pl.ds(c * size, size)], "seq", first[h])
            for c in range(cut)] for h in range(2)]
    plain = [send(base + 2 * cut + h, give.at[h, halves[h]], take.at[h, halves[h]], "seq", first[h]) for h in range(2)]
    summed = [[send(base + 2 * cut + 2 + h * cut + c, give.at[1 - h, pieces[h][c]], take.at[1 - h, pieces[h][c]],
                    "seq", second[h]) for c in range(cut)] for h in range(2)]

    def start_far(h):
        for copy in far[h]:
            copy.start()

    def merge(h, c):
        far[h][c].wait_recv()

        def step(i, carry):
            rows = pl.ds(pl.multiple_of(h * half + c * size + i * 64, 64), 64)
            more = pl.ds(pl.multiple_of(c * size + i * 64, 64), 64)
            give[1 - h, rows, :] = (give[1 - h, rows, :].astype(jnp.float32)
                                    + transit[h, more, :].astype(jnp.float32)).astype(jnp.bfloat16)
            return carry

        lax.fori_loop(0, size // 64, step, 0)
        summed[h][c].start()

    def finish(h):
        plain[h].wait()
        for c in range(cut):
            summed[h][c].wait()
            far[h][c].wait_send()

    return start_far, (plain[0].start, plain[1].start), merge, finish


def middle_kernel(out_ref, x_ref, weight_in, gain_ref, dy0_in, dy1_in, dy2_in, dy3_in,
                  hidden_out, branch_out, grads_out, dh_out, do_ref, gain_grad_ref,
                  weight_ref, dy_ref, hidden_ref, branch_ref, grads_ref, dh_ref, mixed_ref, normed_ref, act_ref, dgu_ref, give_ref, transit_ref, take_ref, own_ref, low_ref, do_give_ref,
                  local_sem, send_sem, recv_sem):
    low = jnp.bfloat16
    rows, model = x_ref.shape
    width = out_ref.shape[1]
    units = act_ref.shape[2]
    gate_at, up_at, down_at = model, model + units, model + 2 * units
    mine, peers = seq_peers()
    px, py, _ = peers

    def local(index, src, dst):
        copy = pltpu.make_async_copy(src, dst, local_sem.at[index])
        copy.start()
        return copy

    out_in = local(0, weight_in.at[:, :model], weight_ref.at[:, :model])
    feed_in = [local(1, weight_in.at[:, model:], weight_ref.at[:, model:])]
    feed_in += [local(2 + k, dy_in, dy_ref.at[k]) for k, dy_in in enumerate((dy0_in, dy1_in, dy2_in, dy3_in))]
    half = rows // 2
    halves = (pl.ds(0, half), pl.ds(half, half))
    whole = pl.ds(0, rows)
    send = sender(send_sem, recv_sem)

    def tiles(count, body):
        def step(i, carry):
            body(pl.multiple_of(i * TILE, TILE))
            return carry
        lax.fori_loop(0, count // TILE, step, 0)

    def half_of(owner, h):
        return pl.ds(pl.multiple_of(owner * rows + h * half, half), half)

    greet(peers)
    turn = [[send(3 * h + k, out_ref.at[half_of(peer, h), :], mixed_ref.at[halves[h], span(mine, width)], "seq", peer)
             for k, peer in enumerate(peers)] for h in range(2)]
    for h in range(2):
        for k in (2, 0, 1):
            turn[h][k].start()
    mixed_ref[:, span(mine, width)] = out_ref[span(mine, rows), :]
    x_sends = [send(6 + h, normed_ref.at[0, halves[h]], normed_ref.at[1, halves[h]], "seq", px) for h in range(2)]
    y_sends = [send(8 + h, normed_ref.at[0, halves[h]], normed_ref.at[2, halves[h]], "seq", py) for h in range(2)]
    x_relay = send(10, normed_ref.at[1, halves[0]], normed_ref.at[3, halves[0]], "seq", py)
    y_relay = send(11, normed_ref.at[2, halves[1]], normed_ref.at[3, halves[1]], "seq", px)
    for h in range(2):
        for k in range(3):
            turn[h][k].wait_recv()
        if h == 0:
            out_in.wait()

        def project(c, h=h):
            cols = pl.ds(c, TILE)
            hidden_ref[halves[h], cols] = x_ref[halves[h], cols].astype(jnp.float32) + dot(
                mixed_ref[halves[h], :], weight_ref[:, cols])

        tiles(model, project)

        def norm(i, carry, h=h):
            part = pl.ds(pl.multiple_of(h * half + i * 64, 64), 64)
            value = hidden_ref[part, :]
            normed_ref[0, part, :] = (value * rms_scale(value) * gain_ref[...]).astype(low)
            return carry

        lax.fori_loop(0, half // 64, norm, 0)
        x_sends[h].start()
        y_sends[h].start()

    def feed(slot, part):
        def body(f):
            gate = dot(normed_ref[slot, part, :], weight_ref[:, pl.ds(gate_at + f, TILE)])
            up = dot(normed_ref[slot, part, :], weight_ref[:, pl.ds(up_at + f, TILE)])
            grad_act = dot(dy_ref[slot, part, :], weight_ref[:, pl.ds(down_at + f, TILE)])
            sigmoid = jax.nn.sigmoid(gate)
            silu = gate * sigmoid
            act_ref[slot, part, pl.ds(f, TILE)] = (silu * up).astype(low)
            dgu_ref[slot, part, pl.ds(f, TILE)] = (
                grad_act * up * sigmoid * (1.0 + gate * (1.0 - sigmoid))).astype(low)
            dgu_ref[slot, part, pl.ds(units + f, TILE)] = (grad_act * silu).astype(low)
        tiles(units, body)

    def back(slot, part):
        def body(c):
            cols = pl.ds(c, TILE)
            value = dot(dgu_ref[slot, part, :], weight_ref[cols, gate_at:down_at], NT)
            if slot == 0:
                own_ref[part, cols] = value
            else:
                give_ref[slot - 1, part, cols] = value.astype(low)
        tiles(model, body)

    def branch(slot):
        def body(c):
            cols = pl.ds(c, TILE)
            branch_ref[slot, :, cols] = dot(act_ref[slot], weight_ref[cols, down_at:], NT).astype(low)
        tiles(model, body)

    def work(slot, h):
        feed(slot, halves[h])
        back(slot, halves[h])

    start_far, start_plain, merge, finish = collect(send, 12, give_ref, transit_ref, take_ref, peers, 2)
    outs = [local(6, hidden_ref, hidden_out)]
    for copy in feed_in:
        copy.wait()
    feed(0, whole)
    back(0, whole)
    x_sends[0].wait_recv()
    x_relay.start()
    work(1, 0)
    start_plain[0]()
    y_sends[0].wait_recv()
    work(2, 0)
    y_sends[1].wait_recv()
    y_relay.start()
    work(2, 1)
    start_plain[1]()
    x_sends[1].wait_recv()
    work(1, 1)
    branch(0)
    outs.append(local(7, branch_ref.at[0], branch_out.at[0]))
    x_relay.wait_recv()
    work(3, 0)
    start_far(0)
    y_relay.wait_recv()
    work(3, 1)
    start_far(1)

    def gate_up_grad(first, count):
        def step(i, carry):
            f = pl.multiple_of(i * TILE, TILE)
            for d in range(0, model, 512):
                part = pl.ds(d, 512)
                acc = dot(normed_ref[0, :, part], dgu_ref[0, :, pl.ds(f, TILE)], TN)
                for slot in range(1, 4):
                    acc += dot(normed_ref[slot, :, part], dgu_ref[slot, :, pl.ds(f, TILE)], TN)
                grads_ref[part, pl.ds(f, TILE)] = acc.astype(low)
            return carry
        lax.fori_loop(first, first + count, step, 0)

    merge(0, 0)
    gate_up_grad(0, 1)
    merge(1, 0)
    merge(0, 1)
    gate_up_grad(1, 1)
    merge(1, 1)
    gate_up_grad(2, 2 * units // TILE - 2)
    outs.append(local(8, grads_ref.at[:, :2 * units], grads_out.at[:, :2 * units]))
    gain_grad_ref[...] = jnp.zeros_like(gain_grad_ref)
    sends = [[send(22 + 3 * h + k, do_give_ref.at[k, halves[h]], do_ref.at[half_of(mine, h), :], "seq", peer)
              for k, peer in enumerate(peers)] for h in range(2)]
    for h in range(2):
        finish(h)

        def norm_back(i, carry, h=h):
            part = pl.ds(pl.multiple_of(h * half + i * 64, 64), 64)
            value = hidden_ref[part, :]
            inv = rms_scale(value)
            grad = own_ref[part, :] + take_ref[0, part, :].astype(jnp.float32) + take_ref[1, part, :].astype(jnp.float32)
            gain_grad_ref[0:1, :] += jnp.sum(grad * value * inv, axis=0, keepdims=True)
            scaled = grad * gain_ref[...]
            dh = dy_ref[0, part, :].astype(jnp.float32) + (
                inv * scaled - value * inv**3 * jnp.mean(value * scaled, axis=-1, keepdims=True))
            dh_ref[part, :] = dh
            low_ref[part, :] = dh.astype(low)
            return carry

        lax.fori_loop(0, half // 64, norm_back, 0)
        for k in (2, 0, 1):
            do_give_ref[k, halves[h], :] = dot(
                low_ref[halves[h], :], weight_ref[span(peers[k], width), :model], NT).astype(low)
            sends[h][k].start()
        do_ref[half_of(mine, h), :] = dot(low_ref[halves[h], :], weight_ref[span(mine, width), :model], NT).astype(low)

    outs.append(local(9, dh_ref, dh_out))

    def down_grad(f):
        for d in range(0, model, 512):
            part = pl.ds(d, 512)
            acc = dot(dy_ref[0, :, part], act_ref[0, :, pl.ds(f, TILE)], TN)
            for slot in range(1, 4):
                acc += dot(dy_ref[slot, :, part], act_ref[slot, :, pl.ds(f, TILE)], TN)
            grads_ref[part, pl.ds(2 * units + f, TILE)] = acc.astype(low)

    tiles(units, down_grad)
    outs.append(local(10, grads_ref.at[:, 2 * units:3 * units], grads_out.at[:, 2 * units:3 * units]))
    for slot in range(1, 4):
        branch(slot)
        outs.append(local(10 + slot, branch_ref.at[slot], branch_out.at[slot]))

    def out_grad(c):
        cols = pl.ds(c, TILE)
        grads_ref[:, pl.ds(3 * units + c, TILE)] = dot(mixed_ref[...], low_ref[:, cols], TN).astype(low)

    tiles(model, out_grad)
    outs.append(local(14, grads_ref.at[:, 3 * units:], grads_out.at[:, 3 * units:]))
    for copy in outs:
        copy.wait()
    for h in range(2):
        x_sends[h].wait_send()
        y_sends[h].wait_send()
        for k in range(3):
            turn[h][k].wait_send()
            sends[h][k].wait()
    x_relay.wait_send()
    y_relay.wait_send()


def middle(dealt_out, x, weights, gain, dy, units):
    low = jnp.bfloat16
    group_len, width = dealt_out.shape
    rows, model = x.shape
    f32 = jnp.float32
    shape = jax.ShapeDtypeStruct
    return pl.pallas_call(
        middle_kernel,
        name="middle",
        out_shape=(
            shape((rows, model), f32),
            shape((4, rows, model), low),
            shape((model, 3 * units + model), low),
            shape((rows, model), f32),
            shape((group_len, width), low),
            shape((8, model), f32),
        ),
        in_specs=[vmem(), vmem(), hbm(), vmem()] + [hbm()] * 4,
        out_specs=(hbm(), hbm(), hbm(), hbm(), vmem(), vmem()),
        scratch_shapes=[
            pltpu.VMEM(weights.shape, low),
            pltpu.VMEM((4, rows, model), low),
            pltpu.VMEM((rows, model), f32),
            pltpu.VMEM((4, rows, model), low),
            pltpu.VMEM((model, 3 * units + model), low),
            pltpu.VMEM((rows, model), f32),
            pltpu.VMEM((rows, model), low),
            pltpu.VMEM((4, rows, model), low),
            pltpu.VMEM((4, rows, units), low),
            pltpu.VMEM((4, rows, 2 * units), low),
            pltpu.VMEM((3, rows, model), low),
            pltpu.VMEM((2, rows // 2, model), low),
            pltpu.VMEM((2, rows, model), low),
            pltpu.VMEM((rows, model), f32),
            pltpu.VMEM((rows, model), low),
            pltpu.VMEM((3, rows, width), low),
            pltpu.SemaphoreType.DMA((15,)),
            pltpu.SemaphoreType.DMA((28,)),
            pltpu.SemaphoreType.DMA((28,)),
        ],
        compiler_params=pltpu.CompilerParams(
            vmem_limit_bytes=62 << 20, collective_id=1, has_side_effects=True),
        cost_estimate=pl.CostEstimate(flops=60_000_000_000, bytes_accessed=40 << 20, transcendentals=0),
    )(dealt_out, x, weights, gain, *dy)


def gather_kernel(x_ref, all_ref, local_sem, send_sem, recv_sem):
    rows = x_ref.shape[0]
    mine, peers = seq_peers()
    send = sender(send_sem, recv_sem)
    half = rows // 2
    px, py, _ = peers

    def part(owner, h):
        return all_ref.at[pl.ds(pl.multiple_of(owner * rows + h * half, half), half)]

    greet(peers)
    x_sends = [send(h, x_ref.at[pl.ds(h * half, half)], part(mine, h), "seq", px) for h in range(2)]
    y_sends = [send(2 + h, x_ref.at[pl.ds(h * half, half)], part(mine, h), "seq", py) for h in range(2)]
    for copy in (x_sends[0], y_sends[1], x_sends[1], y_sends[0]):
        copy.start()
    keep = pltpu.make_async_copy(x_ref, all_ref.at[span(mine, rows)], local_sem)
    keep.start()
    x_relay = send(4, part(px, 0), part(px, 0), "seq", py)
    y_relay = send(5, part(py, 1), part(py, 1), "seq", px)
    x_sends[0].wait_recv()
    x_relay.start()
    y_sends[1].wait_recv()
    y_relay.start()
    x_sends[1].wait_recv()
    y_sends[0].wait_recv()
    for copy in x_sends + y_sends:
        copy.wait_send()
    x_relay.wait()
    y_relay.wait()
    keep.wait()


def gather_rows(x):
    rows, model = x.shape
    return pl.pallas_call(
        gather_kernel,
        name="gather_rows",
        out_shape=jax.ShapeDtypeStruct((4 * rows, model), x.dtype),
        in_specs=[pl.BlockSpec(memory_space=pl.ANY)],
        out_specs=pl.BlockSpec(memory_space=pl.ANY),
        scratch_shapes=[
            pltpu.SemaphoreType.DMA,
            pltpu.SemaphoreType.DMA((6,)),
            pltpu.SemaphoreType.DMA((6,)),
        ],
        compiler_params=pltpu.CompilerParams(collective_id=0, has_side_effects=True),
        cost_estimate=pl.CostEstimate(flops=40_000_000_000, bytes_accessed=20 << 20, transcendentals=0),
    )(x)


def rear_kernel(grad_ref, normed_ref, slab_ref, gains_ref, x_ref, dh_ref, input_grad_ref, gain_grad_ref, piece_ref,
                give_ref, transit_ref, take_ref, own_ref, term_ref, twin_ref, sum_ref, shard_take_ref, send_sem, recv_sem):
    low = jnp.bfloat16
    rows, model = x_ref.shape
    shard, columns = piece_ref.shape
    count = model // shard
    mine, peers = seq_peers()
    place, sibling, others = shard_peers(count)
    send = sender(send_sem, recv_sem)

    half = rows // 2

    def partial(owner, first, count, store):
        block = pl.ds(pl.multiple_of(owner * rows + first, half), count)

        def body(i, carry):
            cols = pl.ds(pl.multiple_of(i * TILE, TILE), TILE)
            store(cols, dot(grad_ref[block, :], slab_ref[cols, :columns], NT))
            return carry
        lax.fori_loop(0, model // TILE, body, 0)

    def hand(k, first, count):
        def store(cols, value):
            give_ref[k, pl.ds(first, count), cols] = value.astype(low)
        partial(peers[k], first, count, store)

    def keep(cols, value):
        own_ref[:, cols] = value

    greet(peers, [sibling] + others)
    start_far, start_plain, merge, finish = collect(send, 0, give_ref, transit_ref, take_ref, peers, 2)
    for h in range(2):
        hand(2, h * half, half)
        start_far(h)
    for h in range(2):
        hand(h, 0, rows)
        start_plain[h]()

    def weight_term(i, carry):
        part = pl.ds(pl.multiple_of(i * TILE, TILE), TILE)
        term_ref[part, :] = dot(normed_ref[:, part], grad_ref[...], TN).astype(low)
        return carry

    lax.fori_loop(0, model // TILE, weight_term, 0)
    twins = []
    for k in range(count // 2):
        part = span(lax.rem(sibling + 2 * k, count), shard)
        twins.append(send(10 + k, term_ref.at[part], twin_ref.at[k], "fsdp", sibling))
        twins[k].start()
    for c in range(2):
        for h in range(2):
            merge(h, c)
    direct = []
    for k in range(count // 2):
        twins[k].wait_recv()
        part = span(lax.rem(place + 2 * k, count), shard)
        sum_ref[k] = (term_ref[part, :].astype(jnp.float32) + twin_ref[k].astype(jnp.float32)).astype(low)
        if k > 0:
            copy = send(10 + count // 2 + k, sum_ref.at[k], shard_take_ref.at[k], "fsdp", others[k - 1])
            copy.start()
            direct.append(copy)
    partial(mine, 0, rows, keep)
    for copy in twins:
        copy.wait_send()
    gain_grad_ref[...] = jnp.zeros_like(gain_grad_ref)

    def norm_back(i, carry):
        part = pl.ds(pl.multiple_of(i * 64, 64), 64)
        x = x_ref[part, :].astype(jnp.float32)
        inv = rms_scale(x)
        grad = own_ref[part, :] + take_ref[0, part, :].astype(jnp.float32) + take_ref[1, part, :].astype(jnp.float32)
        gain_grad_ref[0:1, :] += jnp.sum(grad * x * inv, axis=0, keepdims=True)
        scaled = grad * gains_ref[0:1, :]
        input_grad_ref[part, :] = (dh_ref[part, :] + (
            inv * scaled - x * inv**3 * jnp.mean(x * scaled, axis=-1, keepdims=True))).astype(low)
        return carry

    for h in range(2):
        finish(h)
        lax.fori_loop(h * half // 64, (h + 1) * half // 64, norm_back, 0)
    total = sum_ref[0].astype(jnp.float32)
    for k in range(1, count // 2):
        direct[k - 1].wait()
        total += shard_take_ref[k].astype(jnp.float32)
    piece_ref[...] = total.astype(low)


def rear(grad, normed, slab, gains, x, dh, shard):
    low = jnp.bfloat16
    rows, model = x.shape
    columns = grad.shape[1]
    count = model // shard
    shape = jax.ShapeDtypeStruct
    copies = 12 + count
    return pl.pallas_call(
        rear_kernel,
        name="rear",
        out_shape=(shape((rows, model), low), shape((8, model), jnp.float32), shape((shard, columns), low)),
        in_specs=[vmem()] * 6,
        out_specs=(vmem(),) * 3,
        scratch_shapes=[
            pltpu.VMEM((3, rows, model), low),
            pltpu.VMEM((2, rows // 2, model), low),
            pltpu.VMEM((2, rows, model), low),
            pltpu.VMEM((rows, model), jnp.float32),
            pltpu.VMEM((model, columns), low),
            pltpu.VMEM((count // 2, shard, columns), low),
            pltpu.VMEM((count // 2, shard, columns), low),
            pltpu.VMEM((count // 2, shard, columns), low),
            pltpu.SemaphoreType.DMA((copies,)),
            pltpu.SemaphoreType.DMA((copies,)),
        ],
        compiler_params=pltpu.CompilerParams(
            vmem_limit_bytes=48 << 20, collective_id=2, has_side_effects=True),
        cost_estimate=pl.CostEstimate(flops=50_000_000_000, bytes_accessed=20 << 20, transcendentals=0),
    )(grad, normed, slab, gains, x, dh)


def last_kernel(pieces_ref, qkv_ref, gain_a_ref, gain_b_ref, out_qkv_ref, out_out_ref, out_gate_up_ref, out_down_ref,
                gains_ref, block_ref, slots_ref, gain_own_ref, gain_take_ref, gain_slots_ref, send_sem, recv_sem):
    low = jnp.bfloat16
    shard, columns = qkv_ref.shape
    model = gain_a_ref.shape[1]
    count = model // shard
    units = out_down_ref.shape[1] // 4
    width = columns // 3
    mine, peers = seq_peers()
    place, sibling, _ = shard_peers(count)
    everyone = [lax.rem(place + k, count) for k in range(1, count)]
    send = sender(send_sem, recv_sem)
    block_ref[:, :columns] = qkv_ref[...]
    block_ref[:, columns:] = pieces_ref[...]
    gain_own_ref[0:1, :] = gain_a_ref[0:1, :]
    gain_own_ref[1:2, :] = gain_b_ref[0:1, :]
    gain_own_ref[2:8, :] = jnp.zeros((6, model), jnp.float32)
    greet(peers, everyone)
    forward, arrivals, finish = spread(send, 0, block_ref, [slots_ref.at[k] for k in range(3)], peers)
    gain_sends = [send(6 + k, gain_own_ref, gain_take_ref.at[k], "fsdp", peer) for k, peer in enumerate(everyone)]
    for copy in gain_sends:
        copy.start()

    def place_block(source, owner, first):
        at = columns
        for b in range(3):
            out_qkv_ref[:, span(b * 4 + owner, width)] = source[:, b * width:(b + 1) * width]
        for b in range(2):
            out_gate_up_ref[:, span(b * 4 + owner, units)] = source[:, at:at + units]
            at += units
        out_down_ref[:, span(owner, units)] = source[:, at:at + units]
        at += units
        if first:
            out_out_ref[...] = source[:, at:].astype(jnp.float32)
        else:
            out_out_ref[...] += source[:, at:].astype(jnp.float32)

    place_block(block_ref, mine, True)
    forward()
    total = gain_own_ref[...]
    for k, copy in enumerate(gain_sends):
        copy.wait_recv()
        total += gain_take_ref[k]
    gains_ref[...] = total
    seq_sends = [send(6 + len(everyone) + k, gains_ref, gain_slots_ref.at[k], "seq", peer) for k, peer in enumerate(peers)]
    for copy in seq_sends:
        copy.start()
    for k in range(3):
        arrivals[k]()
        place_block(slots_ref.at[k], peers[k], False)
    for copy in seq_sends:
        copy.wait()
    gains_ref[...] += gain_slots_ref[0] + gain_slots_ref[1] + gain_slots_ref[2]
    for copy in gain_sends:
        copy.wait_send()
    finish()


def last(pieces, qkv_piece, gain_a, gain_b, units):
    low = jnp.bfloat16
    shard, columns = qkv_piece.shape
    model = gain_a.shape[1]
    count = model // shard
    f32 = jnp.float32
    shape = jax.ShapeDtypeStruct
    wide = columns + pieces.shape[1]
    copies = 9 + count
    return pl.pallas_call(
        last_kernel,
        name="last",
        out_shape=(
            shape((shard, 4 * columns), low),
            shape((shard, model), f32),
            shape((shard, 8 * units), low),
            shape((shard, 4 * units), low),
            shape((8, model), f32),
        ),
        in_specs=[vmem()] * 4,
        out_specs=(vmem(),) * 5,
        scratch_shapes=[
            pltpu.VMEM((shard, wide), low),
            pltpu.VMEM((3, shard, wide), low),
            pltpu.VMEM((8, model), f32),
            pltpu.VMEM((count - 1, 8, model), f32),
            pltpu.VMEM((3, 8, model), f32),
            pltpu.SemaphoreType.DMA((copies,)),
            pltpu.SemaphoreType.DMA((copies,)),
        ],
        compiler_params=pltpu.CompilerParams(
            vmem_limit_bytes=40 << 20, collective_id=3, has_side_effects=True),
        cost_estimate=pl.CostEstimate(flops=40_000_000_000, bytes_accessed=20 << 20, transcendentals=0),
    )(pieces, qkv_piece, gain_a, gain_b)


def swaps(rows):
    return [lax.ppermute(piece, "seq", table) for piece, table in zip(
        rows, ([(i, i ^ 1) for i in range(4)], [(i, (i + 2) % 4) for i in range(4)], [(i, 3 - i) for i in range(4)]))]


def on_device(block_input, norm_gain_a, weight_qkv, weight_out, norm_gain_b, weight_gate_up, weight_down,
              cotangent, permutation, lengths, offsets):
    low = jnp.bfloat16
    f32 = jnp.float32
    seq_count = lax.axis_size("seq")
    mine = lax.axis_index("seq")
    row_count, model_width = block_input.shape[1:]
    group_len = row_count * seq_count
    shard = weight_qkv.shape[0]
    head_width = weight_qkv.shape[1] // 3 // seq_count
    part_units = weight_down.shape[1] // seq_count
    perm = permutation[0]
    offs = offsets[0]
    position = jnp.arange(group_len, dtype=jnp.int32)
    start = jnp.max(jnp.where(offs[None, :] <= position[:, None], offs[None, :], 0), axis=1)

    def columns(weight, width):
        blocks = weight.shape[1] // (seq_count * width)
        return [lax.dynamic_slice_in_dim(weight, (b * seq_count + mine) * width, width, axis=1) for b in range(blocks)]

    def gather_weight(parts):
        return lax.all_gather(jnp.concatenate(parts, axis=1).astype(low), "fsdp", axis=0, tiled=True)

    gain_cols = jnp.pad(jnp.stack([norm_gain_a, norm_gain_b], axis=1), ((0, 0), (0, 126)))
    slab = gather_weight(columns(weight_qkv, head_width) + [gain_cols])
    weights = gather_weight([weight_out] + columns(weight_gate_up, part_units) + columns(weight_down, part_units))
    rows_all = gather_rows(block_input[0])
    grad_own, rows_all = lax.optimization_barrier((cotangent[0], rows_all))
    grad_rows = [cotangent[0]] + swaps([grad_own] * 3)
    ordered, dealt_out, wide_out, log_total, normed_a, gains = attention_forward(offs, rows_all, slab, perm, start)
    hidden, branch, grads, grad_hidden, grad_heads, gain_b_term = middle(
        dealt_out, block_input[0], weights, gains[1:2], grad_rows, part_units)
    pieces = lax.psum_scatter(grads, "fsdp", scatter_dimension=0, tiled=True)
    branch_sum = branch[0].astype(f32)
    for piece in swaps([branch[k] for k in (1, 2, 3)]):
        branch_sum = branch_sum + piece.astype(f32)
    result_rows = (hidden + branch_sum).astype(low)
    dealt_grad = attention_backward(offs, grad_heads, ordered, perm, start, wide_out, log_total)
    input_grad, gain_a_term, qkv_piece = rear(dealt_grad, normed_a, slab, gains, block_input[0], grad_hidden, shard)
    grad_qkv, grad_out, grad_gate_up, grad_down, gain_terms = last(
        pieces, qkv_piece, gain_a_term, gain_b_term, part_units)
    gain_terms = lax.dynamic_slice_in_dim(gain_terms, lax.axis_index("fsdp") * shard, shard, axis=1)
    return (
        result_rows[None],
        input_grad[None],
        gain_terms[0],
        grad_qkv.astype(f32),
        grad_out,
        gain_terms[1],
        grad_gate_up.astype(f32),
        grad_down.astype(f32),
    )


def solution(mesh):
    rows = P("fsdp", "seq", None)
    vector = P("fsdp")
    matrix = P("fsdp", None)
    return jax.shard_map(
        on_device,
        mesh=mesh,
        in_specs=(rows, vector, matrix, matrix, vector, matrix, matrix, rows, matrix, matrix, matrix),
        out_specs=(rows, rows, vector, matrix, matrix, vector, matrix, matrix),
        check_vma=False,
    )
```

```python
import jax
import jax.numpy as jnp
from jax import lax
from jax.experimental import pallas as pl
from jax.experimental.pallas import tpu as pltpu
from jax.sharding import PartitionSpec as P

HEAD_DIM = 64
BLK = 256
LOG2E = 1.4426950408889634

NT = (((1,), (1,)), ((), ()))
NN = (((1,), (0,)), ((), ()))


def dot(a, b, dims=NN):
    return lax.dot_general(a, b, dims, preferred_element_type=jnp.float32)


def first_block(offs_ref, row0):
    best = jnp.int32(0)
    for k in range(offs_ref.shape[0]):
        off = offs_ref[k]
        best = jnp.where(off <= row0, jnp.maximum(best, off), best)
    return best // BLK


def sort_rows(perm_row_ref, src_ref, dst_ref):
    group_len = src_ref.shape[0]

    def step(i, carry):
        rows = pl.ds(pl.multiple_of(i * BLK, BLK), BLK)
        pos = lax.broadcasted_iota(jnp.int32, (BLK, group_len), 0) + i * BLK
        pick = (perm_row_ref[...] == pos).astype(jnp.float32).astype(jnp.bfloat16)
        dst_ref[rows, :] = dot(pick, src_ref[...]).astype(dst_ref.dtype)
        return carry

    lax.fori_loop(0, group_len // BLK, step, 0)


def deal_rows(perm_col_ref, src_ref, dst_ref):
    group_len = src_ref.shape[0]

    def step(i, carry):
        rows = pl.ds(pl.multiple_of(i * BLK, BLK), BLK)
        pos = lax.broadcasted_iota(jnp.int32, (BLK, group_len), 1)
        pick = (perm_col_ref[rows, :] == pos).astype(jnp.float32).astype(jnp.bfloat16)
        dst_ref[rows, :] = dot(pick, src_ref[...]).astype(dst_ref.dtype)
        return carry

    lax.fori_loop(0, group_len // BLK, step, 0)


def allowed_block(start_ref, cols, qb, kb):
    key_pos = lax.broadcasted_iota(jnp.int32, (BLK, BLK), 0) + kb * BLK
    query_pos = lax.broadcasted_iota(jnp.int32, (BLK, BLK), 1) + qb * BLK
    return (key_pos <= query_pos) & (key_pos >= start_ref[:, cols])


def forward_kernel(offs_ref, x_ref, slab_ref, perm_row_ref, perm_col_ref, start_ref,
                   sorted_ref, dealt_ref, wide_ref, lse_ref, normed_ref, gains_ref, qkv_ref, vt_ref, low_ref):
    group_len, model = x_ref.shape
    width = qkv_ref.shape[1] // 3
    heads = width // HEAD_DIM
    scale = HEAD_DIM ** -0.5 * LOG2E

    def gain(i, carry):
        part = pl.ds(pl.multiple_of(i * 128, 128), 128)
        gains_ref[:, part] = slab_ref[part, 3 * width:].astype(jnp.float32).T[:8]
        return carry

    lax.fori_loop(0, model // 128, gain, 0)

    def project(i, carry):
        rows = pl.ds(pl.multiple_of(i * BLK, BLK), BLK)
        for r in range(0, BLK, 64):
            part = pl.ds(pl.multiple_of(i * BLK + r, 64), 64)
            x = x_ref[part, :].astype(jnp.float32)
            normed_ref[part, :] = (x * rms_scale(x) * gains_ref[0:1, :]).astype(jnp.bfloat16)
        qkv_ref[rows, :] = dot(normed_ref[rows, :], slab_ref[:, :3 * width]).astype(jnp.bfloat16)
        return carry

    lax.fori_loop(0, group_len // BLK, project, 0)
    sort_rows(perm_row_ref, qkv_ref, sorted_ref)

    def flip(i, carry):
        rows = pl.ds(pl.multiple_of(i * BLK, BLK), BLK)
        vt_ref[:, rows] = sorted_ref[rows, 2 * width:].T
        return carry

    lax.fori_loop(0, group_len // BLK, flip, 0)

    def query_step(qb, carry):
        qrow = pl.multiple_of(qb * BLK, BLK)
        cols = pl.ds(qrow, BLK)

        def key_step(kb, state):
            krow = pl.multiple_of(kb * BLK, BLK)
            krows = pl.ds(krow, BLK)
            allowed = allowed_block(start_ref, cols, qb, kb)
            fresh = []
            for h in range(heads):
                top, total, acc = state[3 * h: 3 * h + 3]
                hq = slice(h * HEAD_DIM, (h + 1) * HEAD_DIM)
                hk = slice(width + h * HEAD_DIM, width + (h + 1) * HEAD_DIM)
                s = dot(sorted_ref[krows, hk], sorted_ref[cols, hq], NT) * scale
                s = jnp.where(allowed, s, -1e30)
                new_top = jnp.maximum(top, jnp.max(s, axis=0, keepdims=True))
                shrink = jnp.exp2(top - new_top)
                p = jnp.exp2(s - new_top)
                total = total * shrink + jnp.sum(p, axis=0, keepdims=True)
                acc = acc * shrink + dot(vt_ref[hq, krows], p.astype(jnp.bfloat16))
                fresh += [new_top, total, acc]
            return tuple(fresh)

        init = []
        for h in range(heads):
            init += [jnp.full((1, BLK), -1e30, jnp.float32), jnp.zeros((1, BLK), jnp.float32),
                     jnp.zeros((HEAD_DIM, BLK), jnp.float32)]
        state = lax.fori_loop(first_block(offs_ref, qrow), qb + 1, key_step, tuple(init))
        parts = []
        for h in range(heads):
            top, total, acc = state[3 * h: 3 * h + 3]
            out = acc / total
            wide_ref[h * HEAD_DIM:(h + 1) * HEAD_DIM, cols] = out
            lse_ref[h:h + 1, cols] = top + jnp.log2(total)
            parts.append(out)
        low_ref[cols, :] = jnp.concatenate(parts, axis=0).T.astype(jnp.bfloat16)
        return carry

    lax.fori_loop(0, group_len // BLK, query_step, 0)
    deal_rows(perm_col_ref, low_ref, dealt_ref)


def backward_kernel(offs_ref, grad_ref, sorted_ref, perm_row_ref, perm_col_ref, start_ref, wide_ref, lse_ref,
                    dealt_ref, do_ref, kt_ref, delta_ref, dk_ref, dv_ref, low_ref):
    group_len = sorted_ref.shape[0]
    width = sorted_ref.shape[1] // 3
    heads = width // HEAD_DIM
    unit = HEAD_DIM ** -0.5
    scale = unit * LOG2E
    sort_rows(perm_row_ref, grad_ref, do_ref)
    dk_ref[...] = jnp.zeros_like(dk_ref)
    dv_ref[...] = jnp.zeros_like(dv_ref)

    def flip(i, carry):
        rows = pl.ds(pl.multiple_of(i * BLK, BLK), BLK)
        kt_ref[:, rows] = sorted_ref[rows, width: 2 * width].T
        product = do_ref[rows, :].astype(jnp.float32).T * wide_ref[:, rows]
        for h in range(heads):
            delta_ref[h:h + 1, rows] = jnp.sum(product[h * HEAD_DIM:(h + 1) * HEAD_DIM], axis=0, keepdims=True)
        return carry

    lax.fori_loop(0, group_len // BLK, flip, 0)

    def query_step(qb, carry):
        qrow = pl.multiple_of(qb * BLK, BLK)
        cols = pl.ds(qrow, BLK)

        def key_step(kb, state):
            krow = pl.multiple_of(kb * BLK, BLK)
            krows = pl.ds(krow, BLK)
            allowed = allowed_block(start_ref, cols, qb, kb)
            fresh = []
            for h in range(heads):
                hq = slice(h * HEAD_DIM, (h + 1) * HEAD_DIM)
                hk = slice(width + h * HEAD_DIM, width + (h + 1) * HEAD_DIM)
                hv = slice(2 * width + h * HEAD_DIM, 2 * width + (h + 1) * HEAD_DIM)
                q = sorted_ref[cols, hq]
                do = do_ref[cols, hq]
                s = dot(sorted_ref[krows, hk], q, NT) * scale
                s = jnp.where(allowed, s, -1e30)
                p = jnp.exp2(s - lse_ref[h:h + 1, cols])
                dp = dot(sorted_ref[krows, hv], do, NT)
                ds = (p * (dp - delta_ref[h:h + 1, cols])).astype(jnp.bfloat16)
                dv_ref[krows, hq] += dot(p.astype(jnp.bfloat16), do)
                dk_ref[krows, hq] += dot(ds, q)
                fresh.append(state[h] + dot(kt_ref[hq, krows], ds))
            return tuple(fresh)

        state = lax.fori_loop(first_block(offs_ref, qrow), qb + 1, key_step,
                              tuple(jnp.zeros((HEAD_DIM, BLK), jnp.float32) for _ in range(heads)))
        low_ref[cols, :width] = (jnp.concatenate(state, axis=0) * unit).T.astype(jnp.bfloat16)
        return carry

    lax.fori_loop(0, group_len // BLK, query_step, 0)
    low_ref[:, width:2 * width] = (dk_ref[...] * unit).astype(jnp.bfloat16)
    low_ref[:, 2 * width:] = dv_ref[...].astype(jnp.bfloat16)
    deal_rows(perm_col_ref, low_ref, dealt_ref)


def hbm():
    return pl.BlockSpec(memory_space=pl.ANY)


def vmem():
    return pl.BlockSpec(memory_space=pltpu.VMEM)


def attention_forward(offs, rows, slab, perm, start):
    group_len, model = rows.shape
    columns = slab.shape[1] - 128
    width = columns // 3
    shape = jax.ShapeDtypeStruct
    return pl.pallas_call(
        forward_kernel,
        name="attention_forward",
        out_shape=(
            shape((group_len, columns), jnp.bfloat16),
            shape((group_len, width), jnp.bfloat16),
            shape((width, group_len), jnp.float32),
            shape((8, group_len), jnp.float32),
            shape((group_len, model), jnp.bfloat16),
            shape((8, model), jnp.float32),
        ),
        in_specs=[pl.BlockSpec(memory_space=pltpu.SMEM)] + [vmem()] * 5,
        out_specs=(vmem(),) * 6,
        scratch_shapes=[
            pltpu.VMEM((group_len, columns), jnp.bfloat16),
            pltpu.VMEM((width, group_len), jnp.bfloat16),
            pltpu.VMEM((group_len, width), jnp.bfloat16),
        ],
        compiler_params=pltpu.CompilerParams(vmem_limit_bytes=48 << 20),
        cost_estimate=pl.CostEstimate(flops=24_000_000_000, bytes_accessed=16 << 20, transcendentals=0),
    )(offs, rows, slab, perm.reshape(1, group_len), perm.reshape(group_len, 1), start.reshape(1, group_len))


def attention_backward(offs, grad, ordered, perm, start, wide, lse):
    group_len, columns = ordered.shape
    width = columns // 3
    return pl.pallas_call(
        backward_kernel,
        name="attention_backward",
        out_shape=jax.ShapeDtypeStruct((group_len, columns), jnp.bfloat16),
        in_specs=[pl.BlockSpec(memory_space=pltpu.SMEM)] + [vmem()] * 7,
        out_specs=vmem(),
        scratch_shapes=[
            pltpu.VMEM((group_len, width), jnp.bfloat16),
            pltpu.VMEM((width, group_len), jnp.bfloat16),
            pltpu.VMEM((8, group_len), jnp.float32),
            pltpu.VMEM((group_len, width), jnp.float32),
            pltpu.VMEM((group_len, width), jnp.float32),
            pltpu.VMEM((group_len, columns), jnp.bfloat16),
        ],
        compiler_params=pltpu.CompilerParams(vmem_limit_bytes=48 << 20),
        cost_estimate=pl.CostEstimate(flops=40_000_000_000, bytes_accessed=16 << 20, transcendentals=0),
    )(offs, grad, ordered, perm.reshape(1, group_len), perm.reshape(group_len, 1), start.reshape(1, group_len), wide, lse)


epsilon = 1e-05


def rms_scale(values):
    return lax.rsqrt(jnp.mean(values * values, axis=-1, keepdims=True) + epsilon)


MESH = pl.DeviceIdType.MESH
TN = (((0,), (0,)), ((), ()))
TILE = 256


def seq_peers():
    mine = lax.axis_index("seq")
    return mine, (mine + 1 - 2 * lax.rem(mine, 2), lax.rem(mine + 2, 4), 3 - mine)


def greet(peers, others=()):
    barrier = pltpu.get_barrier_semaphore()
    for peer in others:
        pl.semaphore_signal(barrier, inc=1, device_id={"fsdp": peer}, device_id_type=MESH)
    for peer in peers:
        pl.semaphore_signal(barrier, inc=1, device_id={"seq": peer}, device_id_type=MESH)
    pl.semaphore_wait(barrier, len(peers) + len(others))


def span(index, size):
    return pl.ds(pl.multiple_of(index * size, size), size)


def sender(send_sem, recv_sem):
    def send(index, src, dst, axis, peer):
        return pltpu.make_async_remote_copy(
            src_ref=src, dst_ref=dst, send_sem=send_sem.at[index], recv_sem=recv_sem.at[index],
            device_id={axis: peer}, device_id_type=MESH)
    return send


def shard_peers(count):
    mine = lax.axis_index("fsdp")
    sibling = mine + 1 - 2 * lax.rem(mine, 2)
    return mine, sibling, [lax.rem(mine + 2 * k, count) for k in range(1, count // 2)]


def starter(local_sem):
    def local(index, src, dst):
        copy = pltpu.make_async_copy(src, dst, local_sem.at[index])
        copy.start()
        return copy
    return local


def pair_sum(send, base, place, sibling, others, source, twin, total, take, shard):
    count = 2 * (len(others) + 1)
    twins = [send(base + k, source(span(lax.rem(sibling + 2 * k, count), shard)), twin.at[k], "fsdp", sibling)
             for k in range(count // 2)]
    direct = [send(base + count // 2 + k, total.at[k], take.at[k], "fsdp", others[k - 1]) for k in range(1, count // 2)]

    def start():
        for copy in twins:
            copy.start()

    def pass_on():
        for k in range(1, count // 2) :
            twins[k].wait_recv()
            total[k] = (source(span(lax.rem(place + 2 * k, count), shard))[...].astype(jnp.float32)
                        + twin[k].astype(jnp.float32)).astype(jnp.bfloat16)
            direct[k - 1].start()

    def finish(out_ref):
        twins[0].wait_recv()
        value = source(span(place, shard))[...].astype(jnp.float32) + twin[0].astype(jnp.float32)
        for k in range(1, count // 2):
            direct[k - 1].wait()
            value += take[k].astype(jnp.float32)
        out_ref[...] = value.astype(jnp.bfloat16)
        for copy in twins:
            copy.wait_send()

    return start, pass_on, finish


def spread(send, base, own, slots, peers):
    px, py, _ = peers
    half = own.shape[0] // 2
    top, bottom = pl.ds(0, half), pl.ds(half, half)
    x_slot, y_slot, far_slot = slots
    x_top = send(base, own.at[top], x_slot.at[top], "seq", px)
    y_bottom = send(base + 1, own.at[bottom], y_slot.at[bottom], "seq", py)
    x_bottom = send(base + 2, own.at[bottom], x_slot.at[bottom], "seq", px)
    y_top = send(base + 3, own.at[top], y_slot.at[top], "seq", py)
    x_relay = send(base + 4, x_slot.at[top], far_slot.at[top], "seq", py)
    y_relay = send(base + 5, y_slot.at[bottom], far_slot.at[bottom], "seq", px)
    for copy in (x_top, y_bottom, x_bottom, y_top):
        copy.start()

    def forward():
        x_top.wait_recv()
        x_relay.start()
        y_bottom.wait_recv()
        y_relay.start()

    def finish():
        for copy in (x_top, y_bottom, x_bottom, y_top, x_relay, y_relay):
            copy.wait_send()

    return forward, (x_bottom.wait_recv, y_top.wait_recv, lambda: (x_relay.wait_recv(), y_relay.wait_recv())), finish


def collect(send, base, give, transit, take, peers, cut):
    px, py, _ = peers
    half = give.shape[1] // 2
    size = half // cut
    halves = (pl.ds(0, half), pl.ds(half, half))
    pieces = [[pl.ds(h * half + c * size, size) for c in range(cut)] for h in range(2)]
    first, second = (px, py), (py, px)
    far = [[send(base + h * cut + c, give.at[2, pieces[h][c]], transit.at[h, pl.ds(c * size, size)], "seq", first[h])
            for c in range(cut)] for h in range(2)]
    plain = [send(base + 2 * cut + h, give.at[h, halves[h]], take.at[h, halves[h]], "seq", first[h]) for h in range(2)]
    summed = [[send(base + 2 * cut + 2 + h * cut + c, give.at[1 - h, pieces[h][c]], take.at[1 - h, pieces[h][c]],
                    "seq", second[h]) for c in range(cut)] for h in range(2)]

    def start_far(h):
        for copy in far[h]:
            copy.start()

    def merge(h, c):
        far[h][c].wait_recv()

        def step(i, carry):
            rows = pl.ds(pl.multiple_of(h * half + c * size + i * 64, 64), 64)
            more = pl.ds(pl.multiple_of(c * size + i * 64, 64), 64)
            give[1 - h, rows, :] = (give[1 - h, rows, :].astype(jnp.float32)
                                    + transit[h, more, :].astype(jnp.float32)).astype(jnp.bfloat16)
            return carry

        lax.fori_loop(0, size // 64, step, 0)
        summed[h][c].start()

    def finish(h):
        plain[h].wait()
        for c in range(cut):
            summed[h][c].wait()
            far[h][c].wait_send()

    return start_far, (plain[0].start, plain[1].start), merge, finish


def middle_kernel(out_ref, x_ref, weight_in, tail_in, gain_ref, dy0_in, dy1_in, dy2_in, dy3_in,
                  hidden_out, branch0_out, branch1_out, branch2_out, branch3_out, grads_out, dh_out,
                  do_ref, gain_grad_ref, down_piece_ref,
                  weight_ref, dy_ref, hidden_ref, branch_ref, grads_ref, dh_ref, mixed_ref, normed_ref, act_ref, dgu_ref,
                  give_ref, transit_ref, take_ref, own_ref, low_ref, do_give_ref, twin_ref, total_ref, shard_take_ref,
                  local_sem, send_sem, recv_sem):
    low = jnp.bfloat16
    rows, model = x_ref.shape
    width = out_ref.shape[1]
    units = act_ref.shape[2]
    early = units - TILE
    tail_at = model + 3 * early
    shard = tail_in.shape[0]
    count = model // shard
    mine, peers = seq_peers()
    px, py, _ = peers
    place, sibling, others = shard_peers(count)
    half = rows // 2
    halves = (pl.ds(0, half), pl.ds(half, half))
    whole = pl.ds(0, rows)
    send = sender(send_sem, recv_sem)
    local = starter(local_sem)
    branch_outs = (branch0_out, branch1_out, branch2_out, branch3_out)
    out_in = local(0, weight_in.at[:, :model], weight_ref.at[:, :model])
    feed_in = [local(1, weight_in.at[:, model:], weight_ref.at[:, model:tail_at])]
    feed_in += [local(2 + k, dy_in, dy_ref.at[k]) for k, dy_in in enumerate((dy0_in, dy1_in, dy2_in, dy3_in))]

    def tiles(amount, body, first=0):
        def step(i, carry):
            body(pl.multiple_of(i * TILE, TILE))
            return carry
        lax.fori_loop(first, first + amount // TILE, step, 0)

    def half_of(owner, h):
        return pl.ds(pl.multiple_of(owner * rows + h * half, half), half)

    greet(peers, [sibling] + others)
    turn = [[send(3 * h + k, out_ref.at[half_of(peer, h), :], mixed_ref.at[halves[h], span(mine, width)], "seq", peer)
             for k, peer in enumerate(peers)] for h in range(2)]
    for h in range(2):
        for k in (2, 0, 1):
            turn[h][k].start()

    def tail_of(owner):
        return weight_ref.at[span(owner, shard), tail_at:]

    tails = [send(28 + k, tail_in, tail_of(place), "fsdp", peer) for k, peer in enumerate([sibling] + others)]
    for k in list(range(1, len(tails))) + [0]:
        tails[k].start()
    tail_ref = weight_ref.at[span(place, shard), tail_at:]
    tail_ref[...] = tail_in[...]
    twins = []

    def pass_tail(k):
        tails[k].wait_recv()
        part = tail_of(lax.rem(place - 2 * k + count, count))
        copy = send(28 + count // 2 + k, part, part, "fsdp", sibling)
        copy.start()
        twins.append(copy)

    steps = [range(1 + (len(others) * t) // 3, 1 + (len(others) * (t + 1)) // 3) for t in range(3)]
    mixed_ref[:, span(mine, width)] = out_ref[span(mine, rows), :]
    x_sends = [send(6 + h, normed_ref.at[0, halves[h]], normed_ref.at[1, halves[h]], "seq", px) for h in range(2)]
    y_sends = [send(8 + h, normed_ref.at[0, halves[h]], normed_ref.at[2, halves[h]], "seq", py) for h in range(2)]
    x_relay = send(10, normed_ref.at[1, halves[0]], normed_ref.at[3, halves[0]], "seq", py)
    y_relay = send(11, normed_ref.at[2, halves[1]], normed_ref.at[3, halves[1]], "seq", px)
    for h in range(2):
        for k in range(3):
            turn[h][k].wait_recv()
        if h == 0:
            out_in.wait()

        def project(c, h=h):
            cols = pl.ds(c, TILE)
            hidden_ref[halves[h], cols] = x_ref[halves[h], cols].astype(jnp.float32) + dot(
                mixed_ref[halves[h], :], weight_ref[:, cols])

        tiles(model, project)

        def norm(i, carry, h=h):
            part = pl.ds(pl.multiple_of(h * half + i * 64, 64), 64)
            value = hidden_ref[part, :]
            normed_ref[0, part, :] = (value * rms_scale(value) * gain_ref[...]).astype(low)
            return carry

        lax.fori_loop(0, half // 64, norm, 0)
        x_sends[h].start()
        y_sends[h].start()
        for k in steps[h]:
            pass_tail(k)

    def unit_tile(slot, part, gate_at, up_at, down_at, act_at, dgate_at, dup_at):
        gate = dot(normed_ref[slot, part, :], weight_ref[:, pl.ds(gate_at, TILE)])
        up = dot(normed_ref[slot, part, :], weight_ref[:, pl.ds(up_at, TILE)])
        grad_act = dot(dy_ref[slot, part, :], weight_ref[:, pl.ds(down_at, TILE)])
        sigmoid = jax.nn.sigmoid(gate)
        silu = gate * sigmoid
        act_ref[slot, part, pl.ds(act_at, TILE)] = (silu * up).astype(low)
        dgu_ref[slot, part, pl.ds(dgate_at, TILE)] = (
            grad_act * up * sigmoid * (1.0 + gate * (1.0 - sigmoid))).astype(low)
        dgu_ref[slot, part, pl.ds(dup_at, TILE)] = (grad_act * silu).astype(low)

    def feed_early(slot, part):
        tiles(early, lambda f: unit_tile(
            slot, part, model + f, model + early + f, model + 2 * early + f, f, f, early + f))

    def feed_tail(slot, part):
        unit_tile(slot, part, tail_at, tail_at + TILE, tail_at + 2 * TILE, early, 2 * early, 2 * early + TILE)

    def back(slot, part):
        def body(c):
            cols = pl.ds(c, TILE)
            value = dot(dgu_ref[slot, part, :2 * early], weight_ref[cols, model:model + 2 * early], NT) + dot(
                dgu_ref[slot, part, 2 * early:], weight_ref[cols, tail_at:tail_at + 2 * TILE], NT)
            if slot == 0:
                own_ref[part, cols] = value
            else:
                give_ref[slot - 1, part, cols] = value.astype(low)
        tiles(model, body)

    def branch(slot, target):
        def body(c):
            cols = pl.ds(c, TILE)
            target[:, cols] = (
                dot(act_ref[slot, :, :early], weight_ref[cols, model + 2 * early:tail_at], NT)
                + dot(act_ref[slot, :, early:], weight_ref[cols, tail_at + 2 * TILE:], NT)).astype(low)
        tiles(model, body)

    def work(slot, h):
        feed_early(slot, halves[h])
        feed_tail(slot, halves[h])
        back(slot, halves[h])

    start_far, start_plain, merge, finish = collect(send, 12, give_ref, transit_ref, take_ref, peers, 2)
    outs = [local(6, hidden_ref, hidden_out)]
    for copy in feed_in:
        copy.wait()
    feed_early(0, whole)
    for k in steps[2]:
        pass_tail(k)
    tails[0].wait_recv()
    for copy in twins:
        copy.wait_recv()
    feed_tail(0, whole)
    back(0, whole)
    x_sends[0].wait_recv()
    x_relay.start()
    work(1, 0)
    start_plain[0]()
    y_sends[0].wait_recv()
    work(2, 0)
    y_sends[1].wait_recv()
    y_relay.start()
    work(2, 1)
    start_plain[1]()
    x_sends[1].wait_recv()
    work(1, 1)
    branch(0, branch_ref)
    outs.append(local(7, branch_ref, branch0_out))
    x_relay.wait_recv()
    work(3, 0)
    start_far(0)
    y_relay.wait_recv()
    work(3, 1)
    start_far(1)

    def gate_up_grad(first, amount):
        def step(i, carry):
            f = pl.multiple_of(i * TILE, TILE)
            for d in range(0, model, 512):
                part = pl.ds(d, 512)
                acc = dot(normed_ref[0, :, part], dgu_ref[0, :, pl.ds(f, TILE)], TN)
                for slot in range(1, 4):
                    acc += dot(normed_ref[slot, :, part], dgu_ref[slot, :, pl.ds(f, TILE)], TN)
                grads_ref[part, pl.ds(f, TILE)] = acc.astype(low)
            return carry
        lax.fori_loop(first, first + amount, step, 0)

    down_cols = pl.ds(2 * units, units)

    def down_grad(f):
        for d in range(0, model, 512):
            part = pl.ds(d, 512)
            acc = dot(dy_ref[0, :, part], act_ref[0, :, pl.ds(f, TILE)], TN)
            for slot in range(1, 4):
                acc += dot(dy_ref[slot, :, part], act_ref[slot, :, pl.ds(f, TILE)], TN)
            grads_ref[part, pl.ds(2 * units + f, TILE)] = acc.astype(low)

    shard_start, shard_pass, shard_finish = pair_sum(
        send, 28 + count, place, sibling, others, lambda part: grads_ref.at[part, down_cols],
        twin_ref, total_ref, shard_take_ref, shard)
    for t, (h, c) in enumerate(((0, 0), (1, 0), (0, 1), (1, 1))):
        tiles(units // 4, down_grad, t * (units // 4 // TILE))
        merge(h, c)
    shard_start()
    gate_up_grad(0, 3)
    shard_pass()
    gate_up_grad(3, 1)
    gain_grad_ref[...] = jnp.zeros_like(gain_grad_ref)
    sends = [[send(22 + 3 * h + k, do_give_ref.at[k, halves[h]], do_ref.at[half_of(mine, h), :], "seq", peer)
              for k, peer in enumerate(peers)] for h in range(2)]
    for h in range(2):
        finish(h)

        def norm_back(i, carry, h=h):
            part = pl.ds(pl.multiple_of(h * half + i * 64, 64), 64)
            value = hidden_ref[part, :]
            inv = rms_scale(value)
            grad = own_ref[part, :] + take_ref[0, part, :].astype(jnp.float32) + take_ref[1, part, :].astype(jnp.float32)
            gain_grad_ref[0:1, :] += jnp.sum(grad * value * inv, axis=0, keepdims=True)
            scaled = grad * gain_ref[...]
            dh = dy_ref[0, part, :].astype(jnp.float32) + (
                inv * scaled - value * inv**3 * jnp.mean(value * scaled, axis=-1, keepdims=True))
            dh_ref[part, :] = dh
            low_ref[part, :] = dh.astype(low)
            return carry

        lax.fori_loop(0, half // 64, norm_back, 0)
        for k in (2, 0, 1):
            do_give_ref[k, halves[h], :] = dot(
                low_ref[halves[h], :], weight_ref[span(peers[k], width), :model], NT).astype(low)
            sends[h][k].start()
        do_ref[half_of(mine, h), :] = dot(low_ref[halves[h], :], weight_ref[span(mine, width), :model], NT).astype(low)
    outs.append(local(8, dh_ref, dh_out))
    gate_up_grad(4, 2 * units // TILE - 4)
    outs.append(local(9, grads_ref.at[:, :2 * units], grads_out.at[:, :2 * units]))
    for slot in range(1, 4):
        branch(slot, dgu_ref.at[slot, :, :model])
        outs.append(local(9 + slot, dgu_ref.at[slot, :, :model], branch_outs[slot]))

    def out_grad(c):
        cols = pl.ds(c, TILE)
        grads_ref[:, pl.ds(3 * units + c, TILE)] = dot(mixed_ref[...], low_ref[:, cols], TN).astype(low)

    tiles(model, out_grad)
    outs.append(local(13, grads_ref.at[:, 3 * units:], grads_out.at[:, 2 * units:]))
    shard_finish(down_piece_ref)
    for copy in outs:
        copy.wait()
    for copy in tails + twins:
        copy.wait_send()
    for h in range(2):
        x_sends[h].wait_send()
        y_sends[h].wait_send()
        for k in range(3):
            turn[h][k].wait_send()
            sends[h][k].wait()
    x_relay.wait_send()
    y_relay.wait_send()


def middle(dealt_out, x, weights, tail, gain, dy, units):
    low = jnp.bfloat16
    group_len, width = dealt_out.shape
    rows, model = x.shape
    shard = tail.shape[0]
    count = model // shard
    f32 = jnp.float32
    shape = jax.ShapeDtypeStruct
    copies = 28 + 2 * count
    return pl.pallas_call(
        middle_kernel,
        name="middle",
        out_shape=(
            shape((rows, model), f32),
            *[shape((rows, model), low)] * 4,
            shape((model, 2 * units + model), low),
            shape((rows, model), f32),
            shape((group_len, width), low),
            shape((8, model), f32),
            shape((shard, units), low),
        ),
        in_specs=[vmem(), vmem(), hbm(), vmem(), vmem()] + [hbm()] * 4,
        out_specs=(hbm(),) * 7 + (vmem(),) * 3,
        scratch_shapes=[
            pltpu.VMEM((model, model + 3 * units), low),
            pltpu.VMEM((4, rows, model), low),
            pltpu.VMEM((rows, model), f32),
            pltpu.VMEM((rows, model), low),
            pltpu.VMEM((model, 3 * units + model), low),
            pltpu.VMEM((rows, model), f32),
            pltpu.VMEM((rows, model), low),
            pltpu.VMEM((4, rows, model), low),
            pltpu.VMEM((4, rows, units), low),
            pltpu.VMEM((4, rows, 2 * units), low),
            pltpu.VMEM((3, rows, model), low),
            pltpu.VMEM((2, rows // 2, model), low),
            pltpu.VMEM((2, rows, model), low),
            pltpu.VMEM((rows, model), f32),
            pltpu.VMEM((rows, model), low),
            pltpu.VMEM((3, rows, width), low),
            pltpu.VMEM((count // 2, shard, units), low),
            pltpu.VMEM((count // 2, shard, units), low),
            pltpu.VMEM((count // 2, shard, units), low),
            pltpu.SemaphoreType.DMA((14,)),
            pltpu.SemaphoreType.DMA((copies,)),
            pltpu.SemaphoreType.DMA((copies,)),
        ],
        compiler_params=pltpu.CompilerParams(
            vmem_limit_bytes=62 << 20, collective_id=1, has_side_effects=True),
        cost_estimate=pl.CostEstimate(flops=60_000_000_000, bytes_accessed=40 << 20, transcendentals=0),
    )(dealt_out, x, weights, tail, gain, *dy)


def gather_kernel(x_ref, all_ref, local_sem, send_sem, recv_sem):
    rows = x_ref.shape[0]
    mine, peers = seq_peers()
    send = sender(send_sem, recv_sem)
    half = rows // 2
    px, py, _ = peers

    def part(owner, h):
        return all_ref.at[pl.ds(pl.multiple_of(owner * rows + h * half, half), half)]

    greet(peers)
    x_sends = [send(h, x_ref.at[pl.ds(h * half, half)], part(mine, h), "seq", px) for h in range(2)]
    y_sends = [send(2 + h, x_ref.at[pl.ds(h * half, half)], part(mine, h), "seq", py) for h in range(2)]
    for copy in (x_sends[0], y_sends[1], x_sends[1], y_sends[0]):
        copy.start()
    keep = pltpu.make_async_copy(x_ref, all_ref.at[span(mine, rows)], local_sem)
    keep.start()
    x_relay = send(4, part(px, 0), part(px, 0), "seq", py)
    y_relay = send(5, part(py, 1), part(py, 1), "seq", px)
    x_sends[0].wait_recv()
    x_relay.start()
    y_sends[1].wait_recv()
    y_relay.start()
    x_sends[1].wait_recv()
    y_sends[0].wait_recv()
    for copy in x_sends + y_sends:
        copy.wait_send()
    x_relay.wait()
    y_relay.wait()
    keep.wait()


def gather_rows(x):
    rows, model = x.shape
    return pl.pallas_call(
        gather_kernel,
        name="gather_rows",
        out_shape=jax.ShapeDtypeStruct((4 * rows, model), x.dtype),
        in_specs=[pl.BlockSpec(memory_space=pl.ANY)],
        out_specs=pl.BlockSpec(memory_space=pl.ANY),
        scratch_shapes=[
            pltpu.SemaphoreType.DMA,
            pltpu.SemaphoreType.DMA((6,)),
            pltpu.SemaphoreType.DMA((6,)),
        ],
        compiler_params=pltpu.CompilerParams(collective_id=0, has_side_effects=True),
        cost_estimate=pl.CostEstimate(flops=40_000_000_000, bytes_accessed=20 << 20, transcendentals=0),
    )(x)


def rear_kernel(grad_ref, normed_in, slab_ref, gains_ref, x_in, dh_in, hidden_in, branch0_in, branch1_in, branch2_in,
                branch3_in, result_ref, input_grad_ref, gain_grad_ref, piece_ref,
                normed_ref, x_ref, dh_ref, hidden_ref, branch_ref, give_ref, transit_ref, take_ref, own_ref, term_ref,
                twin_ref, total_ref, shard_take_ref, local_sem, send_sem, recv_sem):
    low = jnp.bfloat16
    rows, model = result_ref.shape
    shard, columns = piece_ref.shape
    count = model // shard
    half = rows // 2
    mine, peers = seq_peers()
    place, sibling, others = shard_peers(count)
    send = sender(send_sem, recv_sem)
    local = starter(local_sem)
    normed_copy = local(0, normed_in, normed_ref)
    row_copies = [local(1, x_in, x_ref), local(2, dh_in, dh_ref)]
    result_copies = [local(3, hidden_in, hidden_ref)]
    result_copies += [local(4 + k, piece, branch_ref.at[k])
                      for k, piece in enumerate((branch0_in, branch1_in, branch2_in, branch3_in))]

    def partial(owner, first, amount, store):
        block = pl.ds(pl.multiple_of(owner * rows + first, half), amount)

        def body(i, carry):
            cols = pl.ds(pl.multiple_of(i * TILE, TILE), TILE)
            store(cols, dot(grad_ref[block, :], slab_ref[cols, :columns], NT))
            return carry

        lax.fori_loop(0, model // TILE, body, 0)

    def hand(k, first, amount):
        def store(cols, value):
            give_ref[k, pl.ds(first, amount), cols] = value.astype(low)
        partial(peers[k], first, amount, store)

    def keep(cols, value):
        own_ref[:, cols] = value

    greet(peers, [sibling] + others)
    start_far, start_plain, merge, finish = collect(send, 0, give_ref, transit_ref, take_ref, peers, 2)
    for h in range(2):
        hand(2, h * half, half)
        start_far(h)
    for h in range(2):
        hand(h, 0, rows)
        start_plain[h]()

    def weight_term(i, carry):
        part = pl.ds(pl.multiple_of(i * TILE, TILE), TILE)
        term_ref[part, :] = dot(normed_ref[:, part], grad_ref[...], TN).astype(low)
        return carry

    normed_copy.wait()
    lax.fori_loop(0, model // TILE, weight_term, 0)
    shard_start, shard_pass, shard_finish = pair_sum(
        send, 10, place, sibling, others, lambda part: term_ref.at[part], twin_ref, total_ref, shard_take_ref, shard)
    shard_start()
    for c in range(2):
        for h in range(2):
            merge(h, c)
    shard_pass()
    partial(mine, 0, rows, keep)
    for copy in result_copies:
        copy.wait()

    def result(i, carry):
        part = pl.ds(pl.multiple_of(i * 64, 64), 64)
        value = hidden_ref[part, :]
        for k in range(4):
            value += branch_ref[k, part, :].astype(jnp.float32)
        result_ref[part, :] = value.astype(low)
        return carry

    lax.fori_loop(0, rows // 64, result, 0)
    for copy in row_copies:
        copy.wait()
    gain_grad_ref[...] = jnp.zeros_like(gain_grad_ref)

    def norm_back(i, carry):
        part = pl.ds(pl.multiple_of(i * 64, 64), 64)
        x = x_ref[part, :].astype(jnp.float32)
        inv = rms_scale(x)
        grad = own_ref[part, :] + take_ref[0, part, :].astype(jnp.float32) + take_ref[1, part, :].astype(jnp.float32)
        gain_grad_ref[0:1, :] += jnp.sum(grad * x * inv, axis=0, keepdims=True)
        scaled = grad * gains_ref[0:1, :]
        input_grad_ref[part, :] = (dh_ref[part, :] + (
            inv * scaled - x * inv**3 * jnp.mean(x * scaled, axis=-1, keepdims=True))).astype(low)
        return carry

    for h in range(2):
        finish(h)
        lax.fori_loop(h * half // 64, (h + 1) * half // 64, norm_back, 0)
    shard_finish(piece_ref)


def rear(grad, normed, slab, gains, x, dh, hidden, branch, shard):
    low = jnp.bfloat16
    f32 = jnp.float32
    rows, model = x.shape
    group_len, columns = grad.shape
    count = model // shard
    shape = jax.ShapeDtypeStruct
    copies = 10 + count
    return pl.pallas_call(
        rear_kernel,
        name="rear",
        out_shape=(shape((rows, model), low), shape((rows, model), low), shape((8, model), f32),
                   shape((shard, columns), low)),
        in_specs=[vmem(), hbm(), vmem(), vmem()] + [hbm()] * 7,
        out_specs=(vmem(),) * 4,
        scratch_shapes=[
            pltpu.VMEM((group_len, model), low),
            pltpu.VMEM((rows, model), low),
            pltpu.VMEM((rows, model), f32),
            pltpu.VMEM((rows, model), f32),
            pltpu.VMEM((4, rows, model), low),
            pltpu.VMEM((3, rows, model), low),
            pltpu.VMEM((2, rows // 2, model), low),
            pltpu.VMEM((2, rows, model), low),
            pltpu.VMEM((rows, model), f32),
            pltpu.VMEM((model, columns), low),
            pltpu.VMEM((count // 2, shard, columns), low),
            pltpu.VMEM((count // 2, shard, columns), low),
            pltpu.VMEM((count // 2, shard, columns), low),
            pltpu.SemaphoreType.DMA((8,)),
            pltpu.SemaphoreType.DMA((copies,)),
            pltpu.SemaphoreType.DMA((copies,)),
        ],
        compiler_params=pltpu.CompilerParams(
            vmem_limit_bytes=56 << 20, collective_id=2, has_side_effects=True),
        cost_estimate=pl.CostEstimate(flops=50_000_000_000, bytes_accessed=20 << 20, transcendentals=0),
    )(grad, normed, slab, gains, x, dh, hidden, *branch)


def last_kernel(pieces_ref, qkv_ref, down_ref, gain_a_ref, gain_b_ref, out_qkv_ref, out_out_ref, out_gate_up_ref, out_down_ref,
                gains_ref, block_ref, slots_ref, gain_own_ref, gain_take_ref, gain_slots_ref, send_sem, recv_sem):
    low = jnp.bfloat16
    shard, columns = qkv_ref.shape
    model = gain_a_ref.shape[1]
    count = model // shard
    units = out_down_ref.shape[1] // 4
    width = columns // 3
    mine, peers = seq_peers()
    place, sibling, _ = shard_peers(count)
    everyone = [lax.rem(place + k, count) for k in range(1, count)]
    send = sender(send_sem, recv_sem)
    block_ref[:, :columns] = qkv_ref[...]
    block_ref[:, columns:columns + units] = down_ref[...]
    block_ref[:, columns + units:] = pieces_ref[...]
    gain_own_ref[0:1, :] = gain_a_ref[0:1, :]
    gain_own_ref[1:2, :] = gain_b_ref[0:1, :]
    gain_own_ref[2:8, :] = jnp.zeros((6, model), jnp.float32)
    greet(peers, everyone)
    forward, arrivals, finish = spread(send, 0, block_ref, [slots_ref.at[k] for k in range(3)], peers)
    gain_sends = [send(6 + k, gain_own_ref, gain_take_ref.at[k], "fsdp", peer) for k, peer in enumerate(everyone)]
    for copy in gain_sends:
        copy.start()

    def place_block(source, owner, first):
        for b in range(3):
            out_qkv_ref[:, span(b * 4 + owner, width)] = source[:, b * width:(b + 1) * width]
        out_down_ref[:, span(owner, units)] = source[:, columns:columns + units]
        at = columns + units
        for shift, size in ((0, units - TILE), (units - TILE, TILE)):
            for b in range(2):
                out_gate_up_ref[:, pl.ds(pl.multiple_of((b * 4 + owner) * units + shift, TILE), size)] = (
                    source[:, at:at + size])
                at += size
        if first:
            out_out_ref[...] = source[:, at:].astype(jnp.float32)
        else:
            out_out_ref[...] += source[:, at:].astype(jnp.float32)

    place_block(block_ref, mine, True)
    forward()
    total = gain_own_ref[...]
    for k, copy in enumerate(gain_sends):
        copy.wait_recv()
        total += gain_take_ref[k]
    gains_ref[...] = total
    seq_sends = [send(6 + len(everyone) + k, gains_ref, gain_slots_ref.at[k], "seq", peer) for k, peer in enumerate(peers)]
    for copy in seq_sends:
        copy.start()
    for k in range(3):
        arrivals[k]()
        place_block(slots_ref.at[k], peers[k], False)
    for copy in seq_sends:
        copy.wait()
    gains_ref[...] += gain_slots_ref[0] + gain_slots_ref[1] + gain_slots_ref[2]
    for copy in gain_sends:
        copy.wait_send()
    finish()


def last(pieces, qkv_piece, down_piece, gain_a, gain_b, units):
    low = jnp.bfloat16
    shard, columns = qkv_piece.shape
    model = gain_a.shape[1]
    count = model // shard
    f32 = jnp.float32
    shape = jax.ShapeDtypeStruct
    wide = columns + units + pieces.shape[1]
    copies = 9 + count
    return pl.pallas_call(
        last_kernel,
        name="last",
        out_shape=(
            shape((shard, 4 * columns), low),
            shape((shard, model), f32),
            shape((shard, 8 * units), low),
            shape((shard, 4 * units), low),
            shape((8, model), f32),
        ),
        in_specs=[vmem()] * 5,
        out_specs=(vmem(),) * 5,
        scratch_shapes=[
            pltpu.VMEM((shard, wide), low),
            pltpu.VMEM((3, shard, wide), low),
            pltpu.VMEM((8, model), f32),
            pltpu.VMEM((count - 1, 8, model), f32),
            pltpu.VMEM((3, 8, model), f32),
            pltpu.SemaphoreType.DMA((copies,)),
            pltpu.SemaphoreType.DMA((copies,)),
        ],
        compiler_params=pltpu.CompilerParams(
            vmem_limit_bytes=40 << 20, collective_id=3, has_side_effects=True),
        cost_estimate=pl.CostEstimate(flops=40_000_000_000, bytes_accessed=20 << 20, transcendentals=0),
    )(pieces, qkv_piece, down_piece, gain_a, gain_b)


def swaps(rows):
    return [lax.ppermute(piece, "seq", table) for piece, table in zip(
        rows, ([(i, i ^ 1) for i in range(4)], [(i, (i + 2) % 4) for i in range(4)], [(i, 3 - i) for i in range(4)]))]


def on_device(block_input, norm_gain_a, weight_qkv, weight_out, norm_gain_b, weight_gate_up, weight_down,
              cotangent, permutation, lengths, offsets):
    low = jnp.bfloat16
    f32 = jnp.float32
    seq_count = lax.axis_size("seq")
    mine = lax.axis_index("seq")
    row_count, model_width = block_input.shape[1:]
    group_len = row_count * seq_count
    shard = weight_qkv.shape[0]
    head_width = weight_qkv.shape[1] // 3 // seq_count
    part_units = weight_down.shape[1] // seq_count
    perm = permutation[0]
    offs = offsets[0]
    position = jnp.arange(group_len, dtype=jnp.int32)
    start = jnp.max(jnp.where(offs[None, :] <= position[:, None], offs[None, :], 0), axis=1)

    def columns(weight, width, first, amount):
        blocks = weight.shape[1] // (seq_count * width)
        return [lax.dynamic_slice_in_dim(weight, (b * seq_count + mine) * width + first, amount, axis=1).astype(low)
                for b in range(blocks)]

    def gather_weight(parts):
        return lax.all_gather(jnp.concatenate(parts, axis=1), "fsdp", axis=0, tiled=True)

    early = part_units - TILE
    gain_cols = jnp.pad(jnp.stack([norm_gain_a, norm_gain_b], axis=1).astype(low), ((0, 0), (0, 126)))
    slab = gather_weight(columns(weight_qkv, head_width, 0, head_width) + [gain_cols])
    weights = gather_weight([weight_out.astype(low)] + columns(weight_gate_up, part_units, 0, early)
                            + columns(weight_down, part_units, 0, early))
    tail = jnp.concatenate(columns(weight_gate_up, part_units, early, TILE)
                           + columns(weight_down, part_units, early, TILE), axis=1)
    rows_all = gather_rows(block_input[0])
    grad_own, rows_all = lax.optimization_barrier((cotangent[0], rows_all))
    grad_rows = [cotangent[0]] + swaps([grad_own] * 3)
    ordered, dealt_out, wide_out, log_total, normed_a, gains = attention_forward(offs, rows_all, slab, perm, start)
    hidden, branch0, branch1, branch2, branch3, grads, grad_hidden, grad_heads, gain_b_term, down_piece = middle(
        dealt_out, block_input[0], weights, tail, gains[1:2], grad_rows, part_units)
    pieces = lax.psum_scatter(grads, "fsdp", scatter_dimension=0, tiled=True)
    branch = [branch0] + swaps([branch1, branch2, branch3])
    dealt_grad = attention_backward(offs, grad_heads, ordered, perm, start, wide_out, log_total)
    result_rows, input_grad, gain_a_term, qkv_piece = rear(
        dealt_grad, normed_a, slab, gains, block_input[0], grad_hidden, hidden, branch, shard)
    grad_qkv, grad_out, grad_gate_up, grad_down, gain_terms = last(
        pieces, qkv_piece, down_piece, gain_a_term, gain_b_term, part_units)
    gain_terms = lax.dynamic_slice_in_dim(gain_terms, lax.axis_index("fsdp") * shard, shard, axis=1)
    return (
        result_rows[None],
        input_grad[None],
        gain_terms[0],
        grad_qkv.astype(f32),
        grad_out,
        gain_terms[1],
        grad_gate_up.astype(f32),
        grad_down.astype(f32),
    )


def solution(mesh):
    rows = P("fsdp", "seq", None)
    vector = P("fsdp")
    matrix = P("fsdp", None)
    return jax.shard_map(
        on_device,
        mesh=mesh,
        in_specs=(rows, vector, matrix, matrix, vector, matrix, matrix, rows, matrix, matrix, matrix),
        out_specs=(rows, rows, vector, matrix, matrix, vector, matrix, matrix),
        check_vma=False,
    )
```

```python
import jax
import jax.numpy as jnp
from jax import lax
from jax.experimental import pallas as pl
from jax.experimental.pallas import tpu as pltpu
from jax.sharding import PartitionSpec as P

HEAD_DIM = 64
BLK = 256
LOG2E = 1.4426950408889634

NT = (((1,), (1,)), ((), ()))
NN = (((1,), (0,)), ((), ()))


def dot(a, b, dims=NN):
    return lax.dot_general(a, b, dims, preferred_element_type=jnp.float32)


def first_block(offs_ref, row0):
    best = jnp.int32(0)
    for k in range(offs_ref.shape[0]):
        off = offs_ref[k]
        best = jnp.where(off <= row0, jnp.maximum(best, off), best)
    return best // BLK


def sort_rows(perm_row_ref, src_ref, dst_ref):
    group_len = src_ref.shape[0]

    def step(i, carry):
        rows = pl.ds(pl.multiple_of(i * BLK, BLK), BLK)
        pos = lax.broadcasted_iota(jnp.int32, (BLK, group_len), 0) + i * BLK
        pick = (perm_row_ref[...] == pos).astype(jnp.float32).astype(jnp.bfloat16)
        dst_ref[rows, :] = dot(pick, src_ref[...]).astype(dst_ref.dtype)
        return carry

    lax.fori_loop(0, group_len // BLK, step, 0)


def deal_rows(perm_col_ref, src_ref, dst_ref, out_ref, sems):
    group_len = src_ref.shape[0]

    def copy_out(i):
        rows = pl.ds(pl.multiple_of(i * BLK, BLK), BLK)
        return pltpu.make_async_copy(dst_ref.at[rows, :], out_ref.at[rows, :], sems.at[i])

    def step(i, carry):
        rows = pl.ds(pl.multiple_of(i * BLK, BLK), BLK)
        pos = lax.broadcasted_iota(jnp.int32, (BLK, group_len), 1)
        pick = (perm_col_ref[rows, :] == pos).astype(jnp.float32).astype(jnp.bfloat16)
        dst_ref[rows, :] = dot(pick, src_ref[...]).astype(dst_ref.dtype)
        copy_out(i).start()
        return carry

    def wait(i, carry):
        copy_out(i).wait()
        return carry

    lax.fori_loop(0, group_len // BLK, step, 0)
    lax.fori_loop(0, group_len // BLK, wait, 0)


def allowed_block(start_ref, cols, qb, kb):
    key_pos = lax.broadcasted_iota(jnp.int32, (BLK, BLK), 0) + kb * BLK
    query_pos = lax.broadcasted_iota(jnp.int32, (BLK, BLK), 1) + qb * BLK
    return (key_pos <= query_pos) & (key_pos >= start_ref[:, cols])


def forward_kernel(offs_ref, x_ref, slab_ref, perm_row_ref, perm_col_ref, start_ref,
                   sorted_out, dealt_out, wide_out, lse_ref, normed_out, gains_ref,
                   sorted_ref, dealt_ref, wide_ref, normed_ref, qkv_ref, vt_ref, low_ref, local_sem, deal_sem):
    group_len, model = x_ref.shape
    width = qkv_ref.shape[1] // 3
    heads = width // HEAD_DIM
    scale = HEAD_DIM ** -0.5 * LOG2E

    def gain(i, carry):
        part = pl.ds(pl.multiple_of(i * 128, 128), 128)
        gains_ref[:, part] = slab_ref[part, 3 * width:].astype(jnp.float32).T[:8]
        return carry

    lax.fori_loop(0, model // 128, gain, 0)

    def project(i, carry):
        rows = pl.ds(pl.multiple_of(i * BLK, BLK), BLK)
        for r in range(0, BLK, 64):
            part = pl.ds(pl.multiple_of(i * BLK + r, 64), 64)
            x = x_ref[part, :].astype(jnp.float32)
            normed_ref[part, :] = (x * rms_scale(x) * gains_ref[0:1, :]).astype(jnp.bfloat16)
        qkv_ref[rows, :] = dot(normed_ref[rows, :], slab_ref[:, :3 * width]).astype(jnp.bfloat16)
        return carry

    lax.fori_loop(0, group_len // BLK, project, 0)
    outs = [pltpu.make_async_copy(normed_ref, normed_out, local_sem.at[0])]
    outs[0].start()
    sort_rows(perm_row_ref, qkv_ref, sorted_ref)
    outs.append(pltpu.make_async_copy(sorted_ref, sorted_out, local_sem.at[1]))
    outs[1].start()

    def flip(i, carry):
        rows = pl.ds(pl.multiple_of(i * BLK, BLK), BLK)
        vt_ref[:, rows] = sorted_ref[rows, 2 * width:].T
        return carry

    lax.fori_loop(0, group_len // BLK, flip, 0)

    def query_step(qb, carry):
        qrow = pl.multiple_of(qb * BLK, BLK)
        cols = pl.ds(qrow, BLK)

        def key_step(kb, state):
            krow = pl.multiple_of(kb * BLK, BLK)
            krows = pl.ds(krow, BLK)
            allowed = allowed_block(start_ref, cols, qb, kb)
            fresh = []
            for h in range(heads):
                top, total, acc = state[3 * h: 3 * h + 3]
                hq = slice(h * HEAD_DIM, (h + 1) * HEAD_DIM)
                hk = slice(width + h * HEAD_DIM, width + (h + 1) * HEAD_DIM)
                s = dot(sorted_ref[krows, hk], sorted_ref[cols, hq], NT) * scale
                s = jnp.where(allowed, s, -1e30)
                new_top = jnp.maximum(top, jnp.max(s, axis=0, keepdims=True))
                shrink = jnp.exp2(top - new_top)
                p = jnp.exp2(s - new_top)
                total = total * shrink + jnp.sum(p, axis=0, keepdims=True)
                acc = acc * shrink + dot(vt_ref[hq, krows], p.astype(jnp.bfloat16))
                fresh += [new_top, total, acc]
            return tuple(fresh)

        init = []
        for h in range(heads):
            init += [jnp.full((1, BLK), -1e30, jnp.float32), jnp.zeros((1, BLK), jnp.float32),
                     jnp.zeros((HEAD_DIM, BLK), jnp.float32)]
        state = lax.fori_loop(first_block(offs_ref, qrow), qb + 1, key_step, tuple(init))
        parts = []
        for h in range(heads):
            top, total, acc = state[3 * h: 3 * h + 3]
            out = acc / total
            wide_ref[h * HEAD_DIM:(h + 1) * HEAD_DIM, cols] = out
            lse_ref[h:h + 1, cols] = top + jnp.log2(total)
            parts.append(out)
        low_ref[cols, :] = jnp.concatenate(parts, axis=0).T.astype(jnp.bfloat16)
        return carry

    lax.fori_loop(0, group_len // BLK, query_step, 0)
    outs.append(pltpu.make_async_copy(wide_ref, wide_out, local_sem.at[2]))
    outs[2].start()
    deal_rows(perm_col_ref, low_ref, dealt_ref, dealt_out, deal_sem)
    for copy in outs:
        copy.wait()


def backward_kernel(offs_ref, grad_ref, sorted_in, perm_row_ref, perm_col_ref, start_ref, wide_in, lse_ref,
                    dealt_out, sorted_ref, wide_ref, dealt_ref, do_ref, kt_ref, delta_ref, dk_ref, dv_ref, low_ref,
                    local_sem, deal_sem):
    copies = [pltpu.make_async_copy(sorted_in, sorted_ref, local_sem.at[0]),
              pltpu.make_async_copy(wide_in, wide_ref, local_sem.at[1])]
    for copy in copies:
        copy.start()
    group_len = sorted_ref.shape[0]
    width = sorted_ref.shape[1] // 3
    heads = width // HEAD_DIM
    unit = HEAD_DIM ** -0.5
    scale = unit * LOG2E
    sort_rows(perm_row_ref, grad_ref, do_ref)
    dk_ref[...] = jnp.zeros_like(dk_ref)
    dv_ref[...] = jnp.zeros_like(dv_ref)
    for copy in copies:
        copy.wait()

    def flip(i, carry):
        rows = pl.ds(pl.multiple_of(i * BLK, BLK), BLK)
        kt_ref[:, rows] = sorted_ref[rows, width: 2 * width].T
        product = do_ref[rows, :].astype(jnp.float32).T * wide_ref[:, rows]
        for h in range(heads):
            delta_ref[h:h + 1, rows] = jnp.sum(product[h * HEAD_DIM:(h + 1) * HEAD_DIM], axis=0, keepdims=True)
        return carry

    lax.fori_loop(0, group_len // BLK, flip, 0)

    def query_step(qb, carry):
        qrow = pl.multiple_of(qb * BLK, BLK)
        cols = pl.ds(qrow, BLK)

        def key_step(kb, state):
            krow = pl.multiple_of(kb * BLK, BLK)
            krows = pl.ds(krow, BLK)
            allowed = allowed_block(start_ref, cols, qb, kb)
            fresh = []
            for h in range(heads):
                hq = slice(h * HEAD_DIM, (h + 1) * HEAD_DIM)
                hk = slice(width + h * HEAD_DIM, width + (h + 1) * HEAD_DIM)
                hv = slice(2 * width + h * HEAD_DIM, 2 * width + (h + 1) * HEAD_DIM)
                q = sorted_ref[cols, hq]
                do = do_ref[cols, hq]
                s = dot(sorted_ref[krows, hk], q, NT) * scale
                s = jnp.where(allowed, s, -1e30)
                p = jnp.exp2(s - lse_ref[h:h + 1, cols])
                dp = dot(sorted_ref[krows, hv], do, NT)
                ds = (p * (dp - delta_ref[h:h + 1, cols])).astype(jnp.bfloat16)
                dv_ref[krows, hq] += dot(p.astype(jnp.bfloat16), do)
                dk_ref[krows, hq] += dot(ds, q)
                fresh.append(state[h] + dot(kt_ref[hq, krows], ds))
            return tuple(fresh)

        state = lax.fori_loop(first_block(offs_ref, qrow), qb + 1, key_step,
                              tuple(jnp.zeros((HEAD_DIM, BLK), jnp.float32) for _ in range(heads)))
        low_ref[cols, :width] = (jnp.concatenate(state, axis=0) * unit).T.astype(jnp.bfloat16)
        return carry

    lax.fori_loop(0, group_len // BLK, query_step, 0)
    low_ref[:, width:2 * width] = (dk_ref[...] * unit).astype(jnp.bfloat16)
    low_ref[:, 2 * width:] = dv_ref[...].astype(jnp.bfloat16)
    deal_rows(perm_col_ref, low_ref, dealt_ref, dealt_out, deal_sem)


def hbm():
    return pl.BlockSpec(memory_space=pltpu.HBM)


def vmem():
    return pl.BlockSpec(memory_space=pltpu.VMEM)


def attention_forward(offs, rows, slab, perm, start):
    group_len, model = rows.shape
    columns = slab.shape[1] - 128
    width = columns // 3
    shape = jax.ShapeDtypeStruct
    return pl.pallas_call(
        forward_kernel,
        name="attention_forward",
        out_shape=(
            shape((group_len, columns), jnp.bfloat16),
            shape((group_len, width), jnp.bfloat16),
            shape((width, group_len), jnp.float32),
            shape((8, group_len), jnp.float32),
            shape((group_len, model), jnp.bfloat16),
            shape((8, model), jnp.float32),
        ),
        in_specs=[pl.BlockSpec(memory_space=pltpu.SMEM)] + [vmem()] * 5,
        out_specs=(hbm(), hbm(), hbm(), vmem(), hbm(), vmem()),
        scratch_shapes=[
            pltpu.VMEM((group_len, columns), jnp.bfloat16),
            pltpu.VMEM((group_len, width), jnp.bfloat16),
            pltpu.VMEM((width, group_len), jnp.float32),
            pltpu.VMEM((group_len, model), jnp.bfloat16),
            pltpu.VMEM((group_len, columns), jnp.bfloat16),
            pltpu.VMEM((width, group_len), jnp.bfloat16),
            pltpu.VMEM((group_len, width), jnp.bfloat16),
            pltpu.SemaphoreType.DMA((3,)),
            pltpu.SemaphoreType.DMA((group_len // BLK,)),
        ],
        compiler_params=pltpu.CompilerParams(vmem_limit_bytes=48 << 20),
        cost_estimate=pl.CostEstimate(flops=24_000_000_000, bytes_accessed=16 << 20, transcendentals=0),
    )(offs, rows, slab, perm.reshape(1, group_len), perm.reshape(group_len, 1), start.reshape(1, group_len))


def attention_backward(offs, grad, ordered, perm, start, wide, lse):
    group_len, columns = ordered.shape
    width = columns // 3
    return pl.pallas_call(
        backward_kernel,
        name="attention_backward",
        out_shape=jax.ShapeDtypeStruct((group_len, columns), jnp.bfloat16),
        in_specs=[pl.BlockSpec(memory_space=pltpu.SMEM), vmem(), hbm(), vmem(), vmem(), vmem(), hbm(), vmem()],
        out_specs=hbm(),
        scratch_shapes=[
            pltpu.VMEM((group_len, columns), jnp.bfloat16),
            pltpu.VMEM((width, group_len), jnp.float32),
            pltpu.VMEM((group_len, columns), jnp.bfloat16),
            pltpu.VMEM((group_len, width), jnp.bfloat16),
            pltpu.VMEM((width, group_len), jnp.bfloat16),
            pltpu.VMEM((8, group_len), jnp.float32),
            pltpu.VMEM((group_len, width), jnp.float32),
            pltpu.VMEM((group_len, width), jnp.float32),
            pltpu.VMEM((group_len, columns), jnp.bfloat16),
            pltpu.SemaphoreType.DMA((2,)),
            pltpu.SemaphoreType.DMA((group_len // BLK,)),
        ],
        compiler_params=pltpu.CompilerParams(vmem_limit_bytes=48 << 20),
        cost_estimate=pl.CostEstimate(flops=40_000_000_000, bytes_accessed=16 << 20, transcendentals=0),
    )(offs, grad, ordered, perm.reshape(1, group_len), perm.reshape(group_len, 1), start.reshape(1, group_len), wide, lse)


epsilon = 1e-05


def rms_scale(values):
    return lax.rsqrt(jnp.mean(values * values, axis=-1, keepdims=True) + epsilon)


MESH = pl.DeviceIdType.MESH
TN = (((0,), (0,)), ((), ()))
TILE = 256


def seq_peers():
    mine = lax.axis_index("seq")
    return mine, (mine + 1 - 2 * lax.rem(mine, 2), lax.rem(mine + 2, 4), 3 - mine)


def greet(peers, others=()):
    barrier = pltpu.get_barrier_semaphore()
    for peer in others:
        pl.semaphore_signal(barrier, inc=1, device_id={"fsdp": peer}, device_id_type=MESH)
    for peer in peers:
        pl.semaphore_signal(barrier, inc=1, device_id={"seq": peer}, device_id_type=MESH)
    return lambda: pl.semaphore_wait(barrier, len(peers) + len(others))


def span(index, size):
    return pl.ds(pl.multiple_of(index * size, size), size)


def sender(send_sem, recv_sem):
    def send(index, src, dst, axis, peer):
        return pltpu.make_async_remote_copy(
            src_ref=src, dst_ref=dst, send_sem=send_sem.at[index], recv_sem=recv_sem.at[index],
            device_id={axis: peer}, device_id_type=MESH)
    return send


def shard_peers(count):
    mine = lax.axis_index("fsdp")
    sibling = mine + 1 - 2 * lax.rem(mine, 2)
    return mine, sibling, [lax.rem(mine + 2 * k, count) for k in range(1, count // 2)]


def starter(local_sem):
    def local(index, src, dst):
        copy = pltpu.make_async_copy(src, dst, local_sem.at[index])
        copy.start()
        return copy
    return local


def pair_sum(send, base, place, sibling, others, source, twin, total, take, shard):
    count = 2 * (len(others) + 1)
    twins = [send(base + k, source(span(lax.rem(sibling + 2 * k, count), shard)), twin.at[k], "fsdp", sibling)
             for k in range(count // 2)]
    direct = [send(base + count // 2 + k, total.at[k], take.at[k], "fsdp", others[k - 1]) for k in range(1, count // 2)]

    def start():
        for copy in twins:
            copy.start()

    def pass_on():
        for k in range(1, count // 2) :
            twins[k].wait_recv()
            total[k] = (source(span(lax.rem(place + 2 * k, count), shard))[...].astype(jnp.float32)
                        + twin[k].astype(jnp.float32)).astype(jnp.bfloat16)
            direct[k - 1].start()

    def finish(out_ref):
        twins[0].wait_recv()
        value = source(span(place, shard))[...].astype(jnp.float32) + twin[0].astype(jnp.float32)
        for k in range(1, count // 2):
            direct[k - 1].wait()
            value += take[k].astype(jnp.float32)
        out_ref[...] = value.astype(jnp.bfloat16)
        for copy in twins:
            copy.wait_send()

    return start, pass_on, finish


def spread(send, base, own, slots, peers):
    px, py, _ = peers
    half = own.shape[0] // 2
    top, bottom = pl.ds(0, half), pl.ds(half, half)
    x_slot, y_slot, far_slot = slots
    x_top = send(base, own.at[top], x_slot.at[top], "seq", px)
    y_bottom = send(base + 1, own.at[bottom], y_slot.at[bottom], "seq", py)
    x_bottom = send(base + 2, own.at[bottom], x_slot.at[bottom], "seq", px)
    y_top = send(base + 3, own.at[top], y_slot.at[top], "seq", py)
    x_relay = send(base + 4, x_slot.at[top], far_slot.at[top], "seq", py)
    y_relay = send(base + 5, y_slot.at[bottom], far_slot.at[bottom], "seq", px)
    for copy in (x_top, y_bottom, x_bottom, y_top):
        copy.start()

    def forward():
        x_top.wait_recv()
        x_relay.start()
        y_bottom.wait_recv()
        y_relay.start()

    def finish():
        for copy in (x_top, y_bottom, x_bottom, y_top, x_relay, y_relay):
            copy.wait_send()

    return forward, (x_bottom.wait_recv, y_top.wait_recv, lambda: (x_relay.wait_recv(), y_relay.wait_recv())), finish


def collect(send, base, give, transit, take, peers, cut):
    px, py, _ = peers
    half = give.shape[1] // 2
    size = half // cut
    halves = (pl.ds(0, half), pl.ds(half, half))
    pieces = [[pl.ds(h * half + c * size, size) for c in range(cut)] for h in range(2)]
    first, second = (px, py), (py, px)
    far = [[send(base + h * cut + c, give.at[2, pieces[h][c]], transit.at[h, pl.ds(c * size, size)], "seq", first[h])
            for c in range(cut)] for h in range(2)]
    plain = [send(base + 2 * cut + h, give.at[h, halves[h]], take.at[h, halves[h]], "seq", first[h]) for h in range(2)]
    summed = [[send(base + 2 * cut + 2 + h * cut + c, give.at[1 - h, pieces[h][c]], take.at[1 - h, pieces[h][c]],
                    "seq", second[h]) for c in range(cut)] for h in range(2)]

    def start_far(h):
        for copy in far[h]:
            copy.start()

    def merge(h, c):
        far[h][c].wait_recv()

        def step(i, carry):
            rows = pl.ds(pl.multiple_of(h * half + c * size + i * 64, 64), 64)
            more = pl.ds(pl.multiple_of(c * size + i * 64, 64), 64)
            give[1 - h, rows, :] = (give[1 - h, rows, :].astype(jnp.float32)
                                    + transit[h, more, :].astype(jnp.float32)).astype(jnp.bfloat16)
            return carry

        lax.fori_loop(0, size // 64, step, 0)
        summed[h][c].start()

    def finish(h):
        plain[h].wait()
        for c in range(cut):
            summed[h][c].wait()
            far[h][c].wait_send()

    return start_far, (plain[0].start, plain[1].start), merge, finish


def middle_kernel(out_ref, x_ref, weight_in, gate_up_in, down_in, gains_ref, dy0_in, dy1_in, dy2_in, dy3_in,
                  hidden_out, branch0_out, branch1_out, branch2_out, branch3_out, grads_out, dh_out,
                  do_ref, gain_grad_ref, down_piece_ref,
                  raw_ref, tail_in, weight_ref, dy_ref, hidden_ref, branch_ref, grads_ref, mixed_ref, normed_ref, act_ref, dgu_ref,
                  give_ref, transit_ref, take_ref, own_ref, low_ref, do_give_ref, twin_ref, total_ref, shard_take_ref,
                  local_sem, send_sem, recv_sem):
    low = jnp.bfloat16
    rows, model = x_ref.shape
    width = out_ref.shape[1]
    units = act_ref.shape[2]
    early = units - TILE
    tail_at = model + 3 * early
    shard = tail_in.shape[0]
    count = model // shard
    mine, peers = seq_peers()
    px, py, _ = peers
    place, sibling, others = shard_peers(count)
    half = rows // 2
    halves = (pl.ds(0, half), pl.ds(half, half))
    whole = pl.ds(0, rows)
    send = sender(send_sem, recv_sem)
    local = starter(local_sem)
    branch_outs = (branch0_out, branch1_out, branch2_out, branch3_out)
    out_in = local(0, weight_in.at[:, :model], weight_ref.at[:, :model])
    feed_in = [local(1, weight_in.at[:, model:], weight_ref.at[:, model:tail_at])]
    feed_in += [local(2 + k, dy_in, dy_ref.at[k]) for k, dy_in in enumerate((dy0_in, dy1_in, dy2_in, dy3_in))]

    def tiles(amount, body, first=0):
        def step(i, carry):
            body(pl.multiple_of(i * TILE, TILE))
            return carry
        lax.fori_loop(first, first + amount // TILE, step, 0)

    def half_of(owner, h):
        return pl.ds(pl.multiple_of(owner * rows + h * half, half), half)

    ready = greet(peers, [sibling] + others)
    raw = [local(14 + b, weight.at[:, pl.ds(pl.multiple_of(at * units + early, TILE), TILE)],
                 raw_ref.at[:, pl.ds(b * TILE, TILE)])
           for b, (weight, at) in enumerate(((gate_up_in, mine), (gate_up_in, 4 + mine), (down_in, mine)))]
    for copy in raw:
        copy.wait()
    tail_in[...] = raw_ref[...].astype(low)
    mixed_ref[:, span(mine, width)] = out_ref[span(mine, rows), :]
    tail_ref = weight_ref.at[span(place, shard), tail_at:]
    tail_ref[...] = tail_in[...]
    ready()
    turn = [[send(3 * h + k, out_ref.at[half_of(peer, h), :], mixed_ref.at[halves[h], span(mine, width)], "seq", peer)
             for k, peer in enumerate(peers)] for h in range(2)]
    for h in range(2):
        for k in (2, 0, 1):
            turn[h][k].start()

    def tail_of(owner):
        return weight_ref.at[span(owner, shard), tail_at:]

    tails = [send(28 + k, tail_in, tail_of(place), "fsdp", peer) for k, peer in enumerate([sibling] + others)]
    for k in list(range(1, len(tails))) + [0]:
        tails[k].start()
    parts = [tail_of(lax.rem(place - 2 * k + count, count)) for k in range(1, len(tails))]
    twins = [send(29 + count // 2 + k, part, part, "fsdp", sibling) for k, part in enumerate(parts)]

    def pass_tail(k):
        tails[k].wait_recv()
        twins[k - 1].start()

    steps = [range(1 + (len(others) * t) // 3, 1 + (len(others) * (t + 1)) // 3) for t in range(3)]
    for copy in feed_in:
        copy.wait()

    def grad_act(down_at, dup_at):
        def step(slot, carry):
            dgu_ref[slot, :, pl.ds(dup_at, TILE)] = dot(dy_ref[slot], weight_ref[:, pl.ds(down_at, TILE)]).astype(low)
            return carry
        lax.fori_loop(0, 4, step, 0)

    tiles(early, lambda f: grad_act(model + 2 * early + f, early + f))
    x_sends = [send(6 + h, normed_ref.at[0, halves[h]], normed_ref.at[1, halves[h]], "seq", px) for h in range(2)]
    y_sends = [send(8 + h, normed_ref.at[0, halves[h]], normed_ref.at[2, halves[h]], "seq", py) for h in range(2)]
    x_relay = send(10, normed_ref.at[1, halves[0]], normed_ref.at[3, halves[0]], "seq", py)
    y_relay = send(11, normed_ref.at[2, halves[1]], normed_ref.at[3, halves[1]], "seq", px)
    for h in range(2):
        for k in range(3):
            turn[h][k].wait_recv()
        if h == 0:
            out_in.wait()

        def project(c, h=h):
            cols = pl.ds(c, TILE)
            hidden_ref[halves[h], cols] = x_ref[halves[h], cols].astype(jnp.float32) + dot(
                mixed_ref[halves[h], :], weight_ref[:, cols])

        tiles(model, project)

        def norm(i, carry, h=h):
            part = pl.ds(pl.multiple_of(h * half + i * 64, 64), 64)
            value = hidden_ref[part, :]
            normed_ref[0, part, :] = (value * rms_scale(value) * gains_ref[1:2, :]).astype(low)
            return carry

        lax.fori_loop(0, half // 64, norm, 0)
        x_sends[h].start()
        y_sends[h].start()
        for k in steps[h]:
            pass_tail(k)

    def unit_tile(slot, part, gate_at, up_at, act_at, dgate_at, dup_at):
        gate = dot(normed_ref[slot, part, :], weight_ref[:, pl.ds(gate_at, TILE)])
        up = dot(normed_ref[slot, part, :], weight_ref[:, pl.ds(up_at, TILE)])
        grad_act = dgu_ref[slot, part, pl.ds(dup_at, TILE)].astype(jnp.float32)
        sigmoid = jax.nn.sigmoid(gate)
        silu = gate * sigmoid
        act_ref[slot, part, pl.ds(act_at, TILE)] = (silu * up).astype(low)
        dgu_ref[slot, part, pl.ds(dgate_at, TILE)] = (
            grad_act * up * sigmoid * (1.0 + gate * (1.0 - sigmoid))).astype(low)
        dgu_ref[slot, part, pl.ds(dup_at, TILE)] = (grad_act * silu).astype(low)

    def feed(slot, part):
        def step(i, carry):
            is_tail = (i * TILE == early).astype(jnp.int32)
            f = i * TILE

            def at(usual, last):
                return pl.multiple_of(usual + is_tail * (last - usual), TILE)

            unit_tile(slot, part, at(model + f, tail_at), at(model + early + f, tail_at + TILE),
                      pl.multiple_of(f, TILE), at(f, 2 * early),
                      at(early + f, 2 * early + TILE))
            return carry
        lax.fori_loop(0, units // TILE, step, 0)

    def back(slot, part):
        def body(c):
            cols = pl.ds(c, TILE)
            value = dot(dgu_ref[slot, part, :2 * early], weight_ref[cols, model:model + 2 * early], NT) + dot(
                dgu_ref[slot, part, 2 * early:], weight_ref[cols, tail_at:tail_at + 2 * TILE], NT)

            if isinstance(slot, int):
                own_ref[part, cols] = value
            else:
                give_ref[slot - 1, part, cols] = value.astype(low)
        tiles(model, body)

    start_far, start_plain, merge, finish = collect(send, 12, give_ref, transit_ref, take_ref, peers, 2)
    outs = [local(6, hidden_ref, hidden_out)]
    for k in steps[2]:
        pass_tail(k)
    tails[0].wait_recv()
    for copy in twins:
        copy.wait_recv()
    grad_act(tail_at + 2 * TILE, 2 * early + TILE)
    unit_count = units // TILE

    def branch(i, carry):
        cols = pl.ds(pl.multiple_of(i % (model // TILE) * TILE, TILE), TILE)
        slot = i // (model // TILE)
        branch_ref[slot, :, cols] = (
            dot(act_ref[slot, :, :early], weight_ref[cols, model + 2 * early:tail_at], NT)
            + dot(act_ref[slot, :, early:], weight_ref[cols, tail_at + 2 * TILE:], NT)).astype(low)
        for k in range(4):
            @pl.when(i == (k + 1) * (model // TILE) - 1)
            def _():
                branch_copies[k].start()
        return carry

    branch_copies = [pltpu.make_async_copy(branch_ref.at[k], branch_outs[k], local_sem.at[(7, 10, 11, 12)[k]])
                     for k in range(4)]

    def work(i, carry):
        def flag(test):
            return test.astype(jnp.int32)

        slot = flag(i >= 2) + flag((i == 3) | (i == 4)) + 2 * flag(i >= 6)
        h = flag((i == 1) | (i == 4) | (i == 5) | (i == 7))
        part = pl.ds(pl.multiple_of(h * half, half), half)

        def on(index, *actions):
            @pl.when(i == index)
            def _():
                for action in actions:
                    action()

        on(2, x_sends[0].wait_recv, x_relay.start)
        on(3, y_sends[0].wait_recv)
        on(4, y_sends[1].wait_recv, y_relay.start)
        on(5, x_sends[1].wait_recv)
        @pl.when(i == 6)
        def _():
            lax.fori_loop(0, 2 * (model // TILE), branch, 0)

        on(6, x_relay.wait_recv)
        on(7, y_relay.wait_recv)
        feed(slot, part)
        back(slot, part)
        on(2, start_plain[0])
        on(4, start_plain[1])
        on(6, lambda: start_far(0))
        on(7, lambda: start_far(1))
        return carry

    feed(0, whole)
    back(0, whole)
    lax.fori_loop(2, 8, work, 0)

    def weight_grad(left_ref, right_ref, base, first, amount):
        def step(i, carry):
            part = pl.ds(pl.multiple_of(i % 2 * (model // 2), model // 2), model // 2)
            f = pl.multiple_of(i // 2 * TILE, TILE)
            acc = dot(left_ref[0, :, part], right_ref[0, :, pl.ds(f, TILE)], TN)
            for slot in range(1, 4):
                acc += dot(left_ref[slot, :, part], right_ref[slot, :, pl.ds(f, TILE)], TN)
            grads_ref[part, pl.ds(base + f, TILE)] = acc.astype(low)
            return carry
        lax.fori_loop(2 * first, 2 * (first + amount), step, 0)

    def gate_up_grad(first, amount):
        weight_grad(normed_ref, dgu_ref, 0, first, amount)

    down_cols = pl.ds(2 * units, units)

    shard_start, shard_pass, shard_finish = pair_sum(
        send, 28 + count, place, sibling, others, lambda part: grads_ref.at[part, down_cols],
        twin_ref, total_ref, shard_take_ref, shard)
    weight_grad(dy_ref, act_ref, 2 * units, 0, 2)
    merge(0, 0)
    merge(1, 0)
    weight_grad(dy_ref, act_ref, 2 * units, 2, unit_count - 2)
    merge(0, 1)
    merge(1, 1)
    shard_start()
    gate_up_grad(0, 5)
    shard_pass()
    gain_grad_ref[...] = jnp.zeros_like(gain_grad_ref)
    sends = [[send(22 + 3 * h + k, do_give_ref.at[k, halves[h]], do_ref.at[half_of(mine, h), :], "seq", peer)
              for k, peer in enumerate(peers)] for h in range(2)]
    for h in range(2):
        finish(h)

        def norm_back(i, carry, h=h):
            part = pl.ds(pl.multiple_of(h * half + i * 64, 64), 64)
            value = hidden_ref[part, :]
            inv = rms_scale(value)
            grad = own_ref[part, :] + take_ref[0, part, :].astype(jnp.float32) + take_ref[1, part, :].astype(jnp.float32)
            gain_grad_ref[0:1, :] += jnp.sum(grad * value * inv, axis=0, keepdims=True)
            scaled = grad * gains_ref[1:2, :]
            dh = dy_ref[0, part, :].astype(jnp.float32) + (
                inv * scaled - value * inv**3 * jnp.mean(value * scaled, axis=-1, keepdims=True))
            own_ref[part, :] = dh
            low_ref[part, :] = dh.astype(low)
            return carry

        lax.fori_loop(0, half // 64, norm_back, 0)
        for k in (2, 0, 1):
            do_give_ref[k, halves[h], :] = dot(
                low_ref[halves[h], :], weight_ref[span(peers[k], width), :model], NT).astype(low)
            sends[h][k].start()
        do_ref[half_of(mine, h), :] = dot(low_ref[halves[h], :], weight_ref[span(mine, width), :model], NT).astype(low)
    outs.append(local(8, own_ref, dh_out))
    gate_up_grad(5, 2 * units // TILE - 5)
    outs.append(local(9, grads_ref.at[:, :2 * units], grads_out.at[:, :2 * units]))

    def out_grad(c):
        cols = pl.ds(c, TILE)
        grads_ref[:, pl.ds(3 * units + c, TILE)] = dot(mixed_ref[...], low_ref[:, cols], TN).astype(low)

    tiles(model, out_grad)
    outs.append(local(13, grads_ref.at[:, 3 * units:], grads_out.at[:, 2 * units:]))

    lax.fori_loop(2 * (model // TILE), 4 * (model // TILE), branch, 0)
    outs += branch_copies
    shard_finish(down_piece_ref)
    for copy in outs:
        copy.wait()
    for copy in tails + twins:
        copy.wait_send()
    for h in range(2):
        x_sends[h].wait_send()
        y_sends[h].wait_send()
        for k in range(3):
            turn[h][k].wait_send()
            sends[h][k].wait()
    x_relay.wait_send()
    y_relay.wait_send()


def middle(dealt_out, x, weights, gate_up, down, gains, dy, units):
    low = jnp.bfloat16
    group_len, width = dealt_out.shape
    rows, model = x.shape
    shard = down.shape[0]
    count = model // shard
    f32 = jnp.float32
    shape = jax.ShapeDtypeStruct
    copies = 28 + 2 * count
    return pl.pallas_call(
        middle_kernel,
        name="middle",
        out_shape=(
            shape((rows, model), f32),
            *[shape((rows, model), low)] * 4,
            shape((model, 2 * units + model), low),
            shape((rows, model), f32),
            shape((group_len, width), low),
            shape((8, model), f32),
            shape((shard, units), low),
        ),
        in_specs=[vmem(), vmem(), hbm(), hbm(), hbm(), vmem()] + [hbm()] * 4,
        out_specs=(hbm(),) * 7 + (vmem(),) * 3,
        scratch_shapes=[
            pltpu.VMEM((shard, 3 * TILE), f32),
            pltpu.VMEM((shard, 3 * TILE), low),
            pltpu.VMEM((model, model + 3 * units), low),
            pltpu.VMEM((4, rows, model), low),
            pltpu.VMEM((rows, model), f32),
            pltpu.VMEM((4, rows, model), low),
            pltpu.VMEM((model, 3 * units + model), low),
            pltpu.VMEM((rows, model), low),
            pltpu.VMEM((4, rows, model), low),
            pltpu.VMEM((4, rows, units), low),
            pltpu.VMEM((4, rows, 2 * units), low),
            pltpu.VMEM((3, rows, model), low),
            pltpu.VMEM((2, rows // 2, model), low),
            pltpu.VMEM((2, rows, model), low),
            pltpu.VMEM((rows, model), f32),
            pltpu.VMEM((rows, model), low),
            pltpu.VMEM((3, rows, width), low),
            pltpu.VMEM((count // 2, shard, units), low),
            pltpu.VMEM((count // 2, shard, units), low),
            pltpu.VMEM((count // 2, shard, units), low),
            pltpu.SemaphoreType.DMA((17,)),
            pltpu.SemaphoreType.DMA((copies,)),
            pltpu.SemaphoreType.DMA((copies,)),
        ],
        compiler_params=pltpu.CompilerParams(
            vmem_limit_bytes=62 << 20, collective_id=1, has_side_effects=True),
        cost_estimate=pl.CostEstimate(flops=60_000_000_000, bytes_accessed=40 << 20, transcendentals=0),
    )(dealt_out, x, weights, gate_up, down, gains, *dy)


def gather_kernel(x_ref, all_ref, local_sem, send_sem, recv_sem):
    rows = x_ref.shape[0]
    mine, peers = seq_peers()
    send = sender(send_sem, recv_sem)
    half = rows // 2
    px, py, _ = peers

    def part(owner, h):
        return all_ref.at[pl.ds(pl.multiple_of(owner * rows + h * half, half), half)]

    ready = greet(peers)
    keep = pltpu.make_async_copy(x_ref, all_ref.at[span(mine, rows)], local_sem)
    keep.start()
    ready()
    x_sends = [send(h, x_ref.at[pl.ds(h * half, half)], part(mine, h), "seq", px) for h in range(2)]
    y_sends = [send(2 + h, x_ref.at[pl.ds(h * half, half)], part(mine, h), "seq", py) for h in range(2)]
    for copy in (x_sends[0], y_sends[1], x_sends[1], y_sends[0]):
        copy.start()
    x_relay = send(4, part(px, 0), part(px, 0), "seq", py)
    y_relay = send(5, part(py, 1), part(py, 1), "seq", px)
    x_sends[0].wait_recv()
    x_relay.start()
    y_sends[1].wait_recv()
    y_relay.start()
    x_sends[1].wait_recv()
    y_sends[0].wait_recv()
    for copy in x_sends + y_sends:
        copy.wait_send()
    x_relay.wait()
    y_relay.wait()
    keep.wait()


def gather_rows(x):
    rows, model = x.shape
    return pl.pallas_call(
        gather_kernel,
        name="gather_rows",
        out_shape=jax.ShapeDtypeStruct((4 * rows, model), x.dtype),
        in_specs=[hbm()],
        out_specs=hbm(),
        scratch_shapes=[
            pltpu.SemaphoreType.DMA,
            pltpu.SemaphoreType.DMA((6,)),
            pltpu.SemaphoreType.DMA((6,)),
        ],
        compiler_params=pltpu.CompilerParams(collective_id=0, has_side_effects=True),
        cost_estimate=pl.CostEstimate(flops=40_000_000_000, bytes_accessed=20 << 20, transcendentals=0),
    )(x)


def rear_kernel(grad_ref, normed_in, slab_ref, gains_ref, x_in, dh_in, hidden_in, branch0_in, branch1_in, branch2_in,
                branch3_in, result_out, input_grad_out, gain_grad_ref, piece_ref,
                result_ref, input_grad_ref, normed_ref, x_ref, dh_ref, hidden_ref, branch_ref, give_ref, transit_ref, take_ref, own_ref, term_ref,
                twin_ref, total_ref, shard_take_ref, local_sem, send_sem, recv_sem):
    low = jnp.bfloat16
    rows, model = result_ref.shape
    shard, columns = piece_ref.shape
    count = model // shard
    half = rows // 2
    mine, peers = seq_peers()
    place, sibling, others = shard_peers(count)
    send = sender(send_sem, recv_sem)
    local = starter(local_sem)
    normed_copy = local(0, normed_in, normed_ref)
    row_copies = [local(1, x_in, x_ref), local(2, dh_in, dh_ref)]
    result_copies = [local(3, hidden_in, hidden_ref)]
    result_copies.append(local(4, branch0_in, branch_ref))

    def partial(owner, first, amount, store):
        block = pl.ds(pl.multiple_of(owner * rows + first, half), amount)

        def body(i, carry):
            cols = pl.ds(pl.multiple_of(i * TILE, TILE), TILE)
            store(cols, dot(grad_ref[block, :], slab_ref[cols, :columns], NT))
            return carry

        lax.fori_loop(0, model // TILE, body, 0)

    def hand(k, first, amount):
        def store(cols, value):
            give_ref[k, pl.ds(first, amount), cols] = value.astype(low)
        partial(peers[k], first, amount, store)

    def keep(cols, value):
        own_ref[:, cols] = value

    ready = greet(peers, [sibling] + others)
    hand(2, 0, half)
    ready()
    start_far, start_plain, merge, finish = collect(send, 0, give_ref, transit_ref, take_ref, peers, 2)
    start_far(0)
    hand(2, half, half)
    start_far(1)
    for h in range(2):
        hand(h, 0, rows)
        start_plain[h]()

    def weight_term(i, carry):
        part = pl.ds(pl.multiple_of(i * TILE, TILE), TILE)
        term_ref[part, :] = dot(normed_ref[:, part], grad_ref[...], TN).astype(low)
        return carry

    normed_copy.wait()
    lax.fori_loop(0, model // TILE, weight_term, 0)
    shard_start, shard_pass, shard_finish = pair_sum(
        send, 10, place, sibling, others, lambda part: term_ref.at[part], twin_ref, total_ref, shard_take_ref, shard)
    shard_start()
    for c in range(2):
        for h in range(2):
            merge(h, c)
    shard_pass()
    partial(mine, 0, rows, keep)
    for copy in result_copies:
        copy.wait()

    def result(i, carry):
        part = pl.ds(pl.multiple_of(i * 64, 64), 64)
        value = hidden_ref[part, :]
        for piece in (branch_ref, branch1_in, branch2_in, branch3_in):
            value += piece[part, :].astype(jnp.float32)
        result_ref[part, :] = value.astype(low)
        return carry

    lax.fori_loop(0, rows // 64, result, 0)
    outs = [local(8, result_ref, result_out)]
    for copy in row_copies:
        copy.wait()
    gain_grad_ref[...] = jnp.zeros_like(gain_grad_ref)

    def norm_back(i, carry):
        part = pl.ds(pl.multiple_of(i * 64, 64), 64)
        x = x_ref[part, :].astype(jnp.float32)
        inv = rms_scale(x)
        grad = own_ref[part, :] + take_ref[0, part, :].astype(jnp.float32) + take_ref[1, part, :].astype(jnp.float32)
        gain_grad_ref[0:1, :] += jnp.sum(grad * x * inv, axis=0, keepdims=True)
        scaled = grad * gains_ref[0:1, :]
        input_grad_ref[part, :] = (dh_ref[part, :] + (
            inv * scaled - x * inv**3 * jnp.mean(x * scaled, axis=-1, keepdims=True))).astype(low)
        return carry

    for h in range(2):
        finish(h)
        lax.fori_loop(h * half // 64, (h + 1) * half // 64, norm_back, 0)
        part = pl.ds(h * half, half)
        outs.append(local(9 + h, input_grad_ref.at[part], input_grad_out.at[part]))
    shard_finish(piece_ref)
    for copy in outs:
        copy.wait()


def rear(grad, normed, slab, gains, x, dh, hidden, branch, shard):
    low = jnp.bfloat16
    f32 = jnp.float32
    rows, model = x.shape
    group_len, columns = grad.shape
    count = model // shard
    shape = jax.ShapeDtypeStruct
    copies = 10 + count
    return pl.pallas_call(
        rear_kernel,
        name="rear",
        out_shape=(shape((rows, model), low), shape((rows, model), low), shape((8, model), f32),
                   shape((shard, columns), low)),
        in_specs=[vmem(), hbm(), vmem(), vmem()] + [hbm()] * 4 + [vmem()] * 3,
        out_specs=(hbm(), hbm(), vmem(), vmem()),
        scratch_shapes=[
            pltpu.VMEM((rows, model), low),
            pltpu.VMEM((rows, model), low),
            pltpu.VMEM((group_len, model), low),
            pltpu.VMEM((rows, model), low),
            pltpu.VMEM((rows, model), f32),
            pltpu.VMEM((rows, model), f32),
            pltpu.VMEM((rows, model), low),
            pltpu.VMEM((3, rows, model), low),
            pltpu.VMEM((2, rows // 2, model), low),
            pltpu.VMEM((2, rows, model), low),
            pltpu.VMEM((rows, model), f32),
            pltpu.VMEM((model, columns), low),
            pltpu.VMEM((count // 2, shard, columns), low),
            pltpu.VMEM((count // 2, shard, columns), low),
            pltpu.VMEM((count // 2, shard, columns), low),
            pltpu.SemaphoreType.DMA((11,)),
            pltpu.SemaphoreType.DMA((copies,)),
            pltpu.SemaphoreType.DMA((copies,)),
        ],
        compiler_params=pltpu.CompilerParams(
            vmem_limit_bytes=56 << 20, collective_id=2, has_side_effects=True),
        cost_estimate=pl.CostEstimate(flops=50_000_000_000, bytes_accessed=20 << 20, transcendentals=0),
    )(grad, normed, slab, gains, x, dh, hidden, *branch)


def last_kernel(pieces_ref, qkv_ref, down_ref, gain_a_ref, gain_b_ref, out_qkv_ref, out_out_ref, out_gate_up_ref, out_down_ref,
                gains_ref, block_ref, slots_ref, gain_own_ref, gain_take_ref, gain_slots_ref, local_sem, send_sem, recv_sem):
    low = jnp.bfloat16
    shard, columns = qkv_ref.shape
    model = gain_a_ref.shape[1]
    count = model // shard
    units = out_down_ref.shape[1] // 4
    width = columns // 3
    mine, peers = seq_peers()
    place, sibling, _ = shard_peers(count)
    everyone = [lax.rem(place + k, count) for k in range(1, count)]
    send = sender(send_sem, recv_sem)
    ready = greet(peers, everyone)
    local = starter(local_sem)
    fills = [local(0, qkv_ref, block_ref.at[:, :columns]), local(1, down_ref, block_ref.at[:, columns:columns + units]),
             local(2, pieces_ref, block_ref.at[:, columns + units:])]
    gain_own_ref[0:1, :] = gain_a_ref[0:1, :]
    gain_own_ref[1:2, :] = gain_b_ref[0:1, :]
    gain_own_ref[2:8, :] = jnp.zeros((6, model), jnp.float32)
    for copy in fills:
        copy.wait()
    ready()
    forward, arrivals, finish = spread(send, 0, block_ref, [slots_ref.at[k] for k in range(3)], peers)
    gain_sends = [send(6 + k, gain_own_ref, gain_take_ref.at[k], "fsdp", peer) for k, peer in enumerate(everyone)]
    for copy in gain_sends:
        copy.start()

    def place_block(source, owner, first):
        for b in range(3):
            out_qkv_ref[:, span(b * 4 + owner, width)] = source[:, b * width:(b + 1) * width]
        out_down_ref[:, span(owner, units)] = source[:, columns:columns + units]
        at = columns + units
        for shift, size in ((0, units - TILE), (units - TILE, TILE)):
            for b in range(2):
                out_gate_up_ref[:, pl.ds(pl.multiple_of((b * 4 + owner) * units + shift, TILE), size)] = (
                    source[:, at:at + size])
                at += size
        if first:
            out_out_ref[...] = source[:, at:].astype(jnp.float32)
        else:
            out_out_ref[...] += source[:, at:].astype(jnp.float32)

    place_block(block_ref, mine, True)
    forward()
    total = gain_own_ref[...]
    for k, copy in enumerate(gain_sends):
        copy.wait_recv()
        total += gain_take_ref[k]
    gains_ref[...] = total
    seq_sends = [send(6 + len(everyone) + k, gains_ref, gain_slots_ref.at[k], "seq", peer) for k, peer in enumerate(peers)]
    for copy in seq_sends:
        copy.start()
    for k in range(3):
        arrivals[k]()
        place_block(slots_ref.at[k], peers[k], False)
    for copy in seq_sends:
        copy.wait()
    gains_ref[...] += gain_slots_ref[0] + gain_slots_ref[1] + gain_slots_ref[2]
    for copy in gain_sends:
        copy.wait_send()
    finish()


def last(pieces, qkv_piece, down_piece, gain_a, gain_b, units):
    low = jnp.bfloat16
    shard, columns = qkv_piece.shape
    model = gain_a.shape[1]
    count = model // shard
    f32 = jnp.float32
    shape = jax.ShapeDtypeStruct
    wide = columns + units + pieces.shape[1]
    copies = 9 + count
    return pl.pallas_call(
        last_kernel,
        name="last",
        out_shape=(
            shape((shard, 4 * columns), low),
            shape((shard, model), f32),
            shape((shard, 8 * units), low),
            shape((shard, 4 * units), low),
            shape((8, model), f32),
        ),
        in_specs=[hbm()] * 3 + [vmem()] * 2,
        out_specs=(vmem(),) * 5,
        scratch_shapes=[
            pltpu.VMEM((shard, wide), low),
            pltpu.VMEM((3, shard, wide), low),
            pltpu.VMEM((8, model), f32),
            pltpu.VMEM((count - 1, 8, model), f32),
            pltpu.VMEM((3, 8, model), f32),
            pltpu.SemaphoreType.DMA((3,)),
            pltpu.SemaphoreType.DMA((copies,)),
            pltpu.SemaphoreType.DMA((copies,)),
        ],
        compiler_params=pltpu.CompilerParams(
            vmem_limit_bytes=40 << 20, collective_id=3, has_side_effects=True),
        cost_estimate=pl.CostEstimate(flops=40_000_000_000, bytes_accessed=20 << 20, transcendentals=0),
    )(pieces, qkv_piece, down_piece, gain_a, gain_b)


def widen_kernel(*refs):
    for source, target in zip(refs[:6], refs[6:]):
        target[...] = source[...].astype(target.dtype)


def widen(shard, arrays):
    steps = max(shard // 32, 1)
    specs = [pl.BlockSpec((array.shape[0] // steps, array.shape[1]), lambda i: (i, 0)) for array in arrays]
    return pl.pallas_call(
        widen_kernel,
        name="widen",
        grid=(steps,),
        out_shape=[jax.ShapeDtypeStruct(array.shape, jnp.float32 if array.shape[0] == shard else array.dtype)
                   for array in arrays],
        in_specs=specs,
        out_specs=specs,
        compiler_params=pltpu.CompilerParams(vmem_limit_bytes=40 << 20),
    )(*arrays)


def swaps(rows):
    return [lax.ppermute(piece, "seq", table) for piece, table in zip(
        rows, ([(i, i ^ 1) for i in range(4)], [(i, (i + 2) % 4) for i in range(4)], [(i, 3 - i) for i in range(4)]))]


def on_device(block_input, norm_gain_a, weight_qkv, weight_out, norm_gain_b, weight_gate_up, weight_down,
              cotangent, permutation, lengths, offsets):
    low = jnp.bfloat16
    f32 = jnp.float32
    seq_count = lax.axis_size("seq")
    mine = lax.axis_index("seq")
    row_count, model_width = block_input.shape[1:]
    group_len = row_count * seq_count
    shard = weight_qkv.shape[0]
    head_width = weight_qkv.shape[1] // 3 // seq_count
    part_units = weight_down.shape[1] // seq_count
    perm = permutation[0]
    offs = offsets[0]
    position = jnp.arange(group_len, dtype=jnp.int32)
    start = jnp.max(jnp.where(offs[None, :] <= position[:, None], offs[None, :], 0), axis=1)

    def columns(weight, width, first, amount):
        blocks = weight.shape[1] // (seq_count * width)
        return [lax.dynamic_slice_in_dim(weight, (b * seq_count + mine) * width + first, amount, axis=1).astype(low)
                for b in range(blocks)]

    def gather_weight(parts):
        return lax.all_gather(jnp.concatenate(parts, axis=1), "fsdp", axis=0, tiled=True)

    early = part_units - TILE
    gain_cols = jnp.pad(jnp.stack([norm_gain_a, norm_gain_b], axis=1).astype(low), ((0, 0), (0, 126)))
    slab = gather_weight(columns(weight_qkv, head_width, 0, head_width) + [gain_cols])
    weights = gather_weight([weight_out.astype(low)] + columns(weight_gate_up, part_units, 0, early)
                            + columns(weight_down, part_units, 0, early))
    rows_all = gather_rows(block_input[0])
    grad_own, rows_all = lax.optimization_barrier((cotangent[0], rows_all))
    grad_rows = [cotangent[0]] + swaps([grad_own] * 3)
    ordered, dealt_out, wide_out, log_total, normed_a, gains = attention_forward(offs, rows_all, slab, perm, start)
    hidden, branch0, branch1, branch2, branch3, grads, grad_hidden, grad_heads, gain_b_term, down_piece = middle(
        dealt_out, block_input[0], weights, weight_gate_up, weight_down, gains, grad_rows, part_units)
    pieces = lax.psum_scatter(grads, "fsdp", scatter_dimension=0, tiled=True)
    branch = [branch0] + swaps([branch1, branch2, branch3])
    dealt_grad = attention_backward(offs, grad_heads, ordered, perm, start, wide_out, log_total)
    result_rows, input_grad, gain_a_term, qkv_piece = rear(
        dealt_grad, normed_a, slab, gains, block_input[0], grad_hidden, hidden, branch, shard)
    grad_qkv, grad_out, grad_gate_up, grad_down, gain_terms = last(
        pieces, qkv_piece, down_piece, gain_a_term, gain_b_term, part_units)
    gain_terms = lax.dynamic_slice_in_dim(gain_terms, lax.axis_index("fsdp") * shard, shard, axis=1)
    grad_qkv, grad_out, grad_gate_up, grad_down, result_rows, input_grad = widen(
        shard, [grad_qkv, grad_out, grad_gate_up, grad_down, result_rows, input_grad])
    return (
        result_rows[None],
        input_grad[None],
        gain_terms[0],
        grad_qkv,
        grad_out,
        gain_terms[1],
        grad_gate_up,
        grad_down,
    )


def solution(mesh):
    rows = P("fsdp", "seq", None)
    vector = P("fsdp")
    matrix = P("fsdp", None)
    return jax.shard_map(
        on_device,
        mesh=mesh,
        in_specs=(rows, vector, matrix, matrix, vector, matrix, matrix, rows, matrix, matrix, matrix),
        out_specs=(rows, rows, vector, matrix, matrix, vector, matrix, matrix),
        check_vma=False,
    )
```

```python
import jax
import jax.numpy as jnp
from jax import lax
from jax.experimental import pallas as pl
from jax.experimental.pallas import tpu as pltpu
from jax.sharding import PartitionSpec as P

HEAD_DIM = 64
BLK = 256
LOG2E = 1.4426950408889634

NT = (((1,), (1,)), ((), ()))
NN = (((1,), (0,)), ((), ()))


def dot(a, b, dims=NN):
    return lax.dot_general(a, b, dims, preferred_element_type=jnp.float32)


def first_block(offs_ref, row0):
    best = jnp.int32(0)
    for k in range(offs_ref.shape[0]):
        off = offs_ref[k]
        best = jnp.where(off <= row0, jnp.maximum(best, off), best)
    return best // BLK


def sort_rows(perm_row_ref, src_ref, dst_ref):
    group_len = src_ref.shape[0]

    def step(i, carry):
        rows = pl.ds(pl.multiple_of(i * BLK, BLK), BLK)
        pos = lax.broadcasted_iota(jnp.int32, (BLK, group_len), 0) + i * BLK
        pick = (perm_row_ref[...] == pos).astype(jnp.float32).astype(jnp.bfloat16)
        dst_ref[rows, :] = dot(pick, src_ref[...]).astype(dst_ref.dtype)
        return carry

    lax.fori_loop(0, group_len // BLK, step, 0)


def deal_rows(perm_col_ref, src_ref, dst_ref, out_ref, sems):
    group_len = src_ref.shape[0]

    def copy_out(i):
        rows = pl.ds(pl.multiple_of(i * BLK, BLK), BLK)
        return pltpu.make_async_copy(dst_ref.at[rows, :], out_ref.at[rows, :], sems.at[i])

    def step(i, carry):
        rows = pl.ds(pl.multiple_of(i * BLK, BLK), BLK)
        pos = lax.broadcasted_iota(jnp.int32, (BLK, group_len), 1)
        pick = (perm_col_ref[rows, :] == pos).astype(jnp.float32).astype(jnp.bfloat16)
        dst_ref[rows, :] = dot(pick, src_ref[...]).astype(dst_ref.dtype)
        copy_out(i).start()
        return carry

    def wait(i, carry):
        copy_out(i).wait()
        return carry

    lax.fori_loop(0, group_len // BLK, step, 0)
    lax.fori_loop(0, group_len // BLK, wait, 0)


def allowed_block(start_ref, cols, qb, kb):
    key_pos = lax.broadcasted_iota(jnp.int32, (BLK, BLK), 0) + kb * BLK
    query_pos = lax.broadcasted_iota(jnp.int32, (BLK, BLK), 1) + qb * BLK
    return (key_pos <= query_pos) & (key_pos >= start_ref[:, cols])


def forward_kernel(offs_ref, x_ref, slab_ref, perm_row_ref, perm_col_ref, start_ref,
                   sorted_out, dealt_out, wide_out, lse_ref, normed_out, gains_ref,
                   sorted_ref, dealt_ref, wide_ref, normed_ref, qkv_ref, vt_ref, low_ref, local_sem, deal_sem):
    group_len, model = x_ref.shape
    width = qkv_ref.shape[1] // 3
    heads = width // HEAD_DIM
    scale = HEAD_DIM ** -0.5 * LOG2E

    def gain(i, carry):
        part = pl.ds(pl.multiple_of(i * 128, 128), 128)
        gains_ref[:, part] = slab_ref[part, 3 * width:].astype(jnp.float32).T[:8]
        return carry

    lax.fori_loop(0, model // 128, gain, 0)

    def project(i, carry):
        rows = pl.ds(pl.multiple_of(i * BLK, BLK), BLK)
        for r in range(0, BLK, 64):
            part = pl.ds(pl.multiple_of(i * BLK + r, 64), 64)
            x = x_ref[part, :].astype(jnp.float32)
            normed_ref[part, :] = (x * rms_scale(x) * gains_ref[0:1, :]).astype(jnp.bfloat16)
        qkv_ref[rows, :] = dot(normed_ref[rows, :], slab_ref[:, :3 * width]).astype(jnp.bfloat16)
        return carry

    lax.fori_loop(0, group_len // BLK, project, 0)
    outs = [pltpu.make_async_copy(normed_ref, normed_out, local_sem.at[0])]
    outs[0].start()
    sort_rows(perm_row_ref, qkv_ref, sorted_ref)
    outs.append(pltpu.make_async_copy(sorted_ref, sorted_out, local_sem.at[1]))
    outs[1].start()

    def flip(i, carry):
        rows = pl.ds(pl.multiple_of(i * BLK, BLK), BLK)
        vt_ref[:, rows] = sorted_ref[rows, 2 * width:].T
        return carry

    lax.fori_loop(0, group_len // BLK, flip, 0)

    def query_step(qb, carry):
        qrow = pl.multiple_of(qb * BLK, BLK)
        cols = pl.ds(qrow, BLK)

        def key_step(kb, state):
            krow = pl.multiple_of(kb * BLK, BLK)
            krows = pl.ds(krow, BLK)
            allowed = allowed_block(start_ref, cols, qb, kb)
            fresh = []
            for h in range(heads):
                top, total, acc = state[3 * h: 3 * h + 3]
                hq = slice(h * HEAD_DIM, (h + 1) * HEAD_DIM)
                hk = slice(width + h * HEAD_DIM, width + (h + 1) * HEAD_DIM)
                s = dot(sorted_ref[krows, hk], sorted_ref[cols, hq], NT) * scale
                s = jnp.where(allowed, s, -1e30)
                new_top = jnp.maximum(top, jnp.max(s, axis=0, keepdims=True))
                shrink = jnp.exp2(top - new_top)
                p = jnp.exp2(s - new_top)
                total = total * shrink + jnp.sum(p, axis=0, keepdims=True)
                acc = acc * shrink + dot(vt_ref[hq, krows], p.astype(jnp.bfloat16))
                fresh += [new_top, total, acc]
            return tuple(fresh)

        init = []
        for h in range(heads):
            init += [jnp.full((1, BLK), -1e30, jnp.float32), jnp.zeros((1, BLK), jnp.float32),
                     jnp.zeros((HEAD_DIM, BLK), jnp.float32)]
        state = lax.fori_loop(first_block(offs_ref, qrow), qb + 1, key_step, tuple(init))
        parts = []
        for h in range(heads):
            top, total, acc = state[3 * h: 3 * h + 3]
            out = acc / total
            wide_ref[h * HEAD_DIM:(h + 1) * HEAD_DIM, cols] = out
            lse_ref[h:h + 1, cols] = top + jnp.log2(total)
            parts.append(out)
        low_ref[cols, :] = jnp.concatenate(parts, axis=0).T.astype(jnp.bfloat16)
        return carry

    lax.fori_loop(0, group_len // BLK, query_step, 0)
    outs.append(pltpu.make_async_copy(wide_ref, wide_out, local_sem.at[2]))
    outs[2].start()
    deal_rows(perm_col_ref, low_ref, dealt_ref, dealt_out, deal_sem)
    for copy in outs:
        copy.wait()


def backward_kernel(offs_ref, grad_ref, sorted_in, perm_row_ref, perm_col_ref, start_ref, wide_in, lse_ref,
                    dealt_out, sorted_ref, wide_ref, dealt_ref, do_ref, kt_ref, delta_ref, dk_ref, dv_ref, low_ref,
                    local_sem, deal_sem):
    copies = [pltpu.make_async_copy(sorted_in, sorted_ref, local_sem.at[0]),
              pltpu.make_async_copy(wide_in, wide_ref, local_sem.at[1])]
    for copy in copies:
        copy.start()
    group_len = sorted_ref.shape[0]
    width = sorted_ref.shape[1] // 3
    heads = width // HEAD_DIM
    unit = HEAD_DIM ** -0.5
    scale = unit * LOG2E
    sort_rows(perm_row_ref, grad_ref, do_ref)
    dk_ref[...] = jnp.zeros_like(dk_ref)
    dv_ref[...] = jnp.zeros_like(dv_ref)
    for copy in copies:
        copy.wait()

    def flip(i, carry):
        rows = pl.ds(pl.multiple_of(i * BLK, BLK), BLK)
        kt_ref[:, rows] = sorted_ref[rows, width: 2 * width].T
        product = do_ref[rows, :].astype(jnp.float32).T * wide_ref[:, rows]
        for h in range(heads):
            delta_ref[h:h + 1, rows] = jnp.sum(product[h * HEAD_DIM:(h + 1) * HEAD_DIM], axis=0, keepdims=True)
        return carry

    lax.fori_loop(0, group_len // BLK, flip, 0)

    def query_step(qb, carry):
        qrow = pl.multiple_of(qb * BLK, BLK)
        cols = pl.ds(qrow, BLK)

        def key_step(kb, state):
            krow = pl.multiple_of(kb * BLK, BLK)
            krows = pl.ds(krow, BLK)
            allowed = allowed_block(start_ref, cols, qb, kb)
            fresh = []
            for h in range(heads):
                hq = slice(h * HEAD_DIM, (h + 1) * HEAD_DIM)
                hk = slice(width + h * HEAD_DIM, width + (h + 1) * HEAD_DIM)
                hv = slice(2 * width + h * HEAD_DIM, 2 * width + (h + 1) * HEAD_DIM)
                q = sorted_ref[cols, hq]
                do = do_ref[cols, hq]
                s = dot(sorted_ref[krows, hk], q, NT) * scale
                s = jnp.where(allowed, s, -1e30)
                p = jnp.exp2(s - lse_ref[h:h + 1, cols])
                dp = dot(sorted_ref[krows, hv], do, NT)
                ds = (p * (dp - delta_ref[h:h + 1, cols])).astype(jnp.bfloat16)
                dv_ref[krows, hq] += dot(p.astype(jnp.bfloat16), do)
                dk_ref[krows, hq] += dot(ds, q)
                fresh.append(state[h] + dot(kt_ref[hq, krows], ds))
            return tuple(fresh)

        state = lax.fori_loop(first_block(offs_ref, qrow), qb + 1, key_step,
                              tuple(jnp.zeros((HEAD_DIM, BLK), jnp.float32) for _ in range(heads)))
        low_ref[cols, :width] = (jnp.concatenate(state, axis=0) * unit).T.astype(jnp.bfloat16)
        return carry

    lax.fori_loop(0, group_len // BLK, query_step, 0)
    low_ref[:, width:2 * width] = (dk_ref[...] * unit).astype(jnp.bfloat16)
    low_ref[:, 2 * width:] = dv_ref[...].astype(jnp.bfloat16)
    deal_rows(perm_col_ref, low_ref, dealt_ref, dealt_out, deal_sem)


def hbm():
    return pl.BlockSpec(memory_space=pltpu.HBM)


def vmem():
    return pl.BlockSpec(memory_space=pltpu.VMEM)


def attention_forward(offs, rows, slab, perm, start):
    group_len, model = rows.shape
    columns = slab.shape[1] - 128
    width = columns // 3
    shape = jax.ShapeDtypeStruct
    return pl.pallas_call(
        forward_kernel,
        name="attention_forward",
        out_shape=(
            shape((group_len, columns), jnp.bfloat16),
            shape((group_len, width), jnp.bfloat16),
            shape((width, group_len), jnp.float32),
            shape((8, group_len), jnp.float32),
            shape((group_len, model), jnp.bfloat16),
            shape((8, model), jnp.float32),
        ),
        in_specs=[pl.BlockSpec(memory_space=pltpu.SMEM)] + [vmem()] * 5,
        out_specs=(hbm(), hbm(), hbm(), vmem(), hbm(), vmem()),
        scratch_shapes=[
            pltpu.VMEM((group_len, columns), jnp.bfloat16),
            pltpu.VMEM((group_len, width), jnp.bfloat16),
            pltpu.VMEM((width, group_len), jnp.float32),
            pltpu.VMEM((group_len, model), jnp.bfloat16),
            pltpu.VMEM((group_len, columns), jnp.bfloat16),
            pltpu.VMEM((width, group_len), jnp.bfloat16),
            pltpu.VMEM((group_len, width), jnp.bfloat16),
            pltpu.SemaphoreType.DMA((3,)),
            pltpu.SemaphoreType.DMA((group_len // BLK,)),
        ],
        compiler_params=pltpu.CompilerParams(vmem_limit_bytes=62 << 20),
        cost_estimate=pl.CostEstimate(flops=24_000_000_000, bytes_accessed=16 << 20, transcendentals=0),
    )(offs, rows, slab, perm.reshape(1, group_len), perm.reshape(group_len, 1), start.reshape(1, group_len))


def attention_backward(offs, grad, ordered, perm, start, wide, lse):
    group_len, columns = ordered.shape
    width = columns // 3
    return pl.pallas_call(
        backward_kernel,
        name="attention_backward",
        out_shape=jax.ShapeDtypeStruct((group_len, columns), jnp.bfloat16),
        in_specs=[pl.BlockSpec(memory_space=pltpu.SMEM), vmem(), hbm(), vmem(), vmem(), vmem(), hbm(), vmem()],
        out_specs=hbm(),
        scratch_shapes=[
            pltpu.VMEM((group_len, columns), jnp.bfloat16),
            pltpu.VMEM((width, group_len), jnp.float32),
            pltpu.VMEM((group_len, columns), jnp.bfloat16),
            pltpu.VMEM((group_len, width), jnp.bfloat16),
            pltpu.VMEM((width, group_len), jnp.bfloat16),
            pltpu.VMEM((8, group_len), jnp.float32),
            pltpu.VMEM((group_len, width), jnp.float32),
            pltpu.VMEM((group_len, width), jnp.float32),
            pltpu.VMEM((group_len, columns), jnp.bfloat16),
            pltpu.SemaphoreType.DMA((2,)),
            pltpu.SemaphoreType.DMA((group_len // BLK,)),
        ],
        compiler_params=pltpu.CompilerParams(vmem_limit_bytes=62 << 20),
        cost_estimate=pl.CostEstimate(flops=40_000_000_000, bytes_accessed=16 << 20, transcendentals=0),
    )(offs, grad, ordered, perm.reshape(1, group_len), perm.reshape(group_len, 1), start.reshape(1, group_len), wide, lse)


epsilon = 1e-05


def rms_scale(values):
    return lax.rsqrt(jnp.mean(values * values, axis=-1, keepdims=True) + epsilon)


MESH = pl.DeviceIdType.MESH
TN = (((0,), (0,)), ((), ()))
TILE = 256


def seq_peers():
    mine = lax.axis_index("seq")
    return mine, (mine + 1 - 2 * lax.rem(mine, 2), lax.rem(mine + 2, 4), 3 - mine)


def greet(peers, others=()):
    barrier = pltpu.get_barrier_semaphore()
    for peer in others:
        pl.semaphore_signal(barrier, inc=1, device_id={"fsdp": peer}, device_id_type=MESH)
    for peer in peers:
        pl.semaphore_signal(barrier, inc=1, device_id={"seq": peer}, device_id_type=MESH)
    return lambda: pl.semaphore_wait(barrier, len(peers) + len(others))


def span(index, size):
    return pl.ds(pl.multiple_of(index * size, size), size)


def sender(send_sem, recv_sem):
    def send(index, src, dst, axis, peer):
        return pltpu.make_async_remote_copy(
            src_ref=src, dst_ref=dst, send_sem=send_sem.at[index], recv_sem=recv_sem.at[index],
            device_id={axis: peer}, device_id_type=MESH)
    return send


def shard_peers(count):
    mine = lax.axis_index("fsdp")
    sibling = mine + 1 - 2 * lax.rem(mine, 2)
    return mine, sibling, [lax.rem(mine + 2 * k, count) for k in range(1, count // 2)]


def starter(local_sem):
    def local(index, src, dst):
        copy = pltpu.make_async_copy(src, dst, local_sem.at[index])
        copy.start()
        return copy
    return local


def pair_sum(send, base, place, sibling, others, source, twin, total, take, shard):
    count = 2 * (len(others) + 1)
    twins = [send(base + k, source(span(lax.rem(sibling + 2 * k, count), shard)), twin.at[k], "fsdp", sibling)
             for k in range(count // 2)]
    direct = [send(base + count // 2 + k, total.at[k], take.at[k], "fsdp", others[k - 1]) for k in range(1, count // 2)]

    def start():
        for copy in twins:
            copy.start()

    def pass_on():
        for k in range(1, count // 2) :
            twins[k].wait_recv()
            total[k] = (source(span(lax.rem(place + 2 * k, count), shard))[...].astype(jnp.float32)
                        + twin[k].astype(jnp.float32)).astype(jnp.bfloat16)
            direct[k - 1].start()

    def finish(out_ref):
        twins[0].wait_recv()
        value = source(span(place, shard))[...].astype(jnp.float32) + twin[0].astype(jnp.float32)
        for k in range(1, count // 2):
            direct[k - 1].wait()
            value += take[k].astype(jnp.float32)
        out_ref[...] = value.astype(jnp.bfloat16)
        for copy in twins:
            copy.wait_send()

    return start, pass_on, finish


def spread(send, base, own, slots, peers):
    px, py, _ = peers
    half = own.shape[0] // 2
    top, bottom = pl.ds(0, half), pl.ds(half, half)
    x_slot, y_slot, far_slot = slots
    x_top = send(base, own.at[top], x_slot.at[top], "seq", px)
    y_bottom = send(base + 1, own.at[bottom], y_slot.at[bottom], "seq", py)
    x_bottom = send(base + 2, own.at[bottom], x_slot.at[bottom], "seq", px)
    y_top = send(base + 3, own.at[top], y_slot.at[top], "seq", py)
    x_relay = send(base + 4, x_slot.at[top], far_slot.at[top], "seq", py)
    y_relay = send(base + 5, y_slot.at[bottom], far_slot.at[bottom], "seq", px)
    for copy in (x_top, y_bottom, x_bottom, y_top):
        copy.start()

    def forward():
        x_top.wait_recv()
        x_relay.start()
        y_bottom.wait_recv()
        y_relay.start()

    def finish():
        for copy in (x_top, y_bottom, x_bottom, y_top, x_relay, y_relay):
            copy.wait_send()

    return forward, (x_bottom.wait_recv, y_top.wait_recv, lambda: (x_relay.wait_recv(), y_relay.wait_recv())), finish


def collect(send, base, give, transit, take, peers, cut):
    px, py, _ = peers
    half = give.shape[1] // 2
    size = half // cut
    halves = (pl.ds(0, half), pl.ds(half, half))
    pieces = [[pl.ds(h * half + c * size, size) for c in range(cut)] for h in range(2)]
    first, second = (px, py), (py, px)
    far = [[send(base + h * cut + c, give.at[2, pieces[h][c]], transit.at[h, pl.ds(c * size, size)], "seq", first[h])
            for c in range(cut)] for h in range(2)]
    plain = [send(base + 2 * cut + h, give.at[h, halves[h]], take.at[h, halves[h]], "seq", first[h]) for h in range(2)]
    summed = [[send(base + 2 * cut + 2 + h * cut + c, give.at[1 - h, pieces[h][c]], take.at[1 - h, pieces[h][c]],
                    "seq", second[h]) for c in range(cut)] for h in range(2)]

    def start_far(h):
        for copy in far[h]:
            copy.start()

    def merge(h, c):
        far[h][c].wait_recv()

        def step(i, carry):
            rows = pl.ds(pl.multiple_of(h * half + c * size + i * 64, 64), 64)
            more = pl.ds(pl.multiple_of(c * size + i * 64, 64), 64)
            give[1 - h, rows, :] = (give[1 - h, rows, :].astype(jnp.float32)
                                    + transit[h, more, :].astype(jnp.float32)).astype(jnp.bfloat16)
            return carry

        lax.fori_loop(0, size // 64, step, 0)
        summed[h][c].start()

    def finish(h):
        plain[h].wait()
        for c in range(cut):
            summed[h][c].wait()
            far[h][c].wait_send()

    return start_far, (plain[0].start, plain[1].start), merge, finish


def middle_kernel(out_ref, x_ref, weight_in, gate_up_in, down_in, gains_ref, dy0_in, dy1_in, dy2_in, dy3_in,
                  hidden_out, branch0_out, branch1_out, branch2_out, branch3_out, grads_out, dh_out,
                  do_ref, gain_grad_ref, down_piece_ref,
                  raw_ref, tail_in, weight_ref, dy_ref, hidden_ref, branch_ref, grads_ref, mixed_ref, normed_ref, act_ref, dgu_ref,
                  give_ref, transit_ref, take_ref, own_ref, low_ref, do_give_ref, twin_ref, total_ref, shard_take_ref,
                  local_sem, send_sem, recv_sem):
    low = jnp.bfloat16
    rows, model = x_ref.shape
    width = out_ref.shape[1]
    units = act_ref.shape[2]
    early = units - TILE
    tail_at = model + 3 * early
    shard = tail_in.shape[0]
    count = model // shard
    mine, peers = seq_peers()
    px, py, _ = peers
    place, sibling, others = shard_peers(count)
    half = rows // 2
    halves = (pl.ds(0, half), pl.ds(half, half))
    whole = pl.ds(0, rows)
    send = sender(send_sem, recv_sem)
    local = starter(local_sem)
    branch_outs = (branch0_out, branch1_out, branch2_out, branch3_out)
    out_in = local(0, weight_in.at[:, :model], weight_ref.at[:, :model])
    feed_in = [local(1, weight_in.at[:, model:], weight_ref.at[:, model:tail_at])]
    feed_in += [local(2 + k, dy_in, dy_ref.at[k]) for k, dy_in in enumerate((dy0_in, dy1_in, dy2_in, dy3_in))]

    def tiles(amount, body, first=0):
        def step(i, carry):
            body(pl.multiple_of(i * TILE, TILE))
            return carry
        lax.fori_loop(first, first + amount // TILE, step, 0)

    def half_of(owner, h):
        return pl.ds(pl.multiple_of(owner * rows + h * half, half), half)

    ready = greet(peers, [sibling] + others)
    raw = [local(14 + b, weight.at[:, pl.ds(pl.multiple_of(at * units + early, TILE), TILE)],
                 raw_ref.at[:, pl.ds(b * TILE, TILE)])
           for b, (weight, at) in enumerate(((gate_up_in, mine), (gate_up_in, 4 + mine), (down_in, mine)))]
    for copy in raw:
        copy.wait()
    tail_in[...] = raw_ref[...].astype(low)
    mixed_ref[:, span(mine, width)] = out_ref[span(mine, rows), :]
    tail_ref = weight_ref.at[span(place, shard), tail_at:]
    tail_ref[...] = tail_in[...]
    ready()
    turn = [[send(3 * h + k, out_ref.at[half_of(peer, h), :], mixed_ref.at[halves[h], span(mine, width)], "seq", peer)
             for k, peer in enumerate(peers)] for h in range(2)]
    for h in range(2):
        for k in (2, 0, 1):
            turn[h][k].start()

    def tail_of(owner):
        return weight_ref.at[span(owner, shard), tail_at:]

    tails = [send(28 + k, tail_in, tail_of(place), "fsdp", peer) for k, peer in enumerate([sibling] + others)]
    for k in list(range(1, len(tails))) + [0]:
        tails[k].start()
    parts = [tail_of(lax.rem(place - 2 * k + count, count)) for k in range(1, len(tails))]
    twins = [send(29 + count // 2 + k, part, part, "fsdp", sibling) for k, part in enumerate(parts)]

    def pass_tail(k):
        tails[k].wait_recv()
        twins[k - 1].start()

    steps = [range(1 + (len(others) * t) // 3, 1 + (len(others) * (t + 1)) // 3) for t in range(3)]
    for copy in feed_in:
        copy.wait()

    def grad_act(down_at, dup_at):
        def step(slot, carry):
            dgu_ref[slot, :, pl.ds(dup_at, TILE)] = dot(dy_ref[slot], weight_ref[:, pl.ds(down_at, TILE)]).astype(low)
            return carry
        lax.fori_loop(0, 4, step, 0)

    tiles(early, lambda f: grad_act(model + 2 * early + f, early + f))
    x_sends = [send(6 + h, normed_ref.at[0, halves[h]], normed_ref.at[1, halves[h]], "seq", px) for h in range(2)]
    y_sends = [send(8 + h, normed_ref.at[0, halves[h]], normed_ref.at[2, halves[h]], "seq", py) for h in range(2)]
    x_relay = send(10, normed_ref.at[1, halves[0]], normed_ref.at[3, halves[0]], "seq", py)
    y_relay = send(11, normed_ref.at[2, halves[1]], normed_ref.at[3, halves[1]], "seq", px)
    for h in range(2):
        for k in range(3):
            turn[h][k].wait_recv()
        if h == 0:
            out_in.wait()

        def project(c, h=h):
            cols = pl.ds(c, TILE)
            hidden_ref[halves[h], cols] = x_ref[halves[h], cols].astype(jnp.float32) + dot(
                mixed_ref[halves[h], :], weight_ref[:, cols])

        tiles(model, project)

        def norm(i, carry, h=h):
            part = pl.ds(pl.multiple_of(h * half + i * 64, 64), 64)
            value = hidden_ref[part, :]
            normed_ref[0, part, :] = (value * rms_scale(value) * gains_ref[1:2, :]).astype(low)
            return carry

        lax.fori_loop(0, half // 64, norm, 0)
        x_sends[h].start()
        y_sends[h].start()
        for k in steps[h]:
            pass_tail(k)

    def unit_tile(slot, part, gate_at, up_at, act_at, dgate_at, dup_at):
        gate = dot(normed_ref[slot, part, :], weight_ref[:, pl.ds(gate_at, TILE)])
        up = dot(normed_ref[slot, part, :], weight_ref[:, pl.ds(up_at, TILE)])
        grad_act = dgu_ref[slot, part, pl.ds(dup_at, TILE)].astype(jnp.float32)
        sigmoid = jax.nn.sigmoid(gate)
        silu = gate * sigmoid
        act_ref[slot, part, pl.ds(act_at, TILE)] = (silu * up).astype(low)
        dgu_ref[slot, part, pl.ds(dgate_at, TILE)] = (
            grad_act * up * sigmoid * (1.0 + gate * (1.0 - sigmoid))).astype(low)
        dgu_ref[slot, part, pl.ds(dup_at, TILE)] = (grad_act * silu).astype(low)

    def feed(slot, part):
        def step(i, carry):
            is_tail = (i * TILE == early).astype(jnp.int32)
            f = i * TILE

            def at(usual, last):
                return pl.multiple_of(usual + is_tail * (last - usual), TILE)

            unit_tile(slot, part, at(model + f, tail_at), at(model + early + f, tail_at + TILE),
                      pl.multiple_of(f, TILE), at(f, 2 * early),
                      at(early + f, 2 * early + TILE))
            return carry
        lax.fori_loop(0, units // TILE, step, 0)

    def back(slot, part):
        def body(c):
            cols = pl.ds(c, TILE)
            value = dot(dgu_ref[slot, part, :2 * early], weight_ref[cols, model:model + 2 * early], NT) + dot(
                dgu_ref[slot, part, 2 * early:], weight_ref[cols, tail_at:tail_at + 2 * TILE], NT)

            if isinstance(slot, int):
                own_ref[part, cols] = value
            else:
                give_ref[slot - 1, part, cols] = value.astype(low)
        tiles(model, body)

    start_far, start_plain, merge, finish = collect(send, 12, give_ref, transit_ref, take_ref, peers, 2)
    outs = [local(6, hidden_ref, hidden_out)]
    for k in steps[2]:
        pass_tail(k)
    tails[0].wait_recv()
    for copy in twins:
        copy.wait_recv()
    grad_act(tail_at + 2 * TILE, 2 * early + TILE)
    unit_count = units // TILE

    def branch(i, carry):
        cols = pl.ds(pl.multiple_of(i % (model // TILE) * TILE, TILE), TILE)
        slot = i // (model // TILE)
        branch_ref[slot, :, cols] = (
            dot(act_ref[slot, :, :early], weight_ref[cols, model + 2 * early:tail_at], NT)
            + dot(act_ref[slot, :, early:], weight_ref[cols, tail_at + 2 * TILE:], NT)).astype(low)
        for k in range(4):
            @pl.when(i == (k + 1) * (model // TILE) - 1)
            def _():
                branch_copies[k].start()
        return carry

    branch_copies = [pltpu.make_async_copy(branch_ref.at[k], branch_outs[k], local_sem.at[(7, 10, 11, 12)[k]])
                     for k in range(4)]

    def work(i, carry):
        def flag(test):
            return test.astype(jnp.int32)

        slot = flag(i >= 2) + flag((i == 3) | (i == 4)) + 2 * flag(i >= 6)
        h = flag((i == 1) | (i == 4) | (i == 5) | (i == 7))
        part = pl.ds(pl.multiple_of(h * half, half), half)

        def on(index, *actions):
            @pl.when(i == index)
            def _():
                for action in actions:
                    action()

        on(2, x_sends[0].wait_recv, x_relay.start)
        on(3, y_sends[0].wait_recv)
        on(4, y_sends[1].wait_recv, y_relay.start)
        on(5, x_sends[1].wait_recv)
        @pl.when(i == 6)
        def _():
            lax.fori_loop(0, 2 * (model // TILE), branch, 0)

        on(6, x_relay.wait_recv)
        on(7, y_relay.wait_recv)
        feed(slot, part)
        back(slot, part)
        on(2, start_plain[0])
        on(4, start_plain[1])
        on(6, lambda: start_far(0))
        on(7, lambda: start_far(1))
        return carry

    feed(0, whole)
    back(0, whole)
    lax.fori_loop(2, 8, work, 0)

    def weight_grad(left_ref, right_ref, base, first, amount):
        def step(i, carry):
            part = pl.ds(pl.multiple_of(i % 2 * (model // 2), model // 2), model // 2)
            f = pl.multiple_of(i // 2 * TILE, TILE)
            acc = dot(left_ref[0, :, part], right_ref[0, :, pl.ds(f, TILE)], TN)
            for slot in range(1, 4):
                acc += dot(left_ref[slot, :, part], right_ref[slot, :, pl.ds(f, TILE)], TN)
            grads_ref[part, pl.ds(base + f, TILE)] = acc.astype(low)
            return carry
        lax.fori_loop(2 * first, 2 * (first + amount), step, 0)

    def gate_up_grad(first, amount):
        weight_grad(normed_ref, dgu_ref, 0, first, amount)

    down_cols = pl.ds(2 * units, units)

    shard_start, shard_pass, shard_finish = pair_sum(
        send, 28 + count, place, sibling, others, lambda part: grads_ref.at[part, down_cols],
        twin_ref, total_ref, shard_take_ref, shard)
    weight_grad(dy_ref, act_ref, 2 * units, 0, 2)
    merge(0, 0)
    merge(1, 0)
    weight_grad(dy_ref, act_ref, 2 * units, 2, unit_count - 2)
    merge(0, 1)
    merge(1, 1)
    shard_start()
    gate_up_grad(0, 5)
    shard_pass()
    gain_grad_ref[...] = jnp.zeros_like(gain_grad_ref)
    sends = [[send(22 + 3 * h + k, do_give_ref.at[k, halves[h]], do_ref.at[half_of(mine, h), :], "seq", peer)
              for k, peer in enumerate(peers)] for h in range(2)]
    for h in range(2):
        finish(h)

        def norm_back(i, carry, h=h):
            part = pl.ds(pl.multiple_of(h * half + i * 64, 64), 64)
            value = hidden_ref[part, :]
            inv = rms_scale(value)
            grad = own_ref[part, :] + take_ref[0, part, :].astype(jnp.float32) + take_ref[1, part, :].astype(jnp.float32)
            gain_grad_ref[0:1, :] += jnp.sum(grad * value * inv, axis=0, keepdims=True)
            scaled = grad * gains_ref[1:2, :]
            dh = dy_ref[0, part, :].astype(jnp.float32) + (
                inv * scaled - value * inv**3 * jnp.mean(value * scaled, axis=-1, keepdims=True))
            own_ref[part, :] = dh
            low_ref[part, :] = dh.astype(low)
            return carry

        lax.fori_loop(0, half // 64, norm_back, 0)
        for k in (2, 0, 1):
            do_give_ref[k, halves[h], :] = dot(
                low_ref[halves[h], :], weight_ref[span(peers[k], width), :model], NT).astype(low)
            sends[h][k].start()
        do_ref[half_of(mine, h), :] = dot(low_ref[halves[h], :], weight_ref[span(mine, width), :model], NT).astype(low)
    outs.append(local(8, own_ref, dh_out))
    gate_up_grad(5, 2 * units // TILE - 5)
    outs.append(local(9, grads_ref.at[:, :2 * units], grads_out.at[:, :2 * units]))

    def out_grad(c):
        cols = pl.ds(c, TILE)
        grads_ref[:, pl.ds(3 * units + c, TILE)] = dot(mixed_ref[...], low_ref[:, cols], TN).astype(low)

    tiles(model, out_grad)
    outs.append(local(13, grads_ref.at[:, 3 * units:], grads_out.at[:, 2 * units:]))

    lax.fori_loop(2 * (model // TILE), 4 * (model // TILE), branch, 0)
    outs += branch_copies
    shard_finish(down_piece_ref)
    for copy in outs:
        copy.wait()
    for copy in tails + twins:
        copy.wait_send()
    for h in range(2):
        x_sends[h].wait_send()
        y_sends[h].wait_send()
        for k in range(3):
            turn[h][k].wait_send()
            sends[h][k].wait()
    x_relay.wait_send()
    y_relay.wait_send()


def middle(dealt_out, x, weights, gate_up, down, gains, dy, units):
    low = jnp.bfloat16
    group_len, width = dealt_out.shape
    rows, model = x.shape
    shard = down.shape[0]
    count = model // shard
    f32 = jnp.float32
    shape = jax.ShapeDtypeStruct
    copies = 28 + 2 * count
    return pl.pallas_call(
        middle_kernel,
        name="middle",
        out_shape=(
            shape((rows, model), f32),
            *[shape((rows, model), low)] * 4,
            shape((model, 2 * units + model), low),
            shape((rows, model), f32),
            shape((group_len, width), low),
            shape((8, model), f32),
            shape((shard, units), low),
        ),
        in_specs=[vmem(), vmem(), hbm(), hbm(), hbm(), vmem()] + [hbm()] * 4,
        out_specs=(hbm(),) * 7 + (vmem(),) * 3,
        scratch_shapes=[
            pltpu.VMEM((shard, 3 * TILE), f32),
            pltpu.VMEM((shard, 3 * TILE), low),
            pltpu.VMEM((model, model + 3 * units), low),
            pltpu.VMEM((4, rows, model), low),
            pltpu.VMEM((rows, model), f32),
            pltpu.VMEM((4, rows, model), low),
            pltpu.VMEM((model, 3 * units + model), low),
            pltpu.VMEM((rows, model), low),
            pltpu.VMEM((4, rows, model), low),
            pltpu.VMEM((4, rows, units), low),
            pltpu.VMEM((4, rows, 2 * units), low),
            pltpu.VMEM((3, rows, model), low),
            pltpu.VMEM((2, rows // 2, model), low),
            pltpu.VMEM((2, rows, model), low),
            pltpu.VMEM((rows, model), f32),
            pltpu.VMEM((rows, model), low),
            pltpu.VMEM((3, rows, width), low),
            pltpu.VMEM((count // 2, shard, units), low),
            pltpu.VMEM((count // 2, shard, units), low),
            pltpu.VMEM((count // 2, shard, units), low),
            pltpu.SemaphoreType.DMA((17,)),
            pltpu.SemaphoreType.DMA((copies,)),
            pltpu.SemaphoreType.DMA((copies,)),
        ],
        compiler_params=pltpu.CompilerParams(
            vmem_limit_bytes=62 << 20, collective_id=1, has_side_effects=True),
        cost_estimate=pl.CostEstimate(flops=60_000_000_000, bytes_accessed=40 << 20, transcendentals=0),
    )(dealt_out, x, weights, gate_up, down, gains, *dy)


def gather_kernel(x_ref, all_ref, local_sem, send_sem, recv_sem):
    rows = x_ref.shape[0]
    mine, peers = seq_peers()
    send = sender(send_sem, recv_sem)
    half = rows // 2
    px, py, _ = peers

    def part(owner, h):
        return all_ref.at[pl.ds(pl.multiple_of(owner * rows + h * half, half), half)]

    ready = greet(peers)
    keep = pltpu.make_async_copy(x_ref, all_ref.at[span(mine, rows)], local_sem)
    keep.start()
    ready()
    x_sends = [send(h, x_ref.at[pl.ds(h * half, half)], part(mine, h), "seq", px) for h in range(2)]
    y_sends = [send(2 + h, x_ref.at[pl.ds(h * half, half)], part(mine, h), "seq", py) for h in range(2)]
    for copy in (x_sends[0], y_sends[1], x_sends[1], y_sends[0]):
        copy.start()
    x_relay = send(4, part(px, 0), part(px, 0), "seq", py)
    y_relay = send(5, part(py, 1), part(py, 1), "seq", px)
    x_sends[0].wait_recv()
    x_relay.start()
    y_sends[1].wait_recv()
    y_relay.start()
    x_sends[1].wait_recv()
    y_sends[0].wait_recv()
    for copy in x_sends + y_sends:
        copy.wait_send()
    x_relay.wait()
    y_relay.wait()
    keep.wait()


def gather_rows(x):
    rows, model = x.shape
    return pl.pallas_call(
        gather_kernel,
        name="gather_rows",
        out_shape=jax.ShapeDtypeStruct((4 * rows, model), x.dtype),
        in_specs=[hbm()],
        out_specs=hbm(),
        scratch_shapes=[
            pltpu.SemaphoreType.DMA,
            pltpu.SemaphoreType.DMA((6,)),
            pltpu.SemaphoreType.DMA((6,)),
        ],
        compiler_params=pltpu.CompilerParams(collective_id=0, has_side_effects=True),
        cost_estimate=pl.CostEstimate(flops=40_000_000_000, bytes_accessed=20 << 20, transcendentals=0),
    )(x)


def rear_kernel(grad_ref, normed_in, slab_ref, gains_ref, x_in, dh_in, hidden_in, branch0_in, branch1_in, branch2_in,
                branch3_in, result_out, input_grad_out, gain_grad_ref, piece_ref,
                result_ref, input_grad_ref, normed_ref, x_ref, dh_ref, hidden_ref, branch_ref, give_ref, transit_ref, take_ref, own_ref, term_ref,
                twin_ref, total_ref, shard_take_ref, local_sem, send_sem, recv_sem):
    low = jnp.bfloat16
    rows, model = result_ref.shape
    shard, columns = piece_ref.shape
    count = model // shard
    half = rows // 2
    mine, peers = seq_peers()
    place, sibling, others = shard_peers(count)
    send = sender(send_sem, recv_sem)
    local = starter(local_sem)
    normed_copy = local(0, normed_in, normed_ref)
    row_copies = [local(1, x_in, x_ref), local(2, dh_in, dh_ref)]
    result_copies = [local(3, hidden_in, hidden_ref)]
    result_copies += [local(4 + k, piece, branch_ref.at[k])
                      for k, piece in enumerate((branch0_in, branch1_in, branch2_in, branch3_in))]

    def partial(owner, first, amount, store):
        block = pl.ds(pl.multiple_of(owner * rows + first, half), amount)

        def body(i, carry):
            cols = pl.ds(pl.multiple_of(i * TILE, TILE), TILE)
            store(cols, dot(grad_ref[block, :], slab_ref[cols, :columns], NT))
            return carry

        lax.fori_loop(0, model // TILE, body, 0)

    def hand(k, first, amount):
        def store(cols, value):
            give_ref[k, pl.ds(first, amount), cols] = value.astype(low)
        partial(peers[k], first, amount, store)

    def keep(cols, value):
        own_ref[:, cols] = value

    ready = greet(peers, [sibling] + others)
    hand(2, 0, half)
    ready()
    start_far, start_plain, merge, finish = collect(send, 0, give_ref, transit_ref, take_ref, peers, 2)
    start_far(0)
    hand(2, half, half)
    start_far(1)
    for h in range(2):
        hand(h, 0, rows)
        start_plain[h]()

    def weight_term(i, carry):
        part = pl.ds(pl.multiple_of(i * TILE, TILE), TILE)
        term_ref[part, :] = dot(normed_ref[:, part], grad_ref[...], TN).astype(low)
        return carry

    normed_copy.wait()
    lax.fori_loop(0, model // TILE, weight_term, 0)
    shard_start, shard_pass, shard_finish = pair_sum(
        send, 10, place, sibling, others, lambda part: term_ref.at[part], twin_ref, total_ref, shard_take_ref, shard)
    shard_start()
    for c in range(2):
        for h in range(2):
            merge(h, c)
    shard_pass()
    partial(mine, 0, rows, keep)
    for copy in result_copies:
        copy.wait()

    def result(i, carry):
        part = pl.ds(pl.multiple_of(i * 64, 64), 64)
        value = hidden_ref[part, :]
        for k in range(4):
            value += branch_ref[k, part, :].astype(jnp.float32)
        result_ref[part, :] = value.astype(low)
        return carry

    lax.fori_loop(0, rows // 64, result, 0)
    outs = [local(8, result_ref, result_out)]
    for copy in row_copies:
        copy.wait()
    gain_grad_ref[...] = jnp.zeros_like(gain_grad_ref)

    def norm_back(i, carry):
        part = pl.ds(pl.multiple_of(i * 64, 64), 64)
        x = x_ref[part, :].astype(jnp.float32)
        inv = rms_scale(x)
        grad = own_ref[part, :] + take_ref[0, part, :].astype(jnp.float32) + take_ref[1, part, :].astype(jnp.float32)
        gain_grad_ref[0:1, :] += jnp.sum(grad * x * inv, axis=0, keepdims=True)
        scaled = grad * gains_ref[0:1, :]
        input_grad_ref[part, :] = (dh_ref[part, :] + (
            inv * scaled - x * inv**3 * jnp.mean(x * scaled, axis=-1, keepdims=True))).astype(low)
        return carry

    for h in range(2):
        finish(h)
        lax.fori_loop(h * half // 64, (h + 1) * half // 64, norm_back, 0)
        part = pl.ds(h * half, half)
        outs.append(local(9 + h, input_grad_ref.at[part], input_grad_out.at[part]))
    shard_finish(piece_ref)
    for copy in outs:
        copy.wait()


def rear(grad, normed, slab, gains, x, dh, hidden, branch, shard):
    low = jnp.bfloat16
    f32 = jnp.float32
    rows, model = x.shape
    group_len, columns = grad.shape
    count = model // shard
    shape = jax.ShapeDtypeStruct
    copies = 10 + count
    return pl.pallas_call(
        rear_kernel,
        name="rear",
        out_shape=(shape((rows, model), low), shape((rows, model), low), shape((8, model), f32),
                   shape((shard, columns), low)),
        in_specs=[vmem(), hbm(), vmem(), vmem()] + [hbm()] * 7,
        out_specs=(hbm(), hbm(), vmem(), vmem()),
        scratch_shapes=[
            pltpu.VMEM((rows, model), low),
            pltpu.VMEM((rows, model), low),
            pltpu.VMEM((group_len, model), low),
            pltpu.VMEM((rows, model), low),
            pltpu.VMEM((rows, model), f32),
            pltpu.VMEM((rows, model), f32),
            pltpu.VMEM((4, rows, model), low),
            pltpu.VMEM((3, rows, model), low),
            pltpu.VMEM((2, rows // 2, model), low),
            pltpu.VMEM((2, rows, model), low),
            pltpu.VMEM((rows, model), f32),
            pltpu.VMEM((model, columns), low),
            pltpu.VMEM((count // 2, shard, columns), low),
            pltpu.VMEM((count // 2, shard, columns), low),
            pltpu.VMEM((count // 2, shard, columns), low),
            pltpu.SemaphoreType.DMA((11,)),
            pltpu.SemaphoreType.DMA((copies,)),
            pltpu.SemaphoreType.DMA((copies,)),
        ],
        compiler_params=pltpu.CompilerParams(
            vmem_limit_bytes=62 << 20, collective_id=2, has_side_effects=True),
        cost_estimate=pl.CostEstimate(flops=50_000_000_000, bytes_accessed=20 << 20, transcendentals=0),
    )(grad, normed, slab, gains, x, dh, hidden, *branch)


def last_kernel(pieces_ref, qkv_ref, down_ref, gain_a_ref, gain_b_ref, out_qkv_ref, out_out_ref, out_gate_up_ref, out_down_ref,
                gains_ref, block_ref, slots_ref, out_own_ref, out_take_ref, out_part_ref, out_slots_ref, gain_own_ref, gain_take_ref, gain_slots_ref, local_sem, send_sem, recv_sem):
    low = jnp.bfloat16
    shard, columns = qkv_ref.shape
    model = gain_a_ref.shape[1]
    count = model // shard
    units = out_down_ref.shape[1] // 4
    width = columns // 3
    part = model // 4
    mine, peers = seq_peers()
    place, sibling, _ = shard_peers(count)
    everyone = [lax.rem(place + k, count) for k in range(1, count)]
    send = sender(send_sem, recv_sem)
    ready = greet(peers, everyone)
    local = starter(local_sem)
    fills = [local(0, qkv_ref, block_ref.at[:, :columns]), local(1, down_ref, block_ref.at[:, columns:columns + units]),
             local(2, pieces_ref.at[:, :2 * units], block_ref.at[:, columns + units:])]
    out_fill = local(3, pieces_ref.at[:, 2 * units:], out_own_ref)
    gain_own_ref[0:1, :] = gain_a_ref[0:1, :]
    gain_own_ref[1:2, :] = gain_b_ref[0:1, :]
    gain_own_ref[2:8, :] = jnp.zeros((6, model), jnp.float32)
    for copy in fills:
        copy.wait()
    ready()
    out_fill.wait()
    base = 9 + len(everyone)
    out_turn = [send(base + k, out_own_ref.at[:, span(peer, part)], out_take_ref.at[k], "seq", peer)
                for k, peer in enumerate(peers)]
    for k in (2, 0, 1):
        out_turn[k].start()
    forward, arrivals, finish = spread(send, 0, block_ref, [slots_ref.at[k] for k in range(3)], peers)
    gain_sends = [send(6 + k, gain_own_ref, gain_take_ref.at[k], "fsdp", peer) for k, peer in enumerate(everyone)]
    for copy in gain_sends:
        copy.start()

    def place_block(source, owner):
        for b in range(3):
            out_qkv_ref[:, span(b * 4 + owner, width)] = source[:, b * width:(b + 1) * width]
        out_down_ref[:, span(owner, units)] = source[:, columns:columns + units]
        at = columns + units
        for shift, size in ((0, units - TILE), (units - TILE, TILE)):
            for b in range(2):
                out_gate_up_ref[:, pl.ds(pl.multiple_of((b * 4 + owner) * units + shift, TILE), size)] = (
                    source[:, at:at + size])
                at += size

    place_block(block_ref, mine)
    value = out_own_ref[:, span(mine, part)].astype(jnp.float32)
    for k in range(3):
        out_turn[k].wait_recv()
        value += out_take_ref[k].astype(jnp.float32)
    out_part_ref[...] = value.astype(low)
    out_out_ref[:, span(mine, part)] = out_part_ref[...]
    out_sends = [send(base + 3 + k, out_part_ref, out_slots_ref.at[k], "seq", peer) for k, peer in enumerate(peers)]
    for k in (2, 0, 1):
        out_sends[k].start()
    forward()
    total = gain_own_ref[...]
    for k, copy in enumerate(gain_sends):
        copy.wait_recv()
        total += gain_take_ref[k]
    gains_ref[...] = total
    seq_sends = [send(6 + len(everyone) + k, gains_ref, gain_slots_ref.at[k], "seq", peer) for k, peer in enumerate(peers)]
    for copy in seq_sends:
        copy.start()
    for k in range(3):
        arrivals[k]()
        place_block(slots_ref.at[k], peers[k])
        out_sends[k].wait_recv()
        out_out_ref[:, span(peers[k], part)] = out_slots_ref[k]
    for copy in seq_sends:
        copy.wait()
    gains_ref[...] += gain_slots_ref[0] + gain_slots_ref[1] + gain_slots_ref[2]
    for copy in gain_sends + out_turn + out_sends:
        copy.wait_send()
    finish()


def last(pieces, qkv_piece, down_piece, gain_a, gain_b, units):
    low = jnp.bfloat16
    shard, columns = qkv_piece.shape
    model = gain_a.shape[1]
    count = model // shard
    f32 = jnp.float32
    shape = jax.ShapeDtypeStruct
    wide = columns + 3 * units
    copies = 14 + count
    return pl.pallas_call(
        last_kernel,
        name="last",
        out_shape=(
            shape((shard, 4 * columns), low),
            shape((shard, model), low),
            shape((shard, 8 * units), low),
            shape((shard, 4 * units), low),
            shape((8, model), f32),
        ),
        in_specs=[hbm()] * 3 + [vmem()] * 2,
        out_specs=(vmem(),) * 5,
        scratch_shapes=[
            pltpu.VMEM((shard, wide), low),
            pltpu.VMEM((3, shard, wide), low),
            pltpu.VMEM((shard, model), low),
            pltpu.VMEM((3, shard, model // 4), low),
            pltpu.VMEM((shard, model // 4), low),
            pltpu.VMEM((3, shard, model // 4), low),
            pltpu.VMEM((8, model), f32),
            pltpu.VMEM((count - 1, 8, model), f32),
            pltpu.VMEM((3, 8, model), f32),
            pltpu.SemaphoreType.DMA((4,)),
            pltpu.SemaphoreType.DMA((copies,)),
            pltpu.SemaphoreType.DMA((copies,)),
        ],
        compiler_params=pltpu.CompilerParams(
            vmem_limit_bytes=40 << 20, collective_id=3, has_side_effects=True),
        cost_estimate=pl.CostEstimate(flops=40_000_000_000, bytes_accessed=20 << 20, transcendentals=0),
    )(pieces, qkv_piece, down_piece, gain_a, gain_b)


def widen_kernel(*refs):
    for source, target in zip(refs[:6], refs[6:]):
        target[...] = source[...].astype(target.dtype)


def widen(shard, arrays):
    steps = max(shard // 32, 1)
    specs = [pl.BlockSpec((array.shape[0] // steps, array.shape[1]), lambda i: (i, 0)) for array in arrays]
    return pl.pallas_call(
        widen_kernel,
        name="widen",
        grid=(steps,),
        out_shape=[jax.ShapeDtypeStruct(array.shape, jnp.float32 if array.shape[0] == shard else array.dtype)
                   for array in arrays],
        in_specs=specs,
        out_specs=specs,
        compiler_params=pltpu.CompilerParams(vmem_limit_bytes=40 << 20),
    )(*arrays)


def swaps(rows):
    return [lax.ppermute(piece, "seq", table) for piece, table in zip(
        rows, ([(i, i ^ 1) for i in range(4)], [(i, (i + 2) % 4) for i in range(4)], [(i, 3 - i) for i in range(4)]))]


def on_device(block_input, norm_gain_a, weight_qkv, weight_out, norm_gain_b, weight_gate_up, weight_down,
              cotangent, permutation, lengths, offsets):
    low = jnp.bfloat16
    f32 = jnp.float32
    seq_count = lax.axis_size("seq")
    mine = lax.axis_index("seq")
    row_count, model_width = block_input.shape[1:]
    group_len = row_count * seq_count
    shard = weight_qkv.shape[0]
    head_width = weight_qkv.shape[1] // 3 // seq_count
    part_units = weight_down.shape[1] // seq_count
    perm = permutation[0]
    offs = offsets[0]
    position = jnp.arange(group_len, dtype=jnp.int32)
    start = jnp.max(jnp.where(offs[None, :] <= position[:, None], offs[None, :], 0), axis=1)

    def columns(weight, width, first, amount):
        blocks = weight.shape[1] // (seq_count * width)
        return [lax.dynamic_slice_in_dim(weight, (b * seq_count + mine) * width + first, amount, axis=1).astype(low)
                for b in range(blocks)]

    def gather_weight(parts):
        return lax.all_gather(jnp.concatenate(parts, axis=1), "fsdp", axis=0, tiled=True)

    early = part_units - TILE
    gain_cols = jnp.pad(jnp.stack([norm_gain_a, norm_gain_b], axis=1).astype(low), ((0, 0), (0, 126)))
    slab = gather_weight(columns(weight_qkv, head_width, 0, head_width) + [gain_cols])
    weights = gather_weight([weight_out.astype(low)] + columns(weight_gate_up, part_units, 0, early)
                            + columns(weight_down, part_units, 0, early))
    rows_all = gather_rows(block_input[0])
    grad_own, rows_all = lax.optimization_barrier((cotangent[0], rows_all))
    grad_rows = [cotangent[0]] + swaps([grad_own] * 3)
    ordered, dealt_out, wide_out, log_total, normed_a, gains = attention_forward(offs, rows_all, slab, perm, start)
    hidden, branch0, branch1, branch2, branch3, grads, grad_hidden, grad_heads, gain_b_term, down_piece = middle(
        dealt_out, block_input[0], weights, weight_gate_up, weight_down, gains, grad_rows, part_units)
    pieces = lax.psum_scatter(grads, "fsdp", scatter_dimension=0, tiled=True)
    branch = [branch0] + swaps([branch1, branch2, branch3])
    dealt_grad = attention_backward(offs, grad_heads, ordered, perm, start, wide_out, log_total)
    result_rows, input_grad, gain_a_term, qkv_piece = rear(
        dealt_grad, normed_a, slab, gains, block_input[0], grad_hidden, hidden, branch, shard)
    grad_qkv, grad_out, grad_gate_up, grad_down, gain_terms = last(
        pieces, qkv_piece, down_piece, gain_a_term, gain_b_term, part_units)
    gain_terms = lax.dynamic_slice_in_dim(gain_terms, lax.axis_index("fsdp") * shard, shard, axis=1)
    grad_qkv, grad_out, grad_gate_up, grad_down, result_rows, input_grad = widen(
        shard, [grad_qkv, grad_out, grad_gate_up, grad_down, result_rows, input_grad])
    return (
        result_rows[None],
        input_grad[None],
        gain_terms[0],
        grad_qkv,
        grad_out,
        gain_terms[1],
        grad_gate_up,
        grad_down,
    )


def solution(mesh):
    rows = P("fsdp", "seq", None)
    vector = P("fsdp")
    matrix = P("fsdp", None)
    return jax.shard_map(
        on_device,
        mesh=mesh,
        in_specs=(rows, vector, matrix, matrix, vector, matrix, matrix, rows, matrix, matrix, matrix),
        out_specs=(rows, rows, vector, matrix, matrix, vector, matrix, matrix),
        check_vma=False,
    )
```

```python
import jax
import jax.numpy as jnp
from jax import lax
from jax.experimental import pallas as pl
from jax.experimental.pallas import tpu as pltpu
from jax.sharding import PartitionSpec as P

HEAD_DIM = 64
BLK = 256
LOG2E = 1.4426950408889634

NT = (((1,), (1,)), ((), ()))
NN = (((1,), (0,)), ((), ()))


def dot(a, b, dims=NN):
    return lax.dot_general(a, b, dims, preferred_element_type=jnp.float32)


def first_block(offs_ref, row0):
    best = jnp.int32(0)
    for k in range(offs_ref.shape[0]):
        off = offs_ref[k]
        best = jnp.where(off <= row0, jnp.maximum(best, off), best)
    return best // BLK


def sort_rows(perm_row_ref, src_ref, dst_ref):
    group_len = src_ref.shape[0]

    def step(i, carry):
        rows = pl.ds(pl.multiple_of(i * 1024, 1024), 1024)
        pos = lax.broadcasted_iota(jnp.int32, (1024, group_len), 0) + i * 1024
        pick = (perm_row_ref[...] == pos).astype(jnp.float32).astype(jnp.bfloat16)
        dst_ref[rows, :] = dot(pick, src_ref[...]).astype(dst_ref.dtype)
        return carry

    lax.fori_loop(0, group_len // 1024, step, 0)


def deal_rows(perm_col_ref, src_ref, dst_ref, out_ref, sems):
    group_len = src_ref.shape[0]

    def copy_out(i):
        rows = pl.ds(pl.multiple_of(i * 512, 512), 512)
        return pltpu.make_async_copy(dst_ref.at[rows, :], out_ref.at[rows, :], sems.at[i])

    def step(i, carry):
        rows = pl.ds(pl.multiple_of(i * 512, 512), 512)
        pos = lax.broadcasted_iota(jnp.int32, (512, group_len), 1)
        pick = (perm_col_ref[rows, :] == pos).astype(jnp.float32).astype(jnp.bfloat16)
        dst_ref[rows, :] = dot(pick, src_ref[...]).astype(dst_ref.dtype)
        copy_out(i).start()
        return carry

    def wait(i, carry):
        copy_out(i).wait()
        return carry

    lax.fori_loop(0, group_len // 512, step, 0)
    lax.fori_loop(0, group_len // 512, wait, 0)


def allowed_block(start_ref, cols, qb, kb):
    key_pos = lax.broadcasted_iota(jnp.int32, (BLK, BLK), 0) + kb * BLK
    query_pos = lax.broadcasted_iota(jnp.int32, (BLK, BLK), 1) + qb * BLK
    return (key_pos <= query_pos) & (key_pos >= start_ref[:, cols])


def forward_kernel(offs_ref, x_ref, slab_ref, perm_row_ref, perm_col_ref, start_ref,
                   sorted_out, dealt_out, wide_out, lse_ref, normed_out, gains_ref,
                   sorted_ref, dealt_ref, wide_ref, normed_ref, qkv_ref, vt_ref, low_ref, local_sem, deal_sem):
    group_len, model = x_ref.shape
    width = qkv_ref.shape[1] // 3
    heads = width // HEAD_DIM
    scale = HEAD_DIM ** -0.5 * LOG2E

    def gain(i, carry):
        part = pl.ds(pl.multiple_of(i * 128, 128), 128)
        gains_ref[:, part] = slab_ref[part, 3 * width:].astype(jnp.float32).T[:8]
        return carry

    lax.fori_loop(0, model // 128, gain, 0)

    def project(i, carry):
        rows = pl.ds(pl.multiple_of(i * 512, 512), 512)
        for r in range(0, 512, 64):
            part = pl.ds(pl.multiple_of(i * 512 + r, 64), 64)
            x = x_ref[part, :].astype(jnp.float32)
            normed_ref[part, :] = (x * rms_scale(x) * gains_ref[0:1, :]).astype(jnp.bfloat16)
        qkv_ref[rows, :] = dot(normed_ref[rows, :], slab_ref[:, :3 * width]).astype(jnp.bfloat16)
        return carry

    lax.fori_loop(0, group_len // 512, project, 0)
    outs = [pltpu.make_async_copy(normed_ref, normed_out, local_sem.at[0])]
    outs[0].start()
    sort_rows(perm_row_ref, qkv_ref, sorted_ref)
    outs.append(pltpu.make_async_copy(sorted_ref, sorted_out, local_sem.at[1]))
    outs[1].start()

    def flip(i, carry):
        rows = pl.ds(pl.multiple_of(i * BLK, BLK), BLK)
        vt_ref[:, rows] = sorted_ref[rows, 2 * width:].T
        return carry

    lax.fori_loop(0, group_len // BLK, flip, 0)

    def query_step(qb, carry):
        qrow = pl.multiple_of(qb * BLK, BLK)
        cols = pl.ds(qrow, BLK)

        def key_step(kb, state):
            krow = pl.multiple_of(kb * BLK, BLK)
            krows = pl.ds(krow, BLK)
            allowed = allowed_block(start_ref, cols, qb, kb)
            fresh = []
            for h in range(heads):
                top, total, acc = state[3 * h: 3 * h + 3]
                hq = slice(h * HEAD_DIM, (h + 1) * HEAD_DIM)
                hk = slice(width + h * HEAD_DIM, width + (h + 1) * HEAD_DIM)
                s = dot(sorted_ref[krows, hk], sorted_ref[cols, hq], NT) * scale
                s = jnp.where(allowed, s, -1e30)
                new_top = jnp.maximum(top, jnp.max(s, axis=0, keepdims=True))
                shrink = jnp.exp2(top - new_top)
                p = jnp.exp2(s - new_top)
                total = total * shrink + jnp.sum(p, axis=0, keepdims=True)
                acc = acc * shrink + dot(vt_ref[hq, krows], p.astype(jnp.bfloat16))
                fresh += [new_top, total, acc]
            return tuple(fresh)

        init = []
        for h in range(heads):
            init += [jnp.full((1, BLK), -1e30, jnp.float32), jnp.zeros((1, BLK), jnp.float32),
                     jnp.zeros((HEAD_DIM, BLK), jnp.float32)]
        state = lax.fori_loop(first_block(offs_ref, qrow), qb + 1, key_step, tuple(init))
        parts = []
        for h in range(heads):
            top, total, acc = state[3 * h: 3 * h + 3]
            out = acc / total
            wide_ref[h * HEAD_DIM:(h + 1) * HEAD_DIM, cols] = out
            lse_ref[h:h + 1, cols] = top + jnp.log2(total)
            parts.append(out)
        low_ref[cols, :] = jnp.concatenate(parts, axis=0).T.astype(jnp.bfloat16)
        return carry

    lax.fori_loop(0, group_len // BLK, query_step, 0)
    outs.append(pltpu.make_async_copy(wide_ref, wide_out, local_sem.at[2]))
    outs[2].start()
    deal_rows(perm_col_ref, low_ref, dealt_ref, dealt_out, deal_sem)
    for copy in outs:
        copy.wait()


def backward_kernel(offs_ref, grad_ref, sorted_in, perm_row_ref, perm_col_ref, start_ref, wide_in, lse_ref,
                    dealt_out, sorted_ref, wide_ref, dealt_ref, do_ref, kt_ref, delta_ref, dk_ref, dv_ref, low_ref,
                    local_sem, deal_sem):
    copies = [pltpu.make_async_copy(sorted_in, sorted_ref, local_sem.at[0]),
              pltpu.make_async_copy(wide_in, wide_ref, local_sem.at[1])]
    for copy in copies:
        copy.start()
    group_len = sorted_ref.shape[0]
    width = sorted_ref.shape[1] // 3
    heads = width // HEAD_DIM
    unit = HEAD_DIM ** -0.5
    scale = unit * LOG2E
    sort_rows(perm_row_ref, grad_ref, do_ref)
    dk_ref[...] = jnp.zeros_like(dk_ref)
    dv_ref[...] = jnp.zeros_like(dv_ref)
    for copy in copies:
        copy.wait()

    def flip(i, carry):
        rows = pl.ds(pl.multiple_of(i * BLK, BLK), BLK)
        kt_ref[:, rows] = sorted_ref[rows, width: 2 * width].T
        product = do_ref[rows, :].astype(jnp.float32).T * wide_ref[:, rows]
        for h in range(heads):
            delta_ref[h:h + 1, rows] = jnp.sum(product[h * HEAD_DIM:(h + 1) * HEAD_DIM], axis=0, keepdims=True)
        return carry

    lax.fori_loop(0, group_len // BLK, flip, 0)

    def query_step(qb, carry):
        qrow = pl.multiple_of(qb * BLK, BLK)
        cols = pl.ds(qrow, BLK)

        def key_step(kb, state):
            krow = pl.multiple_of(kb * BLK, BLK)
            krows = pl.ds(krow, BLK)
            allowed = allowed_block(start_ref, cols, qb, kb)
            fresh = []
            for h in range(heads):
                hq = slice(h * HEAD_DIM, (h + 1) * HEAD_DIM)
                hk = slice(width + h * HEAD_DIM, width + (h + 1) * HEAD_DIM)
                hv = slice(2 * width + h * HEAD_DIM, 2 * width + (h + 1) * HEAD_DIM)
                q = sorted_ref[cols, hq]
                do = do_ref[cols, hq]
                s = dot(sorted_ref[krows, hk], q, NT) * scale
                s = jnp.where(allowed, s, -1e30)
                p = jnp.exp2(s - lse_ref[h:h + 1, cols])
                dp = dot(sorted_ref[krows, hv], do, NT)
                ds = (p * (dp - delta_ref[h:h + 1, cols])).astype(jnp.bfloat16)
                dv_ref[krows, hq] += dot(p.astype(jnp.bfloat16), do)
                dk_ref[krows, hq] += dot(ds, q)
                fresh.append(state[h] + dot(kt_ref[hq, krows], ds))
            return tuple(fresh)

        state = lax.fori_loop(first_block(offs_ref, qrow), qb + 1, key_step,
                              tuple(jnp.zeros((HEAD_DIM, BLK), jnp.float32) for _ in range(heads)))
        low_ref[cols, :width] = (jnp.concatenate(state, axis=0) * unit).T.astype(jnp.bfloat16)
        return carry

    lax.fori_loop(0, group_len // BLK, query_step, 0)
    low_ref[:, width:2 * width] = (dk_ref[...] * unit).astype(jnp.bfloat16)
    low_ref[:, 2 * width:] = dv_ref[...].astype(jnp.bfloat16)
    deal_rows(perm_col_ref, low_ref, dealt_ref, dealt_out, deal_sem)


def hbm():
    return pl.BlockSpec(memory_space=pltpu.HBM)


def vmem():
    return pl.BlockSpec(memory_space=pltpu.VMEM)


def attention_forward(offs, rows, slab, perm, start):
    group_len, model = rows.shape
    columns = slab.shape[1] - 128
    width = columns // 3
    shape = jax.ShapeDtypeStruct
    return pl.pallas_call(
        forward_kernel,
        name="attention_forward",
        out_shape=(
            shape((group_len, columns), jnp.bfloat16),
            shape((group_len, width), jnp.bfloat16),
            shape((width, group_len), jnp.float32),
            shape((8, group_len), jnp.float32),
            shape((group_len, model), jnp.bfloat16),
            shape((8, model), jnp.float32),
        ),
        in_specs=[pl.BlockSpec(memory_space=pltpu.SMEM)] + [vmem()] * 5,
        out_specs=(hbm(), hbm(), hbm(), vmem(), hbm(), vmem()),
        scratch_shapes=[
            pltpu.VMEM((group_len, columns), jnp.bfloat16),
            pltpu.VMEM((group_len, width), jnp.bfloat16),
            pltpu.VMEM((width, group_len), jnp.float32),
            pltpu.VMEM((group_len, model), jnp.bfloat16),
            pltpu.VMEM((group_len, columns), jnp.bfloat16),
            pltpu.VMEM((width, group_len), jnp.bfloat16),
            pltpu.VMEM((group_len, width), jnp.bfloat16),
            pltpu.SemaphoreType.DMA((3,)),
            pltpu.SemaphoreType.DMA((group_len // 512,)),
        ],
        compiler_params=pltpu.CompilerParams(vmem_limit_bytes=62 << 20),
        cost_estimate=pl.CostEstimate(flops=24_000_000_000, bytes_accessed=16 << 20, transcendentals=0),
    )(offs, rows, slab, perm.reshape(1, group_len), perm.reshape(group_len, 1), start.reshape(1, group_len))


def attention_backward(offs, grad, ordered, perm, start, wide, lse):
    group_len, columns = ordered.shape
    width = columns // 3
    return pl.pallas_call(
        backward_kernel,
        name="attention_backward",
        out_shape=jax.ShapeDtypeStruct((group_len, columns), jnp.bfloat16),
        in_specs=[pl.BlockSpec(memory_space=pltpu.SMEM), vmem(), hbm(), vmem(), vmem(), vmem(), hbm(), vmem()],
        out_specs=hbm(),
        scratch_shapes=[
            pltpu.VMEM((group_len, columns), jnp.bfloat16),
            pltpu.VMEM((width, group_len), jnp.float32),
            pltpu.VMEM((group_len, columns), jnp.bfloat16),
            pltpu.VMEM((group_len, width), jnp.bfloat16),
            pltpu.VMEM((width, group_len), jnp.bfloat16),
            pltpu.VMEM((8, group_len), jnp.float32),
            pltpu.VMEM((group_len, width), jnp.float32),
            pltpu.VMEM((group_len, width), jnp.float32),
            pltpu.VMEM((group_len, columns), jnp.bfloat16),
            pltpu.SemaphoreType.DMA((2,)),
            pltpu.SemaphoreType.DMA((group_len // 512,)),
        ],
        compiler_params=pltpu.CompilerParams(vmem_limit_bytes=62 << 20),
        cost_estimate=pl.CostEstimate(flops=40_000_000_000, bytes_accessed=16 << 20, transcendentals=0),
    )(offs, grad, ordered, perm.reshape(1, group_len), perm.reshape(group_len, 1), start.reshape(1, group_len), wide, lse)


epsilon = 1e-05


def rms_scale(values):
    return lax.rsqrt(jnp.mean(values * values, axis=-1, keepdims=True) + epsilon)


MESH = pl.DeviceIdType.MESH
TN = (((0,), (0,)), ((), ()))
TILE = 256


def seq_peers():
    mine = lax.axis_index("seq")
    return mine, (mine + 1 - 2 * lax.rem(mine, 2), lax.rem(mine + 2, 4), 3 - mine)


def greet(peers, others=()):
    barrier = pltpu.get_barrier_semaphore()
    for peer in others:
        pl.semaphore_signal(barrier, inc=1, device_id={"fsdp": peer}, device_id_type=MESH)
    for peer in peers:
        pl.semaphore_signal(barrier, inc=1, device_id={"seq": peer}, device_id_type=MESH)
    return lambda: pl.semaphore_wait(barrier, len(peers) + len(others))


def span(index, size):
    return pl.ds(pl.multiple_of(index * size, size), size)


def sender(send_sem, recv_sem):
    def send(index, src, dst, axis, peer):
        return pltpu.make_async_remote_copy(
            src_ref=src, dst_ref=dst, send_sem=send_sem.at[index], recv_sem=recv_sem.at[index],
            device_id={axis: peer}, device_id_type=MESH)
    return send


def shard_peers(count):
    mine = lax.axis_index("fsdp")
    sibling = mine + 1 - 2 * lax.rem(mine, 2)
    return mine, sibling, [lax.rem(mine + 2 * k, count) for k in range(1, count // 2)]


def starter(local_sem):
    def local(index, src, dst):
        copy = pltpu.make_async_copy(src, dst, local_sem.at[index])
        copy.start()
        return copy
    return local


def pair_sum(send, base, place, sibling, others, source, twin, total, take, shard):
    count = 2 * (len(others) + 1)
    twins = [send(base + k, source(span(lax.rem(sibling + 2 * k, count), shard)), twin.at[k], "fsdp", sibling)
             for k in range(count // 2)]
    direct = [send(base + count // 2 + k, total.at[k], take.at[k], "fsdp", others[k - 1]) for k in range(1, count // 2)]

    def start():
        for copy in twins:
            copy.start()

    def pass_on():
        for k in range(1, count // 2) :
            twins[k].wait_recv()
            total[k] = (source(span(lax.rem(place + 2 * k, count), shard))[...].astype(jnp.float32)
                        + twin[k].astype(jnp.float32)).astype(jnp.bfloat16)
            direct[k - 1].start()

    def finish(out_ref):
        twins[0].wait_recv()
        value = source(span(place, shard))[...].astype(jnp.float32) + twin[0].astype(jnp.float32)
        for k in range(1, count // 2):
            direct[k - 1].wait()
            value += take[k].astype(jnp.float32)
        out_ref[...] = value.astype(jnp.bfloat16)
        for copy in twins:
            copy.wait_send()

    return start, pass_on, finish


def spread(send, base, own, slots, peers):
    px, py, _ = peers
    half = own.shape[0] // 2
    top, bottom = pl.ds(0, half), pl.ds(half, half)
    x_slot, y_slot, far_slot = slots
    x_top = send(base, own.at[top], x_slot.at[top], "seq", px)
    y_bottom = send(base + 1, own.at[bottom], y_slot.at[bottom], "seq", py)
    x_bottom = send(base + 2, own.at[bottom], x_slot.at[bottom], "seq", px)
    y_top = send(base + 3, own.at[top], y_slot.at[top], "seq", py)
    x_relay = send(base + 4, x_slot.at[top], far_slot.at[top], "seq", py)
    y_relay = send(base + 5, y_slot.at[bottom], far_slot.at[bottom], "seq", px)
    for copy in (x_top, y_bottom, x_bottom, y_top):
        copy.start()

    def forward():
        x_top.wait_recv()
        x_relay.start()
        y_bottom.wait_recv()
        y_relay.start()

    def finish():
        for copy in (x_top, y_bottom, x_bottom, y_top, x_relay, y_relay):
            copy.wait_send()

    return forward, (x_bottom.wait_recv, y_top.wait_recv, lambda: (x_relay.wait_recv(), y_relay.wait_recv())), finish


def collect(send, base, give, transit, take, peers, cut):
    px, py, _ = peers
    half = give.shape[1] // 2
    size = half // cut
    halves = (pl.ds(0, half), pl.ds(half, half))
    pieces = [[pl.ds(h * half + c * size, size) for c in range(cut)] for h in range(2)]
    first, second = (px, py), (py, px)
    far = [[send(base + h * cut + c, give.at[2, pieces[h][c]], transit.at[h, pl.ds(c * size, size)], "seq", first[h])
            for c in range(cut)] for h in range(2)]
    plain = [send(base + 2 * cut + h, give.at[h, halves[h]], take.at[h, halves[h]], "seq", first[h]) for h in range(2)]
    summed = [[send(base + 2 * cut + 2 + h * cut + c, give.at[1 - h, pieces[h][c]], take.at[1 - h, pieces[h][c]],
                    "seq", second[h]) for c in range(cut)] for h in range(2)]

    def start_far(h):
        for copy in far[h]:
            copy.start()

    def merge(h, c):
        far[h][c].wait_recv()

        def step(i, carry):
            rows = pl.ds(pl.multiple_of(h * half + c * size + i * 64, 64), 64)
            more = pl.ds(pl.multiple_of(c * size + i * 64, 64), 64)
            give[1 - h, rows, :] = (give[1 - h, rows, :].astype(jnp.float32)
                                    + transit[h, more, :].astype(jnp.float32)).astype(jnp.bfloat16)
            return carry

        lax.fori_loop(0, size // 64, step, 0)
        summed[h][c].start()

    def finish(h):
        plain[h].wait()
        for c in range(cut):
            summed[h][c].wait()
            far[h][c].wait_send()

    return start_far, (plain[0].start, plain[1].start), merge, finish


def middle_kernel(out_ref, x_ref, weight_in, gate_up_in, down_in, gains_ref, dy0_in, dy1_in, dy2_in, dy3_in,
                  hidden_out, branch0_out, branch1_out, branch2_out, branch3_out, grads_out, dh_out,
                  do_ref, gain_grad_ref, down_piece_ref,
                  raw_ref, tail_in, weight_ref, dy_ref, hidden_ref, branch_ref, grads_ref, mixed_ref, normed_ref, act_ref, dgu_ref,
                  give_ref, transit_ref, take_ref, own_ref, low_ref, do_give_ref, twin_ref, total_ref, shard_take_ref,
                  local_sem, send_sem, recv_sem):
    low = jnp.bfloat16
    rows, model = x_ref.shape
    width = out_ref.shape[1]
    units = act_ref.shape[2]
    early = units - TILE
    tail_at = model + 3 * early
    shard = tail_in.shape[0]
    count = model // shard
    mine, peers = seq_peers()
    px, py, _ = peers
    place, sibling, others = shard_peers(count)
    half = rows // 2
    halves = (pl.ds(0, half), pl.ds(half, half))
    whole = pl.ds(0, rows)
    send = sender(send_sem, recv_sem)
    local = starter(local_sem)
    branch_outs = (branch0_out, branch1_out, branch2_out, branch3_out)
    out_in = local(0, weight_in.at[:, :model], weight_ref.at[:, :model])
    feed_in = [local(1, weight_in.at[:, model:], weight_ref.at[:, model:tail_at])]
    feed_in += [local(2 + k, dy_in, dy_ref.at[k]) for k, dy_in in enumerate((dy0_in, dy1_in, dy2_in, dy3_in))]

    def tiles(amount, body, first=0):
        def step(i, carry):
            body(pl.multiple_of(i * TILE, TILE))
            return carry
        lax.fori_loop(first, first + amount // TILE, step, 0)

    def half_of(owner, h):
        return pl.ds(pl.multiple_of(owner * rows + h * half, half), half)

    ready = greet(peers, [sibling] + others)
    raw = [local(14 + b, weight.at[:, pl.ds(pl.multiple_of(at * units + early, TILE), TILE)],
                 raw_ref.at[:, pl.ds(b * TILE, TILE)])
           for b, (weight, at) in enumerate(((gate_up_in, mine), (gate_up_in, 4 + mine), (down_in, mine)))]
    for copy in raw:
        copy.wait()
    tail_in[...] = raw_ref[...].astype(low)
    mixed_ref[:, span(mine, width)] = out_ref[span(mine, rows), :]
    tail_ref = weight_ref.at[span(place, shard), tail_at:]
    tail_ref[...] = tail_in[...]
    ready()
    turn = [[send(3 * h + k, out_ref.at[half_of(peer, h), :], mixed_ref.at[halves[h], span(mine, width)], "seq", peer)
             for k, peer in enumerate(peers)] for h in range(2)]
    for h in range(2):
        for k in (2, 0, 1):
            turn[h][k].start()

    def tail_of(owner):
        return weight_ref.at[span(owner, shard), tail_at:]

    tails = [send(28 + k, tail_in, tail_of(place), "fsdp", peer) for k, peer in enumerate([sibling] + others)]
    for k in list(range(1, len(tails))) + [0]:
        tails[k].start()
    parts = [tail_of(lax.rem(place - 2 * k + count, count)) for k in range(1, len(tails))]
    twins = [send(29 + count // 2 + k, part, part, "fsdp", sibling) for k, part in enumerate(parts)]

    def pass_tail(k):
        tails[k].wait_recv()
        twins[k - 1].start()

    steps = [range(1 + (len(others) * t) // 3, 1 + (len(others) * (t + 1)) // 3) for t in range(3)]
    for copy in feed_in:
        copy.wait()

    def grad_act(down_at, dup_at):
        def step(slot, carry):
            dgu_ref[slot, :, pl.ds(dup_at, TILE)] = dot(dy_ref[slot], weight_ref[:, pl.ds(down_at, TILE)]).astype(low)
            return carry
        lax.fori_loop(0, 4, step, 0)

    tiles(early, lambda f: grad_act(model + 2 * early + f, early + f))
    x_sends = [send(6 + h, normed_ref.at[0, halves[h]], normed_ref.at[1, halves[h]], "seq", px) for h in range(2)]
    y_sends = [send(8 + h, normed_ref.at[0, halves[h]], normed_ref.at[2, halves[h]], "seq", py) for h in range(2)]
    x_relay = send(10, normed_ref.at[1, halves[0]], normed_ref.at[3, halves[0]], "seq", py)
    y_relay = send(11, normed_ref.at[2, halves[1]], normed_ref.at[3, halves[1]], "seq", px)
    for h in range(2):
        for k in range(3):
            turn[h][k].wait_recv()
        if h == 0:
            out_in.wait()

        def project(c, h=h):
            cols = pl.ds(c, TILE)
            hidden_ref[halves[h], cols] = x_ref[halves[h], cols].astype(jnp.float32) + dot(
                mixed_ref[halves[h], :], weight_ref[:, cols])

        tiles(model, project)

        def norm(i, carry, h=h):
            part = pl.ds(pl.multiple_of(h * half + i * 64, 64), 64)
            value = hidden_ref[part, :]
            normed_ref[0, part, :] = (value * rms_scale(value) * gains_ref[1:2, :]).astype(low)
            return carry

        lax.fori_loop(0, half // 64, norm, 0)
        x_sends[h].start()
        y_sends[h].start()
        for k in steps[h]:
            pass_tail(k)

    def unit_tile(slot, part, gate_at, up_at, act_at, dgate_at, dup_at):
        gate = dot(normed_ref[slot, part, :], weight_ref[:, pl.ds(gate_at, TILE)])
        up = dot(normed_ref[slot, part, :], weight_ref[:, pl.ds(up_at, TILE)])
        grad_act = dgu_ref[slot, part, pl.ds(dup_at, TILE)].astype(jnp.float32)
        sigmoid = jax.nn.sigmoid(gate)
        silu = gate * sigmoid
        act_ref[slot, part, pl.ds(act_at, TILE)] = (silu * up).astype(low)
        dgu_ref[slot, part, pl.ds(dgate_at, TILE)] = (
            grad_act * up * sigmoid * (1.0 + gate * (1.0 - sigmoid))).astype(low)
        dgu_ref[slot, part, pl.ds(dup_at, TILE)] = (grad_act * silu).astype(low)

    def feed(slot, part):
        def step(i, carry):
            is_tail = (i * TILE == early).astype(jnp.int32)
            f = i * TILE

            def at(usual, last):
                return pl.multiple_of(usual + is_tail * (last - usual), TILE)

            unit_tile(slot, part, at(model + f, tail_at), at(model + early + f, tail_at + TILE),
                      pl.multiple_of(f, TILE), at(f, 2 * early),
                      at(early + f, 2 * early + TILE))
            return carry
        lax.fori_loop(0, units // TILE, step, 0)

    def back(slot, part):
        def body(c):
            cols = pl.ds(c, TILE)
            value = dot(dgu_ref[slot, part, :2 * early], weight_ref[cols, model:model + 2 * early], NT) + dot(
                dgu_ref[slot, part, 2 * early:], weight_ref[cols, tail_at:tail_at + 2 * TILE], NT)

            if isinstance(slot, int):
                own_ref[part, cols] = value
            else:
                give_ref[slot - 1, part, cols] = value.astype(low)
        tiles(model, body)

    start_far, start_plain, merge, finish = collect(send, 12, give_ref, transit_ref, take_ref, peers, 2)
    outs = [local(6, hidden_ref, hidden_out)]
    for k in steps[2]:
        pass_tail(k)
    tails[0].wait_recv()
    for copy in twins:
        copy.wait_recv()
    grad_act(tail_at + 2 * TILE, 2 * early + TILE)
    unit_count = units // TILE

    def branch(i, carry):
        cols = pl.ds(pl.multiple_of(i % (model // TILE) * TILE, TILE), TILE)
        slot = i // (model // TILE)
        branch_ref[slot, :, cols] = (
            dot(act_ref[slot, :, :early], weight_ref[cols, model + 2 * early:tail_at], NT)
            + dot(act_ref[slot, :, early:], weight_ref[cols, tail_at + 2 * TILE:], NT)).astype(low)
        for k in range(4):
            @pl.when(i == (k + 1) * (model // TILE) - 1)
            def _():
                branch_copies[k].start()
        return carry

    branch_copies = [pltpu.make_async_copy(branch_ref.at[k], branch_outs[k], local_sem.at[(7, 10, 11, 12)[k]])
                     for k in range(4)]

    def work(i, carry):
        def flag(test):
            return test.astype(jnp.int32)

        slot = flag(i >= 2) + flag((i == 3) | (i == 4)) + 2 * flag(i >= 6)
        h = flag((i == 1) | (i == 4) | (i == 5) | (i == 7))
        part = pl.ds(pl.multiple_of(h * half, half), half)

        def on(index, *actions):
            @pl.when(i == index)
            def _():
                for action in actions:
                    action()

        on(2, x_sends[0].wait_recv, x_relay.start)
        on(3, y_sends[0].wait_recv)
        on(4, y_sends[1].wait_recv, y_relay.start)
        on(5, x_sends[1].wait_recv)
        @pl.when(i == 6)
        def _():
            lax.fori_loop(0, 2 * (model // TILE), branch, 0)

        on(6, x_relay.wait_recv)
        on(7, y_relay.wait_recv)
        feed(slot, part)
        back(slot, part)
        on(2, start_plain[0])
        on(4, start_plain[1])
        on(6, lambda: start_far(0))
        on(7, lambda: start_far(1))
        return carry

    feed(0, whole)
    back(0, whole)
    lax.fori_loop(2, 8, work, 0)

    def weight_grad(left_ref, right_ref, base, first, amount):
        def step(i, carry):
            part = pl.ds(pl.multiple_of(i % 2 * (model // 2), model // 2), model // 2)
            f = pl.multiple_of(i // 2 * TILE, TILE)
            acc = dot(left_ref[0, :, part], right_ref[0, :, pl.ds(f, TILE)], TN)
            for slot in range(1, 4):
                acc += dot(left_ref[slot, :, part], right_ref[slot, :, pl.ds(f, TILE)], TN)
            grads_ref[part, pl.ds(base + f, TILE)] = acc.astype(low)
            return carry
        lax.fori_loop(2 * first, 2 * (first + amount), step, 0)

    def gate_up_grad(first, amount):
        weight_grad(normed_ref, dgu_ref, 0, first, amount)

    down_cols = pl.ds(2 * units, units)

    shard_start, shard_pass, shard_finish = pair_sum(
        send, 28 + count, place, sibling, others, lambda part: grads_ref.at[part, down_cols],
        twin_ref, total_ref, shard_take_ref, shard)
    weight_grad(dy_ref, act_ref, 2 * units, 0, 2)
    merge(0, 0)
    merge(1, 0)
    weight_grad(dy_ref, act_ref, 2 * units, 2, unit_count - 2)
    merge(0, 1)
    merge(1, 1)
    shard_start()
    gate_up_grad(0, 5)
    shard_pass()
    gain_grad_ref[...] = jnp.zeros_like(gain_grad_ref)
    sends = [[send(22 + 3 * h + k, do_give_ref.at[k, halves[h]], do_ref.at[half_of(mine, h), :], "seq", peer)
              for k, peer in enumerate(peers)] for h in range(2)]
    for h in range(2):
        finish(h)

        def norm_back(i, carry, h=h):
            part = pl.ds(pl.multiple_of(h * half + i * 64, 64), 64)
            value = hidden_ref[part, :]
            inv = rms_scale(value)
            grad = own_ref[part, :] + take_ref[0, part, :].astype(jnp.float32) + take_ref[1, part, :].astype(jnp.float32)
            gain_grad_ref[0:1, :] += jnp.sum(grad * value * inv, axis=0, keepdims=True)
            scaled = grad * gains_ref[1:2, :]
            dh = dy_ref[0, part, :].astype(jnp.float32) + (
                inv * scaled - value * inv**3 * jnp.mean(value * scaled, axis=-1, keepdims=True))
            own_ref[part, :] = dh
            low_ref[part, :] = dh.astype(low)
            return carry

        lax.fori_loop(0, half // 64, norm_back, 0)
        for k in (2, 0, 1):
            do_give_ref[k, halves[h], :] = dot(
                low_ref[halves[h], :], weight_ref[span(peers[k], width), :model], NT).astype(low)
            sends[h][k].start()
        do_ref[half_of(mine, h), :] = dot(low_ref[halves[h], :], weight_ref[span(mine, width), :model], NT).astype(low)
    outs.append(local(8, own_ref, dh_out))
    gate_up_grad(5, 2 * units // TILE - 5)
    outs.append(local(9, grads_ref.at[:, :2 * units], grads_out.at[:, :2 * units]))

    def out_grad(c):
        cols = pl.ds(c, TILE)
        grads_ref[:, pl.ds(3 * units + c, TILE)] = dot(mixed_ref[...], low_ref[:, cols], TN).astype(low)

    tiles(model, out_grad)
    outs.append(local(13, grads_ref.at[:, 3 * units:], grads_out.at[:, 2 * units:]))

    lax.fori_loop(2 * (model // TILE), 4 * (model // TILE), branch, 0)
    outs += branch_copies
    shard_finish(down_piece_ref)
    for copy in outs:
        copy.wait()
    for copy in tails + twins:
        copy.wait_send()
    for h in range(2):
        x_sends[h].wait_send()
        y_sends[h].wait_send()
        for k in range(3):
            turn[h][k].wait_send()
            sends[h][k].wait()
    x_relay.wait_send()
    y_relay.wait_send()


def middle(dealt_out, x, weights, gate_up, down, gains, dy, units):
    low = jnp.bfloat16
    group_len, width = dealt_out.shape
    rows, model = x.shape
    shard = down.shape[0]
    count = model // shard
    f32 = jnp.float32
    shape = jax.ShapeDtypeStruct
    copies = 28 + 2 * count
    return pl.pallas_call(
        middle_kernel,
        name="middle",
        out_shape=(
            shape((rows, model), f32),
            *[shape((rows, model), low)] * 4,
            shape((model, 2 * units + model), low),
            shape((rows, model), f32),
            shape((group_len, width), low),
            shape((8, model), f32),
            shape((shard, units), low),
        ),
        in_specs=[vmem(), vmem(), hbm(), hbm(), hbm(), vmem()] + [hbm()] * 4,
        out_specs=(hbm(),) * 7 + (vmem(),) * 3,
        scratch_shapes=[
            pltpu.VMEM((shard, 3 * TILE), f32),
            pltpu.VMEM((shard, 3 * TILE), low),
            pltpu.VMEM((model, model + 3 * units), low),
            pltpu.VMEM((4, rows, model), low),
            pltpu.VMEM((rows, model), f32),
            pltpu.VMEM((4, rows, model), low),
            pltpu.VMEM((model, 3 * units + model), low),
            pltpu.VMEM((rows, model), low),
            pltpu.VMEM((4, rows, model), low),
            pltpu.VMEM((4, rows, units), low),
            pltpu.VMEM((4, rows, 2 * units), low),
            pltpu.VMEM((3, rows, model), low),
            pltpu.VMEM((2, rows // 2, model), low),
            pltpu.VMEM((2, rows, model), low),
            pltpu.VMEM((rows, model), f32),
            pltpu.VMEM((rows, model), low),
            pltpu.VMEM((3, rows, width), low),
            pltpu.VMEM((count // 2, shard, units), low),
            pltpu.VMEM((count // 2, shard, units), low),
            pltpu.VMEM((count // 2, shard, units), low),
            pltpu.SemaphoreType.DMA((17,)),
            pltpu.SemaphoreType.DMA((copies,)),
            pltpu.SemaphoreType.DMA((copies,)),
        ],
        compiler_params=pltpu.CompilerParams(
            vmem_limit_bytes=62 << 20, collective_id=1, has_side_effects=True),
        cost_estimate=pl.CostEstimate(flops=60_000_000_000, bytes_accessed=40 << 20, transcendentals=0),
    )(dealt_out, x, weights, gate_up, down, gains, *dy)


def gather_kernel(x_ref, all_ref, local_sem, send_sem, recv_sem):
    rows = x_ref.shape[0]
    mine, peers = seq_peers()
    send = sender(send_sem, recv_sem)
    half = rows // 2
    px, py, _ = peers

    def part(owner, h):
        return all_ref.at[pl.ds(pl.multiple_of(owner * rows + h * half, half), half)]

    ready = greet(peers)
    keep = pltpu.make_async_copy(x_ref, all_ref.at[span(mine, rows)], local_sem)
    keep.start()
    ready()
    x_sends = [send(h, x_ref.at[pl.ds(h * half, half)], part(mine, h), "seq", px) for h in range(2)]
    y_sends = [send(2 + h, x_ref.at[pl.ds(h * half, half)], part(mine, h), "seq", py) for h in range(2)]
    for copy in (x_sends[0], y_sends[1], x_sends[1], y_sends[0]):
        copy.start()
    x_relay = send(4, part(px, 0), part(px, 0), "seq", py)
    y_relay = send(5, part(py, 1), part(py, 1), "seq", px)
    x_sends[0].wait_recv()
    x_relay.start()
    y_sends[1].wait_recv()
    y_relay.start()
    x_sends[1].wait_recv()
    y_sends[0].wait_recv()
    for copy in x_sends + y_sends:
        copy.wait_send()
    x_relay.wait()
    y_relay.wait()
    keep.wait()


def gather_rows(x):
    rows, model = x.shape
    return pl.pallas_call(
        gather_kernel,
        name="gather_rows",
        out_shape=jax.ShapeDtypeStruct((4 * rows, model), x.dtype),
        in_specs=[hbm()],
        out_specs=hbm(),
        scratch_shapes=[
            pltpu.SemaphoreType.DMA,
            pltpu.SemaphoreType.DMA((6,)),
            pltpu.SemaphoreType.DMA((6,)),
        ],
        compiler_params=pltpu.CompilerParams(collective_id=0, has_side_effects=True),
        cost_estimate=pl.CostEstimate(flops=40_000_000_000, bytes_accessed=20 << 20, transcendentals=0),
    )(x)


def rear_kernel(grad_in, normed_in, slab_in, gains_ref, x_in, dh_in, hidden_in, branch0_in, branch1_in, branch2_in,
                branch3_in, result_out, input_grad_out, gain_grad_ref, piece_ref,
                grad_ref, slab_ref, result_ref, input_grad_ref, normed_ref, x_ref, dh_ref, hidden_ref, branch_ref, give_ref, transit_ref, take_ref, own_ref, term_ref,
                twin_ref, total_ref, shard_take_ref, local_sem, send_sem, recv_sem):
    low = jnp.bfloat16
    rows, model = result_ref.shape
    shard, columns = piece_ref.shape
    count = model // shard
    half = rows // 2
    mine, peers = seq_peers()
    place, sibling, others = shard_peers(count)
    send = sender(send_sem, recv_sem)
    local = starter(local_sem)
    ready = greet(peers, [sibling] + others)
    first_copies = [local(11, slab_in, slab_ref), local(12, grad_in, grad_ref)]
    normed_copy = local(0, normed_in, normed_ref)
    row_copies = [local(1, x_in, x_ref), local(2, dh_in, dh_ref)]
    result_copies = [local(3, hidden_in, hidden_ref)]
    result_copies += [local(4 + k, piece, branch_ref.at[k])
                      for k, piece in enumerate((branch0_in, branch1_in, branch2_in, branch3_in))]

    def partial(owner, first, amount, store):
        block = pl.ds(pl.multiple_of(owner * rows + first, half), amount)

        def body(i, carry):
            cols = pl.ds(pl.multiple_of(i * TILE, TILE), TILE)
            store(cols, dot(grad_ref[block, :], slab_ref[cols, :columns], NT))
            return carry

        lax.fori_loop(0, model // TILE, body, 0)

    def hand(k, first, amount):
        def store(cols, value):
            give_ref[k, pl.ds(first, amount), cols] = value.astype(low)
        partial(peers[k], first, amount, store)

    def keep(cols, value):
        own_ref[:, cols] = value

    for copy in first_copies:
        copy.wait()
    hand(2, 0, half)
    ready()
    start_far, start_plain, merge, finish = collect(send, 0, give_ref, transit_ref, take_ref, peers, 2)
    start_far(0)
    hand(2, half, half)
    start_far(1)
    for h in range(2):
        hand(h, 0, rows)
        start_plain[h]()

    def weight_term(i, carry):
        part = pl.ds(pl.multiple_of(i * TILE, TILE), TILE)
        term_ref[part, :] = dot(normed_ref[:, part], grad_ref[...], TN).astype(low)
        return carry

    normed_copy.wait()
    lax.fori_loop(0, model // TILE, weight_term, 0)
    shard_start, shard_pass, shard_finish = pair_sum(
        send, 10, place, sibling, others, lambda part: term_ref.at[part], twin_ref, total_ref, shard_take_ref, shard)
    shard_start()
    for c in range(2):
        for h in range(2):
            merge(h, c)
    shard_pass()
    partial(mine, 0, rows, keep)
    for copy in result_copies:
        copy.wait()

    def result(i, carry):
        part = pl.ds(pl.multiple_of(i * 64, 64), 64)
        value = hidden_ref[part, :]
        for k in range(4):
            value += branch_ref[k, part, :].astype(jnp.float32)
        result_ref[part, :] = value.astype(low)
        return carry

    lax.fori_loop(0, rows // 64, result, 0)
    outs = [local(8, result_ref, result_out)]
    for copy in row_copies:
        copy.wait()
    gain_grad_ref[...] = jnp.zeros_like(gain_grad_ref)

    def norm_back(i, carry):
        part = pl.ds(pl.multiple_of(i * 64, 64), 64)
        x = x_ref[part, :].astype(jnp.float32)
        inv = rms_scale(x)
        grad = own_ref[part, :] + take_ref[0, part, :].astype(jnp.float32) + take_ref[1, part, :].astype(jnp.float32)
        gain_grad_ref[0:1, :] += jnp.sum(grad * x * inv, axis=0, keepdims=True)
        scaled = grad * gains_ref[0:1, :]
        input_grad_ref[part, :] = (dh_ref[part, :] + (
            inv * scaled - x * inv**3 * jnp.mean(x * scaled, axis=-1, keepdims=True))).astype(low)
        return carry

    for h in range(2):
        finish(h)
        lax.fori_loop(h * half // 64, (h + 1) * half // 64, norm_back, 0)
        part = pl.ds(h * half, half)
        outs.append(local(9 + h, input_grad_ref.at[part], input_grad_out.at[part]))
    shard_finish(piece_ref)
    for copy in outs:
        copy.wait()


def rear(grad, normed, slab, gains, x, dh, hidden, branch, shard):
    low = jnp.bfloat16
    f32 = jnp.float32
    rows, model = x.shape
    group_len, columns = grad.shape
    count = model // shard
    shape = jax.ShapeDtypeStruct
    copies = 10 + count
    return pl.pallas_call(
        rear_kernel,
        name="rear",
        out_shape=(shape((rows, model), low), shape((rows, model), low), shape((8, model), f32),
                   shape((shard, columns), low)),
        in_specs=[hbm(), hbm(), hbm(), vmem()] + [hbm()] * 7,
        out_specs=(hbm(), hbm(), vmem(), vmem()),
        scratch_shapes=[
            pltpu.VMEM((group_len, columns), low),
            pltpu.VMEM(slab.shape, low),
            pltpu.VMEM((rows, model), low),
            pltpu.VMEM((rows, model), low),
            pltpu.VMEM((group_len, model), low),
            pltpu.VMEM((rows, model), low),
            pltpu.VMEM((rows, model), f32),
            pltpu.VMEM((rows, model), f32),
            pltpu.VMEM((4, rows, model), low),
            pltpu.VMEM((3, rows, model), low),
            pltpu.VMEM((2, rows // 2, model), low),
            pltpu.VMEM((2, rows, model), low),
            pltpu.VMEM((rows, model), f32),
            pltpu.VMEM((model, columns), low),
            pltpu.VMEM((count // 2, shard, columns), low),
            pltpu.VMEM((count // 2, shard, columns), low),
            pltpu.VMEM((count // 2, shard, columns), low),
            pltpu.SemaphoreType.DMA((13,)),
            pltpu.SemaphoreType.DMA((copies,)),
            pltpu.SemaphoreType.DMA((copies,)),
        ],
        compiler_params=pltpu.CompilerParams(
            vmem_limit_bytes=62 << 20, collective_id=2, has_side_effects=True),
        cost_estimate=pl.CostEstimate(flops=50_000_000_000, bytes_accessed=20 << 20, transcendentals=0),
    )(grad, normed, slab, gains, x, dh, hidden, *branch)


def last_kernel(pieces_ref, qkv_ref, down_ref, gain_a_ref, gain_b_ref, out_qkv_ref, out_out_ref, out_gate_up_ref, out_down_ref,
                gains_ref, block_ref, slots_ref, out_own_ref, out_take_ref, out_part_ref, out_slots_ref, gain_own_ref, gain_take_ref, gain_slots_ref, local_sem, send_sem, recv_sem):
    low = jnp.bfloat16
    shard, columns = qkv_ref.shape
    model = gain_a_ref.shape[1]
    count = model // shard
    units = out_down_ref.shape[1] // 4
    width = columns // 3
    part = model // 4
    mine, peers = seq_peers()
    place, sibling, _ = shard_peers(count)
    everyone = [lax.rem(place + k, count) for k in range(1, count)]
    send = sender(send_sem, recv_sem)
    ready = greet(peers, everyone)
    local = starter(local_sem)
    fills = [local(0, qkv_ref, block_ref.at[:, :columns]), local(1, down_ref, block_ref.at[:, columns:columns + units]),
             local(2, pieces_ref.at[:, :2 * units], block_ref.at[:, columns + units:])]
    out_fill = local(3, pieces_ref.at[:, 2 * units:], out_own_ref)
    gain_own_ref[0:1, :] = gain_a_ref[0:1, :]
    gain_own_ref[1:2, :] = gain_b_ref[0:1, :]
    gain_own_ref[2:8, :] = jnp.zeros((6, model), jnp.float32)
    for copy in fills:
        copy.wait()
    ready()
    out_fill.wait()
    base = 9 + len(everyone)
    out_turn = [send(base + k, out_own_ref.at[:, span(peer, part)], out_take_ref.at[k], "seq", peer)
                for k, peer in enumerate(peers)]
    for k in (2, 0, 1):
        out_turn[k].start()
    forward, arrivals, finish = spread(send, 0, block_ref, [slots_ref.at[k] for k in range(3)], peers)
    gain_sends = [send(6 + k, gain_own_ref, gain_take_ref.at[k], "fsdp", peer) for k, peer in enumerate(everyone)]
    for copy in gain_sends:
        copy.start()

    def place_block(source, owner):
        for b in range(3):
            out_qkv_ref[:, span(b * 4 + owner, width)] = source[:, b * width:(b + 1) * width]
        out_down_ref[:, span(owner, units)] = source[:, columns:columns + units]
        at = columns + units
        for shift, size in ((0, units - TILE), (units - TILE, TILE)):
            for b in range(2):
                out_gate_up_ref[:, pl.ds(pl.multiple_of((b * 4 + owner) * units + shift, TILE), size)] = (
                    source[:, at:at + size])
                at += size

    place_block(block_ref, mine)
    value = out_own_ref[:, span(mine, part)].astype(jnp.float32)
    for k in range(3):
        out_turn[k].wait_recv()
        value += out_take_ref[k].astype(jnp.float32)
    out_part_ref[...] = value.astype(low)
    out_out_ref[:, span(mine, part)] = out_part_ref[...]
    out_sends = [send(base + 3 + k, out_part_ref, out_slots_ref.at[k], "seq", peer) for k, peer in enumerate(peers)]
    for k in (2, 0, 1):
        out_sends[k].start()
    forward()
    total = gain_own_ref[...]
    for k, copy in enumerate(gain_sends):
        copy.wait_recv()
        total += gain_take_ref[k]
    gains_ref[...] = total
    seq_sends = [send(6 + len(everyone) + k, gains_ref, gain_slots_ref.at[k], "seq", peer) for k, peer in enumerate(peers)]
    for copy in seq_sends:
        copy.start()
    for k in range(3):
        arrivals[k]()
        place_block(slots_ref.at[k], peers[k])
        out_sends[k].wait_recv()
        out_out_ref[:, span(peers[k], part)] = out_slots_ref[k]
    for copy in seq_sends:
        copy.wait()
    gains_ref[...] += gain_slots_ref[0] + gain_slots_ref[1] + gain_slots_ref[2]
    for copy in gain_sends + out_turn + out_sends:
        copy.wait_send()
    finish()


def last(pieces, qkv_piece, down_piece, gain_a, gain_b, units):
    low = jnp.bfloat16
    shard, columns = qkv_piece.shape
    model = gain_a.shape[1]
    count = model // shard
    f32 = jnp.float32
    shape = jax.ShapeDtypeStruct
    wide = columns + 3 * units
    copies = 14 + count
    return pl.pallas_call(
        last_kernel,
        name="last",
        out_shape=(
            shape((shard, 4 * columns), low),
            shape((shard, model), low),
            shape((shard, 8 * units), low),
            shape((shard, 4 * units), low),
            shape((8, model), f32),
        ),
        in_specs=[hbm()] * 3 + [vmem()] * 2,
        out_specs=(vmem(),) * 5,
        scratch_shapes=[
            pltpu.VMEM((shard, wide), low),
            pltpu.VMEM((3, shard, wide), low),
            pltpu.VMEM((shard, model), low),
            pltpu.VMEM((3, shard, model // 4), low),
            pltpu.VMEM((shard, model // 4), low),
            pltpu.VMEM((3, shard, model // 4), low),
            pltpu.VMEM((8, model), f32),
            pltpu.VMEM((count - 1, 8, model), f32),
            pltpu.VMEM((3, 8, model), f32),
            pltpu.SemaphoreType.DMA((4,)),
            pltpu.SemaphoreType.DMA((copies,)),
            pltpu.SemaphoreType.DMA((copies,)),
        ],
        compiler_params=pltpu.CompilerParams(
            vmem_limit_bytes=40 << 20, collective_id=3, has_side_effects=True),
        cost_estimate=pl.CostEstimate(flops=40_000_000_000, bytes_accessed=20 << 20, transcendentals=0),
    )(pieces, qkv_piece, down_piece, gain_a, gain_b)


def widen_kernel(*refs):
    for source, target in zip(refs[:6], refs[6:]):
        target[...] = source[...].astype(target.dtype)


def widen(shard, arrays):
    steps = max(shard // 32, 1)
    specs = [pl.BlockSpec((array.shape[0] // steps, array.shape[1]), lambda i: (i, 0)) for array in arrays]
    return pl.pallas_call(
        widen_kernel,
        name="widen",
        grid=(steps,),
        out_shape=[jax.ShapeDtypeStruct(array.shape, jnp.float32 if array.shape[0] == shard else array.dtype)
                   for array in arrays],
        in_specs=specs,
        out_specs=specs,
        compiler_params=pltpu.CompilerParams(vmem_limit_bytes=40 << 20),
    )(*arrays)


def swaps(rows):
    return [lax.ppermute(piece, "seq", table) for piece, table in zip(
        rows, ([(i, i ^ 1) for i in range(4)], [(i, (i + 2) % 4) for i in range(4)], [(i, 3 - i) for i in range(4)]))]


def on_device(block_input, norm_gain_a, weight_qkv, weight_out, norm_gain_b, weight_gate_up, weight_down,
              cotangent, permutation, lengths, offsets):
    low = jnp.bfloat16
    f32 = jnp.float32
    seq_count = lax.axis_size("seq")
    mine = lax.axis_index("seq")
    row_count, model_width = block_input.shape[1:]
    group_len = row_count * seq_count
    shard = weight_qkv.shape[0]
    head_width = weight_qkv.shape[1] // 3 // seq_count
    part_units = weight_down.shape[1] // seq_count
    perm = permutation[0]
    offs = offsets[0]
    position = jnp.arange(group_len, dtype=jnp.int32)
    start = jnp.max(jnp.where(offs[None, :] <= position[:, None], offs[None, :], 0), axis=1)

    def columns(weight, width, first, amount):
        blocks = weight.shape[1] // (seq_count * width)
        return [lax.dynamic_slice_in_dim(weight, (b * seq_count + mine) * width + first, amount, axis=1).astype(low)
                for b in range(blocks)]

    def gather_weight(parts):
        return lax.all_gather(jnp.concatenate(parts, axis=1), "fsdp", axis=0, tiled=True)

    early = part_units - TILE
    gain_cols = jnp.pad(jnp.stack([norm_gain_a, norm_gain_b], axis=1).astype(low), ((0, 0), (0, 126)))
    slab = gather_weight(columns(weight_qkv, head_width, 0, head_width) + [gain_cols])
    weights = gather_weight([weight_out.astype(low)] + columns(weight_gate_up, part_units, 0, early)
                            + columns(weight_down, part_units, 0, early))
    rows_all = gather_rows(block_input[0])
    grad_own, rows_all = lax.optimization_barrier((cotangent[0], rows_all))
    grad_rows = [cotangent[0]] + swaps([grad_own] * 3)
    ordered, dealt_out, wide_out, log_total, normed_a, gains = attention_forward(offs, rows_all, slab, perm, start)
    hidden, branch0, branch1, branch2, branch3, grads, grad_hidden, grad_heads, gain_b_term, down_piece = middle(
        dealt_out, block_input[0], weights, weight_gate_up, weight_down, gains, grad_rows, part_units)
    pieces = lax.psum_scatter(grads, "fsdp", scatter_dimension=0, tiled=True)
    branch = [branch0] + swaps([branch1, branch2, branch3])
    dealt_grad = attention_backward(offs, grad_heads, ordered, perm, start, wide_out, log_total)
    result_rows, input_grad, gain_a_term, qkv_piece = rear(
        dealt_grad, normed_a, slab, gains, block_input[0], grad_hidden, hidden, branch, shard)
    grad_qkv, grad_out, grad_gate_up, grad_down, gain_terms = last(
        pieces, qkv_piece, down_piece, gain_a_term, gain_b_term, part_units)
    gain_terms = lax.dynamic_slice_in_dim(gain_terms, lax.axis_index("fsdp") * shard, shard, axis=1)
    grad_qkv, grad_out, grad_gate_up, grad_down, result_rows, input_grad = widen(
        shard, [grad_qkv, grad_out, grad_gate_up, grad_down, result_rows, input_grad])
    return (
        result_rows[None],
        input_grad[None],
        gain_terms[0],
        grad_qkv,
        grad_out,
        gain_terms[1],
        grad_gate_up,
        grad_down,
    )


def solution(mesh):
    rows = P("fsdp", "seq", None)
    vector = P("fsdp")
    matrix = P("fsdp", None)
    return jax.shard_map(
        on_device,
        mesh=mesh,
        in_specs=(rows, vector, matrix, matrix, vector, matrix, matrix, rows, matrix, matrix, matrix),
        out_specs=(rows, rows, vector, matrix, matrix, vector, matrix, matrix),
        check_vma=False,
    )
```

```python
import jax
import jax.numpy as jnp
from jax import lax
from jax.experimental import pallas as pl
from jax.experimental.pallas import tpu as pltpu
from jax.sharding import PartitionSpec as P

HEAD_DIM = 64
BLK = 256
LOG2E = 1.4426950408889634

NT = (((1,), (1,)), ((), ()))
NN = (((1,), (0,)), ((), ()))


def dot(a, b, dims=NN):
    return lax.dot_general(a, b, dims, preferred_element_type=jnp.float32)


def first_block(offs_ref, row0):
    best = jnp.int32(0)
    for k in range(offs_ref.shape[0]):
        off = offs_ref[k]
        best = jnp.where(off <= row0, jnp.maximum(best, off), best)
    return best // BLK


def sort_rows(perm_row_ref, src_ref, dst_ref):
    group_len = src_ref.shape[0]

    def step(i, carry):
        rows = pl.ds(pl.multiple_of(i * 1024, 1024), 1024)
        pos = lax.broadcasted_iota(jnp.int32, (1024, group_len), 0) + i * 1024
        pick = (perm_row_ref[...] == pos).astype(jnp.float32).astype(jnp.bfloat16)
        dst_ref[rows, :] = dot(pick, src_ref[...]).astype(dst_ref.dtype)
        return carry

    lax.fori_loop(0, group_len // 1024, step, 0)


def deal_rows(perm_col_ref, src_ref, dst_ref, out_ref, sems):
    group_len = src_ref.shape[0]

    def copy_out(i):
        rows = pl.ds(pl.multiple_of(i * 512, 512), 512)
        return pltpu.make_async_copy(dst_ref.at[rows, :], out_ref.at[rows, :], sems.at[i])

    def step(i, carry):
        rows = pl.ds(pl.multiple_of(i * 512, 512), 512)
        pos = lax.broadcasted_iota(jnp.int32, (512, group_len), 1)
        pick = (perm_col_ref[rows, :] == pos).astype(jnp.float32).astype(jnp.bfloat16)
        dst_ref[rows, :] = dot(pick, src_ref[...]).astype(dst_ref.dtype)
        copy_out(i).start()
        return carry

    def wait(i, carry):
        copy_out(i).wait()
        return carry

    lax.fori_loop(0, group_len // 512, step, 0)
    lax.fori_loop(0, group_len // 512, wait, 0)


def allowed_block(start_ref, cols, qb, kb):
    key_pos = lax.broadcasted_iota(jnp.int32, (BLK, BLK), 0) + kb * BLK
    query_pos = lax.broadcasted_iota(jnp.int32, (BLK, BLK), 1) + qb * BLK
    return (key_pos <= query_pos) & (key_pos >= start_ref[:, cols])


def forward_kernel(offs_ref, x_ref, slab_ref, perm_row_ref, perm_col_ref, start_ref,
                   sorted_out, dealt_out, wide_out, lse_ref, normed_out, gains_ref,
                   sorted_ref, dealt_ref, wide_ref, normed_ref, qkv_ref, vt_ref, low_ref, local_sem, deal_sem):
    group_len, model = x_ref.shape
    width = qkv_ref.shape[1] // 3
    heads = width // HEAD_DIM
    scale = HEAD_DIM ** -0.5 * LOG2E

    def gain(i, carry):
        part = pl.ds(pl.multiple_of(i * 128, 128), 128)
        gains_ref[:, part] = slab_ref[part, 3 * width:].astype(jnp.float32).T[:8]
        return carry

    lax.fori_loop(0, model // 128, gain, 0)

    def project(i, carry):
        rows = pl.ds(pl.multiple_of(i * 512, 512), 512)
        for r in range(0, 512, 64):
            part = pl.ds(pl.multiple_of(i * 512 + r, 64), 64)
            x = x_ref[part, :].astype(jnp.float32)
            normed_ref[part, :] = (x * rms_scale(x) * gains_ref[0:1, :]).astype(jnp.bfloat16)
        qkv_ref[rows, :] = dot(normed_ref[rows, :], slab_ref[:, :3 * width]).astype(jnp.bfloat16)
        return carry

    lax.fori_loop(0, group_len // 512, project, 0)
    outs = [pltpu.make_async_copy(normed_ref, normed_out, local_sem.at[0])]
    outs[0].start()
    sort_rows(perm_row_ref, qkv_ref, sorted_ref)
    outs.append(pltpu.make_async_copy(sorted_ref, sorted_out, local_sem.at[1]))
    outs[1].start()

    def flip(i, carry):
        rows = pl.ds(pl.multiple_of(i * BLK, BLK), BLK)
        vt_ref[:, rows] = sorted_ref[rows, 2 * width:].T
        return carry

    lax.fori_loop(0, group_len // BLK, flip, 0)

    def query_step(qb, carry):
        qrow = pl.multiple_of(qb * BLK, BLK)
        cols = pl.ds(qrow, BLK)

        def key_step(kb, state):
            krow = pl.multiple_of(kb * BLK, BLK)
            krows = pl.ds(krow, BLK)
            allowed = allowed_block(start_ref, cols, qb, kb)
            fresh = []
            for h in range(heads):
                top, total, acc = state[3 * h: 3 * h + 3]
                hq = slice(h * HEAD_DIM, (h + 1) * HEAD_DIM)
                hk = slice(width + h * HEAD_DIM, width + (h + 1) * HEAD_DIM)
                s = dot(sorted_ref[krows, hk], sorted_ref[cols, hq], NT) * scale
                s = jnp.where(allowed, s, -1e30)
                new_top = jnp.maximum(top, jnp.max(s, axis=0, keepdims=True))
                shrink = jnp.exp2(top - new_top)
                p = jnp.exp2(s - new_top)
                total = total * shrink + jnp.sum(p, axis=0, keepdims=True)
                acc = acc * shrink + dot(vt_ref[hq, krows], p.astype(jnp.bfloat16))
                fresh += [new_top, total, acc]
            return tuple(fresh)

        init = []
        for h in range(heads):
            init += [jnp.full((1, BLK), -1e30, jnp.float32), jnp.zeros((1, BLK), jnp.float32),
                     jnp.zeros((HEAD_DIM, BLK), jnp.float32)]
        state = lax.fori_loop(first_block(offs_ref, qrow), qb + 1, key_step, tuple(init))
        parts = []
        for h in range(heads):
            top, total, acc = state[3 * h: 3 * h + 3]
            out = acc / total
            wide_ref[h * HEAD_DIM:(h + 1) * HEAD_DIM, cols] = out
            lse_ref[h:h + 1, cols] = top + jnp.log2(total)
            parts.append(out)
        low_ref[cols, :] = jnp.concatenate(parts, axis=0).T.astype(jnp.bfloat16)
        return carry

    lax.fori_loop(0, group_len // BLK, query_step, 0)
    outs.append(pltpu.make_async_copy(wide_ref, wide_out, local_sem.at[2]))
    outs[2].start()
    deal_rows(perm_col_ref, low_ref, dealt_ref, dealt_out, deal_sem)
    for copy in outs:
        copy.wait()


def backward_kernel(offs_ref, grad_ref, sorted_in, perm_row_ref, perm_col_ref, start_ref, wide_in, lse_ref,
                    dealt_out, sorted_ref, wide_ref, dealt_ref, do_ref, kt_ref, delta_ref, dk_ref, dv_ref, low_ref,
                    local_sem, deal_sem):
    copies = [pltpu.make_async_copy(sorted_in, sorted_ref, local_sem.at[0]),
              pltpu.make_async_copy(wide_in, wide_ref, local_sem.at[1])]
    for copy in copies:
        copy.start()
    group_len = sorted_ref.shape[0]
    width = sorted_ref.shape[1] // 3
    heads = width // HEAD_DIM
    unit = HEAD_DIM ** -0.5
    scale = unit * LOG2E
    sort_rows(perm_row_ref, grad_ref, do_ref)
    dk_ref[...] = jnp.zeros_like(dk_ref)
    dv_ref[...] = jnp.zeros_like(dv_ref)
    for copy in copies:
        copy.wait()

    def flip(i, carry):
        rows = pl.ds(pl.multiple_of(i * BLK, BLK), BLK)
        kt_ref[:, rows] = sorted_ref[rows, width: 2 * width].T
        product = do_ref[rows, :].astype(jnp.float32).T * wide_ref[:, rows]
        for h in range(heads):
            delta_ref[h:h + 1, rows] = jnp.sum(product[h * HEAD_DIM:(h + 1) * HEAD_DIM], axis=0, keepdims=True)
        return carry

    lax.fori_loop(0, group_len // BLK, flip, 0)

    def query_step(qb, carry):
        qrow = pl.multiple_of(qb * BLK, BLK)
        cols = pl.ds(qrow, BLK)

        def key_step(kb, state):
            krow = pl.multiple_of(kb * BLK, BLK)
            krows = pl.ds(krow, BLK)
            allowed = allowed_block(start_ref, cols, qb, kb)
            fresh = []
            for h in range(heads):
                hq = slice(h * HEAD_DIM, (h + 1) * HEAD_DIM)
                hk = slice(width + h * HEAD_DIM, width + (h + 1) * HEAD_DIM)
                hv = slice(2 * width + h * HEAD_DIM, 2 * width + (h + 1) * HEAD_DIM)
                q = sorted_ref[cols, hq]
                do = do_ref[cols, hq]
                s = dot(sorted_ref[krows, hk], q, NT) * scale
                s = jnp.where(allowed, s, -1e30)
                p = jnp.exp2(s - lse_ref[h:h + 1, cols])
                dp = dot(sorted_ref[krows, hv], do, NT)
                ds = (p * (dp - delta_ref[h:h + 1, cols])).astype(jnp.bfloat16)
                dv_ref[krows, hq] += dot(p.astype(jnp.bfloat16), do)
                dk_ref[krows, hq] += dot(ds, q)
                fresh.append(state[h] + dot(kt_ref[hq, krows], ds))
            return tuple(fresh)

        state = lax.fori_loop(first_block(offs_ref, qrow), qb + 1, key_step,
                              tuple(jnp.zeros((HEAD_DIM, BLK), jnp.float32) for _ in range(heads)))
        low_ref[cols, :width] = (jnp.concatenate(state, axis=0) * unit).T.astype(jnp.bfloat16)
        return carry

    lax.fori_loop(0, group_len // BLK, query_step, 0)
    low_ref[:, width:2 * width] = (dk_ref[...] * unit).astype(jnp.bfloat16)
    low_ref[:, 2 * width:] = dv_ref[...].astype(jnp.bfloat16)
    deal_rows(perm_col_ref, low_ref, dealt_ref, dealt_out, deal_sem)


def hbm():
    return pl.BlockSpec(memory_space=pltpu.HBM)


def vmem():
    return pl.BlockSpec(memory_space=pltpu.VMEM)


def attention_forward(offs, rows, slab, perm, start):
    group_len, model = rows.shape
    columns = slab.shape[1] - 128
    width = columns // 3
    shape = jax.ShapeDtypeStruct
    return pl.pallas_call(
        forward_kernel,
        name="attention_forward",
        out_shape=(
            shape((group_len, columns), jnp.bfloat16),
            shape((group_len, width), jnp.bfloat16),
            shape((width, group_len), jnp.float32),
            shape((8, group_len), jnp.float32),
            shape((group_len, model), jnp.bfloat16),
            shape((8, model), jnp.float32),
        ),
        in_specs=[pl.BlockSpec(memory_space=pltpu.SMEM)] + [vmem()] * 5,
        out_specs=(hbm(), hbm(), hbm(), vmem(), hbm(), vmem()),
        scratch_shapes=[
            pltpu.VMEM((group_len, columns), jnp.bfloat16),
            pltpu.VMEM((group_len, width), jnp.bfloat16),
            pltpu.VMEM((width, group_len), jnp.float32),
            pltpu.VMEM((group_len, model), jnp.bfloat16),
            pltpu.VMEM((group_len, columns), jnp.bfloat16),
            pltpu.VMEM((width, group_len), jnp.bfloat16),
            pltpu.VMEM((group_len, width), jnp.bfloat16),
            pltpu.SemaphoreType.DMA((3,)),
            pltpu.SemaphoreType.DMA((group_len // 512,)),
        ],
        compiler_params=pltpu.CompilerParams(vmem_limit_bytes=62 << 20),
        cost_estimate=pl.CostEstimate(flops=24_000_000_000, bytes_accessed=16 << 20, transcendentals=0),
    )(offs, rows, slab, perm.reshape(1, group_len), perm.reshape(group_len, 1), start.reshape(1, group_len))


def attention_backward(offs, grad, ordered, perm, start, wide, lse):
    group_len, columns = ordered.shape
    width = columns // 3
    return pl.pallas_call(
        backward_kernel,
        name="attention_backward",
        out_shape=jax.ShapeDtypeStruct((group_len, columns), jnp.bfloat16),
        in_specs=[pl.BlockSpec(memory_space=pltpu.SMEM), vmem(), hbm(), vmem(), vmem(), vmem(), hbm(), vmem()],
        out_specs=hbm(),
        scratch_shapes=[
            pltpu.VMEM((group_len, columns), jnp.bfloat16),
            pltpu.VMEM((width, group_len), jnp.float32),
            pltpu.VMEM((group_len, columns), jnp.bfloat16),
            pltpu.VMEM((group_len, width), jnp.bfloat16),
            pltpu.VMEM((width, group_len), jnp.bfloat16),
            pltpu.VMEM((8, group_len), jnp.float32),
            pltpu.VMEM((group_len, width), jnp.float32),
            pltpu.VMEM((group_len, width), jnp.float32),
            pltpu.VMEM((group_len, columns), jnp.bfloat16),
            pltpu.SemaphoreType.DMA((2,)),
            pltpu.SemaphoreType.DMA((group_len // 512,)),
        ],
        compiler_params=pltpu.CompilerParams(vmem_limit_bytes=62 << 20),
        cost_estimate=pl.CostEstimate(flops=40_000_000_000, bytes_accessed=16 << 20, transcendentals=0),
    )(offs, grad, ordered, perm.reshape(1, group_len), perm.reshape(group_len, 1), start.reshape(1, group_len), wide, lse)


epsilon = 1e-05


def rms_scale(values):
    return lax.rsqrt(jnp.mean(values * values, axis=-1, keepdims=True) + epsilon)


MESH = pl.DeviceIdType.MESH
TN = (((0,), (0,)), ((), ()))
TILE = 256


def seq_peers():
    mine = lax.axis_index("seq")
    return mine, (mine + 1 - 2 * lax.rem(mine, 2), lax.rem(mine + 2, 4), 3 - mine)


def greet(peers, others=()):
    barrier = pltpu.get_barrier_semaphore()
    for peer in others:
        pl.semaphore_signal(barrier, inc=1, device_id={"fsdp": peer}, device_id_type=MESH)
    for peer in peers:
        pl.semaphore_signal(barrier, inc=1, device_id={"seq": peer}, device_id_type=MESH)
    return lambda: pl.semaphore_wait(barrier, len(peers) + len(others))


def span(index, size):
    return pl.ds(pl.multiple_of(index * size, size), size)


def sender(send_sem, recv_sem):
    def send(index, src, dst, axis, peer):
        return pltpu.make_async_remote_copy(
            src_ref=src, dst_ref=dst, send_sem=send_sem.at[index], recv_sem=recv_sem.at[index],
            device_id={axis: peer}, device_id_type=MESH)
    return send


def shard_peers(count):
    mine = lax.axis_index("fsdp")
    sibling = mine + 1 - 2 * lax.rem(mine, 2)
    return mine, sibling, [lax.rem(mine + 2 * k, count) for k in range(1, count // 2)]


def starter(local_sem):
    def local(index, src, dst):
        copy = pltpu.make_async_copy(src, dst, local_sem.at[index])
        copy.start()
        return copy
    return local


def pair_sum(send, base, place, sibling, others, source, twin, total, take, shard):
    count = 2 * (len(others) + 1)
    twins = [send(base + k, source(span(lax.rem(sibling + 2 * k, count), shard)), twin.at[k], "fsdp", sibling)
             for k in range(count // 2)]
    direct = [send(base + count // 2 + k, total.at[k], take.at[k], "fsdp", others[k - 1]) for k in range(1, count // 2)]

    def start():
        for copy in twins:
            copy.start()

    def pass_on():
        for k in range(1, count // 2) :
            twins[k].wait_recv()
            total[k] = (source(span(lax.rem(place + 2 * k, count), shard))[...].astype(jnp.float32)
                        + twin[k].astype(jnp.float32)).astype(jnp.bfloat16)
            direct[k - 1].start()

    def finish(out_ref):
        twins[0].wait_recv()
        value = source(span(place, shard))[...].astype(jnp.float32) + twin[0].astype(jnp.float32)
        for k in range(1, count // 2):
            direct[k - 1].wait()
            value += take[k].astype(jnp.float32)
        out_ref[...] = value.astype(jnp.bfloat16)
        for copy in twins:
            copy.wait_send()

    return start, pass_on, finish


def spread(send, base, own, slots, peers):
    px, py, _ = peers
    half = own.shape[0] // 2
    top, bottom = pl.ds(0, half), pl.ds(half, half)
    x_slot, y_slot, far_slot = slots
    x_top = send(base, own.at[top], x_slot.at[top], "seq", px)
    y_bottom = send(base + 1, own.at[bottom], y_slot.at[bottom], "seq", py)
    x_bottom = send(base + 2, own.at[bottom], x_slot.at[bottom], "seq", px)
    y_top = send(base + 3, own.at[top], y_slot.at[top], "seq", py)
    x_relay = send(base + 4, x_slot.at[top], far_slot.at[top], "seq", py)
    y_relay = send(base + 5, y_slot.at[bottom], far_slot.at[bottom], "seq", px)
    for copy in (x_top, y_bottom, x_bottom, y_top):
        copy.start()

    def forward():
        x_top.wait_recv()
        x_relay.start()
        y_bottom.wait_recv()
        y_relay.start()

    def finish():
        for copy in (x_top, y_bottom, x_bottom, y_top, x_relay, y_relay):
            copy.wait_send()

    return forward, (x_bottom.wait_recv, y_top.wait_recv, lambda: (x_relay.wait_recv(), y_relay.wait_recv())), finish


def collect(send, base, give, transit, take, peers, cut):
    px, py, _ = peers
    half = give.shape[1] // 2
    size = half // cut
    halves = (pl.ds(0, half), pl.ds(half, half))
    pieces = [[pl.ds(h * half + c * size, size) for c in range(cut)] for h in range(2)]
    first, second = (px, py), (py, px)
    far = [[send(base + h * cut + c, give.at[2, pieces[h][c]], transit.at[h, pl.ds(c * size, size)], "seq", first[h])
            for c in range(cut)] for h in range(2)]
    plain = [send(base + 2 * cut + h, give.at[h, halves[h]], take.at[h, halves[h]], "seq", first[h]) for h in range(2)]
    summed = [[send(base + 2 * cut + 2 + h * cut + c, give.at[1 - h, pieces[h][c]], take.at[1 - h, pieces[h][c]],
                    "seq", second[h]) for c in range(cut)] for h in range(2)]

    def start_far(h):
        for copy in far[h]:
            copy.start()

    def merge(h, c):
        far[h][c].wait_recv()

        def step(i, carry):
            rows = pl.ds(pl.multiple_of(h * half + c * size + i * 64, 64), 64)
            more = pl.ds(pl.multiple_of(c * size + i * 64, 64), 64)
            give[1 - h, rows, :] = (give[1 - h, rows, :].astype(jnp.float32)
                                    + transit[h, more, :].astype(jnp.float32)).astype(jnp.bfloat16)
            return carry

        lax.fori_loop(0, size // 64, step, 0)
        summed[h][c].start()

    def finish(h):
        plain[h].wait()
        for c in range(cut):
            summed[h][c].wait()
            far[h][c].wait_send()

    return start_far, (plain[0].start, plain[1].start), merge, finish


def middle_kernel(out_ref, x_in, weight_in, gate_up_in, down_in, gains_ref, dy0_in, dy1_in, dy2_in, dy3_in,
                  hidden_out, branch0_out, branch1_out, branch2_out, branch3_out, grads_out, dh_out,
                  do_ref, gain_grad_ref, down_piece_ref,
                  x_ref, raw_ref, tail_in, weight_ref, dy_ref, hidden_ref, branch_ref, grads_ref, mixed_ref, normed_ref, act_ref, dgu_ref,
                  give_ref, transit_ref, take_ref, own_ref, low_ref, do_give_ref, twin_ref, total_ref, shard_take_ref,
                  local_sem, send_sem, recv_sem):
    low = jnp.bfloat16
    rows, model = x_in.shape
    width = out_ref.shape[1]
    units = act_ref.shape[2]
    early = units - TILE
    tail_at = model + 3 * early
    shard = tail_in.shape[0]
    count = model // shard
    mine, peers = seq_peers()
    px, py, _ = peers
    place, sibling, others = shard_peers(count)
    half = rows // 2
    halves = (pl.ds(0, half), pl.ds(half, half))
    whole = pl.ds(0, rows)
    send = sender(send_sem, recv_sem)
    local = starter(local_sem)
    branch_outs = (branch0_out, branch1_out, branch2_out, branch3_out)
    out_in = local(0, weight_in.at[:, :model], weight_ref.at[:, :model])
    feed_in = [local(1, weight_in.at[:, model:], weight_ref.at[:, model:tail_at])]
    feed_in += [local(2 + k, dy_in, dy_ref.at[k]) for k, dy_in in enumerate((dy0_in, dy1_in, dy2_in, dy3_in))]

    def tiles(amount, body, first=0):
        def step(i, carry):
            body(pl.multiple_of(i * TILE, TILE))
            return carry
        lax.fori_loop(first, first + amount // TILE, step, 0)

    def half_of(owner, h):
        return pl.ds(pl.multiple_of(owner * rows + h * half, half), half)

    ready = greet(peers, [sibling] + others)
    raw = [local(14 + b, weight.at[:, pl.ds(pl.multiple_of(at * units + early, TILE), TILE)],
                 raw_ref.at[:, pl.ds(b * TILE, TILE)])
           for b, (weight, at) in enumerate(((gate_up_in, mine), (gate_up_in, 4 + mine), (down_in, mine)))]
    for copy in raw:
        copy.wait()
    tail_in[...] = raw_ref[...].astype(low)
    row_in = [local(17, out_ref.at[span(mine, rows), :], mixed_ref.at[:, span(mine, width)]), local(18, x_in, x_ref)]
    tail_ref = weight_ref.at[span(place, shard), tail_at:]
    tail_ref[...] = tail_in[...]
    ready()
    turn = [[send(3 * h + k, out_ref.at[half_of(peer, h), :], mixed_ref.at[halves[h], span(mine, width)], "seq", peer)
             for k, peer in enumerate(peers)] for h in range(2)]
    for h in range(2):
        for k in (2, 0, 1):
            turn[h][k].start()

    def tail_of(owner):
        return weight_ref.at[span(owner, shard), tail_at:]

    tails = [send(28 + k, tail_in, tail_of(place), "fsdp", peer) for k, peer in enumerate([sibling] + others)]
    for k in list(range(1, len(tails))) + [0]:
        tails[k].start()
    parts = [tail_of(lax.rem(place - 2 * k + count, count)) for k in range(1, len(tails))]
    twins = [send(29 + count // 2 + k, part, part, "fsdp", sibling) for k, part in enumerate(parts)]

    def pass_tail(k):
        tails[k].wait_recv()
        twins[k - 1].start()

    steps = [range(1 + (len(others) * t) // 3, 1 + (len(others) * (t + 1)) // 3) for t in range(3)]
    for copy in feed_in:
        copy.wait()

    def grad_act(down_at, dup_at):
        def step(slot, carry):
            dgu_ref[slot, :, pl.ds(dup_at, TILE)] = dot(dy_ref[slot], weight_ref[:, pl.ds(down_at, TILE)]).astype(low)
            return carry
        lax.fori_loop(0, 4, step, 0)

    tiles(early, lambda f: grad_act(model + 2 * early + f, early + f))
    x_sends = [send(6 + h, normed_ref.at[0, halves[h]], normed_ref.at[1, halves[h]], "seq", px) for h in range(2)]
    y_sends = [send(8 + h, normed_ref.at[0, halves[h]], normed_ref.at[2, halves[h]], "seq", py) for h in range(2)]
    x_relay = send(10, normed_ref.at[1, halves[0]], normed_ref.at[3, halves[0]], "seq", py)
    y_relay = send(11, normed_ref.at[2, halves[1]], normed_ref.at[3, halves[1]], "seq", px)
    for h in range(2):
        for k in range(3):
            turn[h][k].wait_recv()
        if h == 0:
            for copy in [out_in] + row_in:
                copy.wait()

        def project(c, h=h):
            cols = pl.ds(c, TILE)
            hidden_ref[halves[h], cols] = x_ref[halves[h], cols].astype(jnp.float32) + dot(
                mixed_ref[halves[h], :], weight_ref[:, cols])

        tiles(model, project)

        def norm(i, carry, h=h):
            part = pl.ds(pl.multiple_of(h * half + i * 64, 64), 64)
            value = hidden_ref[part, :]
            normed_ref[0, part, :] = (value * rms_scale(value) * gains_ref[1:2, :]).astype(low)
            return carry

        lax.fori_loop(0, half // 64, norm, 0)
        x_sends[h].start()
        y_sends[h].start()
        for k in steps[h]:
            pass_tail(k)

    def unit_tile(slot, part, gate_at, up_at, act_at, dgate_at, dup_at):
        gate = dot(normed_ref[slot, part, :], weight_ref[:, pl.ds(gate_at, TILE)])
        up = dot(normed_ref[slot, part, :], weight_ref[:, pl.ds(up_at, TILE)])
        grad_act = dgu_ref[slot, part, pl.ds(dup_at, TILE)].astype(jnp.float32)
        sigmoid = jax.nn.sigmoid(gate)
        silu = gate * sigmoid
        act_ref[slot, part, pl.ds(act_at, TILE)] = (silu * up).astype(low)
        dgu_ref[slot, part, pl.ds(dgate_at, TILE)] = (
            grad_act * up * sigmoid * (1.0 + gate * (1.0 - sigmoid))).astype(low)
        dgu_ref[slot, part, pl.ds(dup_at, TILE)] = (grad_act * silu).astype(low)

    def feed(slot, part):
        def step(i, carry):
            is_tail = (i * TILE == early).astype(jnp.int32)
            f = i * TILE

            def at(usual, last):
                return pl.multiple_of(usual + is_tail * (last - usual), TILE)

            unit_tile(slot, part, at(model + f, tail_at), at(model + early + f, tail_at + TILE),
                      pl.multiple_of(f, TILE), at(f, 2 * early),
                      at(early + f, 2 * early + TILE))
            return carry
        lax.fori_loop(0, units // TILE, step, 0)

    def back(slot, part):
        def body(c):
            cols = pl.ds(c, TILE)
            value = dot(dgu_ref[slot, part, :2 * early], weight_ref[cols, model:model + 2 * early], NT) + dot(
                dgu_ref[slot, part, 2 * early:], weight_ref[cols, tail_at:tail_at + 2 * TILE], NT)

            if isinstance(slot, int):
                own_ref[part, cols] = value
            else:
                give_ref[slot - 1, part, cols] = value.astype(low)
        tiles(model, body)

    start_far, start_plain, merge, finish = collect(send, 12, give_ref, transit_ref, take_ref, peers, 2)
    outs = [local(6, hidden_ref, hidden_out)]
    for k in steps[2]:
        pass_tail(k)
    tails[0].wait_recv()
    for copy in twins:
        copy.wait_recv()
    grad_act(tail_at + 2 * TILE, 2 * early + TILE)
    unit_count = units // TILE

    def branch(i, carry):
        cols = pl.ds(pl.multiple_of(i % (model // TILE) * TILE, TILE), TILE)
        slot = i // (model // TILE)
        branch_ref[slot, :, cols] = (
            dot(act_ref[slot, :, :early], weight_ref[cols, model + 2 * early:tail_at], NT)
            + dot(act_ref[slot, :, early:], weight_ref[cols, tail_at + 2 * TILE:], NT)).astype(low)
        for k in range(4):
            @pl.when(i == (k + 1) * (model // TILE) - 1)
            def _():
                branch_copies[k].start()
        return carry

    branch_copies = [pltpu.make_async_copy(branch_ref.at[k], branch_outs[k], local_sem.at[(7, 10, 11, 12)[k]])
                     for k in range(4)]

    def work(i, carry):
        def flag(test):
            return test.astype(jnp.int32)

        slot = flag(i >= 2) + flag((i == 3) | (i == 4)) + 2 * flag(i >= 6)
        h = flag((i == 1) | (i == 4) | (i == 5) | (i == 7))
        part = pl.ds(pl.multiple_of(h * half, half), half)

        def on(index, *actions):
            @pl.when(i == index)
            def _():
                for action in actions:
                    action()

        on(2, x_sends[0].wait_recv, x_relay.start)
        on(3, y_sends[0].wait_recv)
        on(4, y_sends[1].wait_recv, y_relay.start)
        on(5, x_sends[1].wait_recv)
        @pl.when(i == 6)
        def _():
            lax.fori_loop(0, 2 * (model // TILE), branch, 0)

        on(6, x_relay.wait_recv)
        on(7, y_relay.wait_recv)
        feed(slot, part)
        back(slot, part)
        on(2, start_plain[0])
        on(4, start_plain[1])
        on(6, lambda: start_far(0))
        on(7, lambda: start_far(1))
        return carry

    feed(0, whole)
    back(0, whole)
    lax.fori_loop(2, 8, work, 0)

    def weight_grad(left_ref, right_ref, base, first, amount):
        def step(i, carry):
            part = pl.ds(pl.multiple_of(i % 2 * (model // 2), model // 2), model // 2)
            f = pl.multiple_of(i // 2 * TILE, TILE)
            acc = dot(left_ref[0, :, part], right_ref[0, :, pl.ds(f, TILE)], TN)
            for slot in range(1, 4):
                acc += dot(left_ref[slot, :, part], right_ref[slot, :, pl.ds(f, TILE)], TN)
            grads_ref[part, pl.ds(base + f, TILE)] = acc.astype(low)
            return carry
        lax.fori_loop(2 * first, 2 * (first + amount), step, 0)

    def gate_up_grad(first, amount):
        weight_grad(normed_ref, dgu_ref, 0, first, amount)

    down_cols = pl.ds(2 * units, units)

    shard_start, shard_pass, shard_finish = pair_sum(
        send, 28 + count, place, sibling, others, lambda part: grads_ref.at[part, down_cols],
        twin_ref, total_ref, shard_take_ref, shard)
    weight_grad(dy_ref, act_ref, 2 * units, 0, 2)
    merge(0, 0)
    merge(1, 0)
    weight_grad(dy_ref, act_ref, 2 * units, 2, unit_count - 2)
    merge(0, 1)
    merge(1, 1)
    shard_start()
    gate_up_grad(0, 5)
    shard_pass()
    gain_grad_ref[...] = jnp.zeros_like(gain_grad_ref)
    sends = [[send(22 + 3 * h + k, do_give_ref.at[k, halves[h]], do_ref.at[half_of(mine, h), :], "seq", peer)
              for k, peer in enumerate(peers)] for h in range(2)]
    for h in range(2):
        finish(h)

        def norm_back(i, carry, h=h):
            part = pl.ds(pl.multiple_of(h * half + i * 64, 64), 64)
            value = hidden_ref[part, :]
            inv = rms_scale(value)
            grad = own_ref[part, :] + take_ref[0, part, :].astype(jnp.float32) + take_ref[1, part, :].astype(jnp.float32)
            gain_grad_ref[0:1, :] += jnp.sum(grad * value * inv, axis=0, keepdims=True)
            scaled = grad * gains_ref[1:2, :]
            dh = dy_ref[0, part, :].astype(jnp.float32) + (
                inv * scaled - value * inv**3 * jnp.mean(value * scaled, axis=-1, keepdims=True))
            own_ref[part, :] = dh
            low_ref[part, :] = dh.astype(low)
            return carry

        lax.fori_loop(0, half // 64, norm_back, 0)
        for k in (2, 0, 1):
            do_give_ref[k, halves[h], :] = dot(
                low_ref[halves[h], :], weight_ref[span(peers[k], width), :model], NT).astype(low)
            sends[h][k].start()
        do_ref[half_of(mine, h), :] = dot(low_ref[halves[h], :], weight_ref[span(mine, width), :model], NT).astype(low)
    outs.append(local(8, own_ref, dh_out))
    gate_up_grad(5, 2 * units // TILE - 5)
    outs.append(local(9, grads_ref.at[:, :2 * units], grads_out.at[:, :2 * units]))

    def out_grad(c):
        cols = pl.ds(c, TILE)
        grads_ref[:, pl.ds(3 * units + c, TILE)] = dot(mixed_ref[...], low_ref[:, cols], TN).astype(low)

    tiles(model, out_grad)
    outs.append(local(13, grads_ref.at[:, 3 * units:], grads_out.at[:, 2 * units:]))

    lax.fori_loop(2 * (model // TILE), 4 * (model // TILE), branch, 0)
    outs += branch_copies
    shard_finish(down_piece_ref)
    for copy in outs:
        copy.wait()
    for copy in tails + twins:
        copy.wait_send()
    for h in range(2):
        x_sends[h].wait_send()
        y_sends[h].wait_send()
        for k in range(3):
            turn[h][k].wait_send()
            sends[h][k].wait()
    x_relay.wait_send()
    y_relay.wait_send()


def middle(dealt_out, x, weights, gate_up, down, gains, dy, units):
    low = jnp.bfloat16
    group_len, width = dealt_out.shape
    rows, model = x.shape
    shard = down.shape[0]
    count = model // shard
    f32 = jnp.float32
    shape = jax.ShapeDtypeStruct
    copies = 28 + 2 * count
    return pl.pallas_call(
        middle_kernel,
        name="middle",
        out_shape=(
            shape((rows, model), f32),
            *[shape((rows, model), low)] * 4,
            shape((model, 2 * units + model), low),
            shape((rows, model), f32),
            shape((group_len, width), low),
            shape((8, model), f32),
            shape((shard, units), low),
        ),
        in_specs=[hbm()] * 5 + [vmem()] + [hbm()] * 4,
        out_specs=(hbm(),) * 7 + (vmem(),) * 3,
        scratch_shapes=[
            pltpu.VMEM((rows, model), low),
            pltpu.VMEM((shard, 3 * TILE), f32),
            pltpu.VMEM((shard, 3 * TILE), low),
            pltpu.VMEM((model, model + 3 * units), low),
            pltpu.VMEM((4, rows, model), low),
            pltpu.VMEM((rows, model), f32),
            pltpu.VMEM((4, rows, model), low),
            pltpu.VMEM((model, 3 * units + model), low),
            pltpu.VMEM((rows, model), low),
            pltpu.VMEM((4, rows, model), low),
            pltpu.VMEM((4, rows, units), low),
            pltpu.VMEM((4, rows, 2 * units), low),
            pltpu.VMEM((3, rows, model), low),
            pltpu.VMEM((2, rows // 2, model), low),
            pltpu.VMEM((2, rows, model), low),
            pltpu.VMEM((rows, model), f32),
            pltpu.VMEM((rows, model), low),
            pltpu.VMEM((3, rows, width), low),
            pltpu.VMEM((count // 2, shard, units), low),
            pltpu.VMEM((count // 2, shard, units), low),
            pltpu.VMEM((count // 2, shard, units), low),
            pltpu.SemaphoreType.DMA((19,)),
            pltpu.SemaphoreType.DMA((copies,)),
            pltpu.SemaphoreType.DMA((copies,)),
        ],
        compiler_params=pltpu.CompilerParams(
            vmem_limit_bytes=62 << 20, collective_id=1, has_side_effects=True),
        cost_estimate=pl.CostEstimate(flops=60_000_000_000, bytes_accessed=40 << 20, transcendentals=0),
    )(dealt_out, x, weights, gate_up, down, gains, *dy)


def gather_kernel(x_ref, all_ref, local_sem, send_sem, recv_sem):
    rows = x_ref.shape[0]
    mine, peers = seq_peers()
    send = sender(send_sem, recv_sem)
    half = rows // 2
    px, py, _ = peers

    def part(owner, h):
        return all_ref.at[pl.ds(pl.multiple_of(owner * rows + h * half, half), half)]

    ready = greet(peers)
    keep = pltpu.make_async_copy(x_ref, all_ref.at[span(mine, rows)], local_sem)
    keep.start()
    ready()
    x_sends = [send(h, x_ref.at[pl.ds(h * half, half)], part(mine, h), "seq", px) for h in range(2)]
    y_sends = [send(2 + h, x_ref.at[pl.ds(h * half, half)], part(mine, h), "seq", py) for h in range(2)]
    for copy in (x_sends[0], y_sends[1], x_sends[1], y_sends[0]):
        copy.start()
    x_relay = send(4, part(px, 0), part(px, 0), "seq", py)
    y_relay = send(5, part(py, 1), part(py, 1), "seq", px)
    x_sends[0].wait_recv()
    x_relay.start()
    y_sends[1].wait_recv()
    y_relay.start()
    x_sends[1].wait_recv()
    y_sends[0].wait_recv()
    for copy in x_sends + y_sends:
        copy.wait_send()
    x_relay.wait()
    y_relay.wait()
    keep.wait()


def gather_rows(x):
    rows, model = x.shape
    return pl.pallas_call(
        gather_kernel,
        name="gather_rows",
        out_shape=jax.ShapeDtypeStruct((4 * rows, model), x.dtype),
        in_specs=[hbm()],
        out_specs=hbm(),
        scratch_shapes=[
            pltpu.SemaphoreType.DMA,
            pltpu.SemaphoreType.DMA((6,)),
            pltpu.SemaphoreType.DMA((6,)),
        ],
        compiler_params=pltpu.CompilerParams(collective_id=0, has_side_effects=True),
        cost_estimate=pl.CostEstimate(flops=40_000_000_000, bytes_accessed=20 << 20, transcendentals=0),
    )(x)


def rear_kernel(grad_in, normed_in, slab_in, gains_ref, x_in, dh_in, hidden_in, branch0_in, branch1_in, branch2_in,
                branch3_in, result_out, input_grad_out, gain_grad_ref, piece_ref,
                grad_ref, slab_ref, result_ref, input_grad_ref, normed_ref, x_ref, dh_ref, hidden_ref, branch_ref, give_ref, transit_ref, take_ref, own_ref, term_ref,
                twin_ref, total_ref, shard_take_ref, local_sem, send_sem, recv_sem):
    low = jnp.bfloat16
    rows, model = result_ref.shape
    shard, columns = piece_ref.shape
    count = model // shard
    half = rows // 2
    mine, peers = seq_peers()
    place, sibling, others = shard_peers(count)
    send = sender(send_sem, recv_sem)
    local = starter(local_sem)
    ready = greet(peers, [sibling] + others)
    first_copies = [local(11, slab_in, slab_ref), local(12, grad_in, grad_ref)]
    normed_copy = local(0, normed_in, normed_ref)
    row_copies = [local(1, x_in, x_ref), local(2, dh_in, dh_ref)]
    result_copies = [local(3, hidden_in, hidden_ref)]
    result_copies += [local(4 + k, piece, branch_ref.at[k])
                      for k, piece in enumerate((branch0_in, branch1_in, branch2_in, branch3_in))]

    def partial(owner, first, amount, store):
        block = pl.ds(pl.multiple_of(owner * rows + first, half), amount)

        def body(i, carry):
            cols = pl.ds(pl.multiple_of(i * TILE, TILE), TILE)
            store(cols, dot(grad_ref[block, :], slab_ref[cols, :columns], NT))
            return carry

        lax.fori_loop(0, model // TILE, body, 0)

    def hand(k, first, amount):
        def store(cols, value):
            give_ref[k, pl.ds(first, amount), cols] = value.astype(low)
        partial(peers[k], first, amount, store)

    def keep(cols, value):
        own_ref[:, cols] = value

    for copy in first_copies:
        copy.wait()
    hand(2, 0, half)
    ready()
    start_far, start_plain, merge, finish = collect(send, 0, give_ref, transit_ref, take_ref, peers, 2)
    start_far(0)
    hand(2, half, half)
    start_far(1)
    for h in range(2):
        hand(h, 0, rows)
        start_plain[h]()

    def weight_term(i, carry):
        part = pl.ds(pl.multiple_of(i * TILE, TILE), TILE)
        term_ref[part, :] = dot(normed_ref[:, part], grad_ref[...], TN).astype(low)
        return carry

    normed_copy.wait()
    lax.fori_loop(0, model // TILE, weight_term, 0)
    shard_start, shard_pass, shard_finish = pair_sum(
        send, 10, place, sibling, others, lambda part: term_ref.at[part], twin_ref, total_ref, shard_take_ref, shard)
    shard_start()
    for c in range(2):
        for h in range(2):
            merge(h, c)
    shard_pass()
    partial(mine, 0, rows, keep)
    for copy in result_copies:
        copy.wait()

    def result(i, carry):
        part = pl.ds(pl.multiple_of(i * 64, 64), 64)
        value = hidden_ref[part, :]
        for k in range(4):
            value += branch_ref[k, part, :].astype(jnp.float32)
        result_ref[part, :] = value.astype(low)
        return carry

    lax.fori_loop(0, rows // 64, result, 0)
    outs = [local(8, result_ref, result_out)]
    for copy in row_copies:
        copy.wait()
    gain_grad_ref[...] = jnp.zeros_like(gain_grad_ref)

    def norm_back(i, carry):
        part = pl.ds(pl.multiple_of(i * 64, 64), 64)
        x = x_ref[part, :].astype(jnp.float32)
        inv = rms_scale(x)
        grad = own_ref[part, :] + take_ref[0, part, :].astype(jnp.float32) + take_ref[1, part, :].astype(jnp.float32)
        gain_grad_ref[0:1, :] += jnp.sum(grad * x * inv, axis=0, keepdims=True)
        scaled = grad * gains_ref[0:1, :]
        input_grad_ref[part, :] = (dh_ref[part, :] + (
            inv * scaled - x * inv**3 * jnp.mean(x * scaled, axis=-1, keepdims=True))).astype(low)
        return carry

    for h in range(2):
        finish(h)
        lax.fori_loop(h * half // 64, (h + 1) * half // 64, norm_back, 0)
        part = pl.ds(h * half, half)
        outs.append(local(9 + h, input_grad_ref.at[part], input_grad_out.at[part]))
    shard_finish(piece_ref)
    for copy in outs:
        copy.wait()


def rear(grad, normed, slab, gains, x, dh, hidden, branch, shard):
    low = jnp.bfloat16
    f32 = jnp.float32
    rows, model = x.shape
    group_len, columns = grad.shape
    count = model // shard
    shape = jax.ShapeDtypeStruct
    copies = 10 + count
    return pl.pallas_call(
        rear_kernel,
        name="rear",
        out_shape=(shape((rows, model), low), shape((rows, model), low), shape((8, model), f32),
                   shape((shard, columns), low)),
        in_specs=[hbm(), hbm(), hbm(), vmem()] + [hbm()] * 7,
        out_specs=(hbm(), hbm(), vmem(), vmem()),
        scratch_shapes=[
            pltpu.VMEM((group_len, columns), low),
            pltpu.VMEM(slab.shape, low),
            pltpu.VMEM((rows, model), low),
            pltpu.VMEM((rows, model), low),
            pltpu.VMEM((group_len, model), low),
            pltpu.VMEM((rows, model), low),
            pltpu.VMEM((rows, model), f32),
            pltpu.VMEM((rows, model), f32),
            pltpu.VMEM((4, rows, model), low),
            pltpu.VMEM((3, rows, model), low),
            pltpu.VMEM((2, rows // 2, model), low),
            pltpu.VMEM((2, rows, model), low),
            pltpu.VMEM((rows, model), f32),
            pltpu.VMEM((model, columns), low),
            pltpu.VMEM((count // 2, shard, columns), low),
            pltpu.VMEM((count // 2, shard, columns), low),
            pltpu.VMEM((count // 2, shard, columns), low),
            pltpu.SemaphoreType.DMA((13,)),
            pltpu.SemaphoreType.DMA((copies,)),
            pltpu.SemaphoreType.DMA((copies,)),
        ],
        compiler_params=pltpu.CompilerParams(
            vmem_limit_bytes=62 << 20, collective_id=2, has_side_effects=True),
        cost_estimate=pl.CostEstimate(flops=50_000_000_000, bytes_accessed=20 << 20, transcendentals=0),
    )(grad, normed, slab, gains, x, dh, hidden, *branch)


def last_kernel(pieces_ref, qkv_ref, down_ref, gain_a_ref, gain_b_ref, out_qkv_ref, out_out_ref, out_gate_up_ref, out_down_ref,
                gains_ref, block_ref, slots_ref, out_own_ref, out_take_ref, out_part_ref, out_slots_ref, gain_own_ref, gain_take_ref, gain_slots_ref, local_sem, send_sem, recv_sem):
    low = jnp.bfloat16
    shard, columns = qkv_ref.shape
    model = gain_a_ref.shape[1]
    count = model // shard
    units = out_down_ref.shape[1] // 4
    width = columns // 3
    part = model // 4
    mine, peers = seq_peers()
    place, sibling, _ = shard_peers(count)
    everyone = [lax.rem(place + k, count) for k in range(1, count)]
    send = sender(send_sem, recv_sem)
    ready = greet(peers, everyone)
    local = starter(local_sem)
    fills = [local(0, qkv_ref, block_ref.at[:, :columns]), local(1, down_ref, block_ref.at[:, columns:columns + units]),
             local(2, pieces_ref.at[:, :2 * units], block_ref.at[:, columns + units:])]
    out_fill = local(3, pieces_ref.at[:, 2 * units:], out_own_ref)
    gain_own_ref[0:1, :] = gain_a_ref[0:1, :]
    gain_own_ref[1:2, :] = gain_b_ref[0:1, :]
    gain_own_ref[2:8, :] = jnp.zeros((6, model), jnp.float32)
    for copy in fills:
        copy.wait()
    ready()
    out_fill.wait()
    base = 9 + len(everyone)
    out_turn = [send(base + k, out_own_ref.at[:, span(peer, part)], out_take_ref.at[k], "seq", peer)
                for k, peer in enumerate(peers)]
    for k in (2, 0, 1):
        out_turn[k].start()
    forward, arrivals, finish = spread(send, 0, block_ref, [slots_ref.at[k] for k in range(3)], peers)
    gain_sends = [send(6 + k, gain_own_ref, gain_take_ref.at[k], "fsdp", peer) for k, peer in enumerate(everyone)]
    for copy in gain_sends:
        copy.start()

    def place_block(source, owner):
        for b in range(3):
            out_qkv_ref[:, span(b * 4 + owner, width)] = source[:, b * width:(b + 1) * width]
        out_down_ref[:, span(owner, units)] = source[:, columns:columns + units]
        at = columns + units
        for shift, size in ((0, units - TILE), (units - TILE, TILE)):
            for b in range(2):
                out_gate_up_ref[:, pl.ds(pl.multiple_of((b * 4 + owner) * units + shift, TILE), size)] = (
                    source[:, at:at + size])
                at += size

    place_block(block_ref, mine)
    value = out_own_ref[:, span(mine, part)].astype(jnp.float32)
    for k in range(3):
        out_turn[k].wait_recv()
        value += out_take_ref[k].astype(jnp.float32)
    out_part_ref[...] = value.astype(low)
    out_out_ref[:, span(mine, part)] = out_part_ref[...]
    out_sends = [send(base + 3 + k, out_part_ref, out_slots_ref.at[k], "seq", peer) for k, peer in enumerate(peers)]
    for k in (2, 0, 1):
        out_sends[k].start()
    forward()
    total = gain_own_ref[...]
    for k, copy in enumerate(gain_sends):
        copy.wait_recv()
        total += gain_take_ref[k]
    gains_ref[...] = total
    seq_sends = [send(6 + len(everyone) + k, gains_ref, gain_slots_ref.at[k], "seq", peer) for k, peer in enumerate(peers)]
    for copy in seq_sends:
        copy.start()
    for k in range(3):
        arrivals[k]()
        place_block(slots_ref.at[k], peers[k])
        out_sends[k].wait_recv()
        out_out_ref[:, span(peers[k], part)] = out_slots_ref[k]
    for copy in seq_sends:
        copy.wait()
    gains_ref[...] += gain_slots_ref[0] + gain_slots_ref[1] + gain_slots_ref[2]
    for copy in gain_sends + out_turn + out_sends:
        copy.wait_send()
    finish()


def last(pieces, qkv_piece, down_piece, gain_a, gain_b, units):
    low = jnp.bfloat16
    shard, columns = qkv_piece.shape
    model = gain_a.shape[1]
    count = model // shard
    f32 = jnp.float32
    shape = jax.ShapeDtypeStruct
    wide = columns + 3 * units
    copies = 14 + count
    return pl.pallas_call(
        last_kernel,
        name="last",
        out_shape=(
            shape((shard, 4 * columns), low),
            shape((shard, model), low),
            shape((shard, 8 * units), low),
            shape((shard, 4 * units), low),
            shape((8, model), f32),
        ),
        in_specs=[hbm()] * 3 + [vmem()] * 2,
        out_specs=(vmem(),) * 5,
        scratch_shapes=[
            pltpu.VMEM((shard, wide), low),
            pltpu.VMEM((3, shard, wide), low),
            pltpu.VMEM((shard, model), low),
            pltpu.VMEM((3, shard, model // 4), low),
            pltpu.VMEM((shard, model // 4), low),
            pltpu.VMEM((3, shard, model // 4), low),
            pltpu.VMEM((8, model), f32),
            pltpu.VMEM((count - 1, 8, model), f32),
            pltpu.VMEM((3, 8, model), f32),
            pltpu.SemaphoreType.DMA((4,)),
            pltpu.SemaphoreType.DMA((copies,)),
            pltpu.SemaphoreType.DMA((copies,)),
        ],
        compiler_params=pltpu.CompilerParams(
            vmem_limit_bytes=40 << 20, collective_id=3, has_side_effects=True),
        cost_estimate=pl.CostEstimate(flops=40_000_000_000, bytes_accessed=20 << 20, transcendentals=0),
    )(pieces, qkv_piece, down_piece, gain_a, gain_b)


def widen_kernel(*refs):
    for source, target in zip(refs[:6], refs[6:]):
        target[...] = source[...].astype(target.dtype)


def widen(shard, arrays):
    steps = max(shard // 32, 1)
    specs = [pl.BlockSpec((array.shape[0] // steps, array.shape[1]), lambda i: (i, 0)) for array in arrays]
    return pl.pallas_call(
        widen_kernel,
        name="widen",
        grid=(steps,),
        out_shape=[jax.ShapeDtypeStruct(array.shape, jnp.float32 if array.shape[0] == shard else array.dtype)
                   for array in arrays],
        in_specs=specs,
        out_specs=specs,
        compiler_params=pltpu.CompilerParams(vmem_limit_bytes=40 << 20),
    )(*arrays)


def swaps(rows):
    return [lax.ppermute(piece, "seq", table) for piece, table in zip(
        rows, ([(i, i ^ 1) for i in range(4)], [(i, (i + 2) % 4) for i in range(4)], [(i, 3 - i) for i in range(4)]))]


def on_device(block_input, norm_gain_a, weight_qkv, weight_out, norm_gain_b, weight_gate_up, weight_down,
              cotangent, permutation, lengths, offsets):
    low = jnp.bfloat16
    f32 = jnp.float32
    seq_count = lax.axis_size("seq")
    mine = lax.axis_index("seq")
    row_count, model_width = block_input.shape[1:]
    group_len = row_count * seq_count
    shard = weight_qkv.shape[0]
    head_width = weight_qkv.shape[1] // 3 // seq_count
    part_units = weight_down.shape[1] // seq_count
    perm = permutation[0]
    offs = offsets[0]
    position = jnp.arange(group_len, dtype=jnp.int32)
    start = jnp.max(jnp.where(offs[None, :] <= position[:, None], offs[None, :], 0), axis=1)

    def columns(weight, width, first, amount):
        blocks = weight.shape[1] // (seq_count * width)
        return [lax.dynamic_slice_in_dim(weight, (b * seq_count + mine) * width + first, amount, axis=1).astype(low)
                for b in range(blocks)]

    def gather_weight(parts):
        return lax.all_gather(jnp.concatenate(parts, axis=1), "fsdp", axis=0, tiled=True)

    early = part_units - TILE
    gain_cols = jnp.pad(jnp.stack([norm_gain_a, norm_gain_b], axis=1).astype(low), ((0, 0), (0, 126)))
    slab = gather_weight(columns(weight_qkv, head_width, 0, head_width) + [gain_cols])
    weights = gather_weight([weight_out.astype(low)] + columns(weight_gate_up, part_units, 0, early)
                            + columns(weight_down, part_units, 0, early))
    rows_all = gather_rows(block_input[0])
    grad_own, rows_all = lax.optimization_barrier((cotangent[0], rows_all))
    grad_rows = [cotangent[0]] + swaps([grad_own] * 3)
    ordered, dealt_out, wide_out, log_total, normed_a, gains = attention_forward(offs, rows_all, slab, perm, start)
    hidden, branch0, branch1, branch2, branch3, grads, grad_hidden, grad_heads, gain_b_term, down_piece = middle(
        dealt_out, block_input[0], weights, weight_gate_up, weight_down, gains, grad_rows, part_units)
    pieces = lax.psum_scatter(grads, "fsdp", scatter_dimension=0, tiled=True)
    branch = [branch0] + swaps([branch1, branch2, branch3])
    dealt_grad = attention_backward(offs, grad_heads, ordered, perm, start, wide_out, log_total)
    result_rows, input_grad, gain_a_term, qkv_piece = rear(
        dealt_grad, normed_a, slab, gains, block_input[0], grad_hidden, hidden, branch, shard)
    grad_qkv, grad_out, grad_gate_up, grad_down, gain_terms = last(
        pieces, qkv_piece, down_piece, gain_a_term, gain_b_term, part_units)
    gain_terms = lax.dynamic_slice_in_dim(gain_terms, lax.axis_index("fsdp") * shard, shard, axis=1)
    grad_qkv, grad_out, grad_gate_up, grad_down, result_rows, input_grad = widen(
        shard, [grad_qkv, grad_out, grad_gate_up, grad_down, result_rows, input_grad])
    return (
        result_rows[None],
        input_grad[None],
        gain_terms[0],
        grad_qkv,
        grad_out,
        gain_terms[1],
        grad_gate_up,
        grad_down,
    )


def solution(mesh):
    rows = P("fsdp", "seq", None)
    vector = P("fsdp")
    matrix = P("fsdp", None)
    return jax.shard_map(
        on_device,
        mesh=mesh,
        in_specs=(rows, vector, matrix, matrix, vector, matrix, matrix, rows, matrix, matrix, matrix),
        out_specs=(rows, rows, vector, matrix, matrix, vector, matrix, matrix),
        check_vma=False,
    )
```
